32 devices in a mesh: groups: 2 (over y), view: 4 (over z), row: 4 (over x, core).
Axes of the slice: x: 2, y: 2, z: 4, core: 2. Of those that a mesh axis runs over, the one named last changes fastest.
Arguments:
- inputs: bfloat16 [64, 292, 16, 16], P(None, 'view', ('groups', 'row')), parts along dimension 2, may hold values from -24 to 24
- cotangent: bfloat16 [64, 292, 16, 16], P(None, None, ('groups', 'row'), 'view'), parts along dimension 2, may hold values from -6 to 6
- keep: int32 [584], P('groups'), parts along dimension 0, may hold values from 0 to 1, as said below
- w_conv: bfloat16 [64, 64, 3, 3], replicated, may hold values from -0.25 to 0.25
- gain: float32 [64], replicated, may hold values from 0.5 to 1.5
- w_query: bfloat16 [64, 64], replicated, may hold values from -3 to 3
- w_key: bfloat16 [64, 64], replicated, may hold values from -3 to 3
- w_value: bfloat16 [64, 64], replicated, may hold values from -0.75 to 0.75
- w_out: bfloat16 [64, 64], replicated, may hold values from -0.75 to 0.75
Outputs:
- output: bfloat16 [64, 292, 16, 16], P(None, None, ('groups', 'row'), 'view'), parts along dimension 2
- d_input: bfloat16 [64, 292, 16, 16], P(None, 'view', ('groups', 'row')), parts along dimension 2
- g_conv: float32 [128, 64, 3, 3], P('groups'), parts along dimension 0
- g_gain: float32 [128], P('groups'), parts along dimension 0
- g_query: float32 [128, 64], P('groups'), parts along dimension 0
- g_key: float32 [128, 64], P('groups'), parts along dimension 0
- g_value: float32 [128, 64], P('groups'), parts along dimension 0
- g_out: float32 [128, 64], P('groups'), parts along dimension 0
The draws below stay inside these ranges and needn't reach their ends.
There are 2 independent parts, one for each index of `groups`. The reference program is written for one: setup_inputs(seed, part) draws one part's arguments, and reference() takes and returns one part's arrays. A program takes and returns all parts, laid end to end along the dimension named above; an argument that names none is the same for every part. Nothing has to cross between parts.
Inputs may be any that keep to these rules, and one draw needn't show every extreme that they name: `keep`: zero at every view from 289 on, one at view 289 // 2.
All inputs are finite; a program needn't handle non-finite values.
Results may differ from the reference program's by a relative error of at most 0.012.
The reference program's roundings to bfloat16 on the way (of `spatial`, `normal_in`, `probs_b`, `attended`, `d_attended`, `d_value`, `d_scores` and `d_spatial`) count: a program that leaves them out, or rounds other values in their place, can miss the bound.
Values may be sent and summed in bfloat16 or wider, within the bound.
No kernel may reach another device: no remote copies, remote signals or barrier semaphores. Data moves between devices by JAX's collectives and lax.ppermute only.
A program may use at most 64 MiB of HBM per device.

```python
import math
import jax
import jax.numpy as jnp
from jax import lax

FEATURE_CHANNELS = 64
ANG = 289
PADDED_VIEWS = 292
STRIP_ROWS = 8
IMAGE_COLUMNS = 16


def draw_inputs(key, part):
    tensor_shape = (FEATURE_CHANNELS, PADDED_VIEWS, STRIP_ROWS, IMAGE_COLUMNS)
    field = jax.random.normal(jax.random.fold_in(key, 3), tensor_shape, jnp.float32)
    return jnp.clip(field, -6.0, 6.0).astype(jnp.bfloat16)


def draw_keep(key, part):
    view_stack = jnp.arange(PADDED_VIEWS, dtype=jnp.int32)
    active_mask = jax.random.randint(key, (PADDED_VIEWS,), 0, 8) > 0
    active_mask = jnp.logical_or(active_mask, view_stack == ANG // 2)
    active_mask = jnp.logical_and(active_mask, view_stack < ANG)
    return active_mask.astype(jnp.int32)


def draw_w_query(key, part):
    matrix = jax.random.normal(jax.random.fold_in(key, 1), (FEATURE_CHANNELS, FEATURE_CHANNELS), jnp.float32) / math.sqrt(FEATURE_CHANNELS)
    return jnp.clip(matrix, -3.0, 3.0).astype(jnp.bfloat16)


def draw_w_key(key, part):
    matrix = jax.random.normal(jax.random.fold_in(key, 2), (FEATURE_CHANNELS, FEATURE_CHANNELS), jnp.float32) / math.sqrt(FEATURE_CHANNELS)
    return jnp.clip(matrix, -3.0, 3.0).astype(jnp.bfloat16)


def level_of(own_key, extent, split, least, high):
    def one(position, parts):
        draws = jax.random.uniform(jax.random.fold_in(jax.random.fold_in(own_key, 6), position), (parts,), jnp.float32, least / len(split), high / len(split))
        return jnp.repeat(jnp.exp(draws), extent[position] // parts).reshape((-1,) + (1,) * (len(extent) - position - 1))

    factor_of = one(*split[0])
    for cut in split[1:]:
        factor_of = factor_of * one(*cut)
    return factor_of


def gaussian(rng, shape, spread, reach, pieces=(), held_as=jnp.bfloat16):
    drawn = jax.random.normal(rng, shape, jnp.float32) * spread
    if len(pieces) > 0:
        drawn = level_of(rng, shape, pieces, -0.22, 0.18) * drawn
    return jnp.clip(drawn, min=-reach, max=reach).astype(held_as)


def setup_inputs(seed: int = 0, part: int = 0) -> dict:
    streams_of = jax.random.split(jax.random.key(seed), 10)
    part_keys = jax.random.split(jax.random.fold_in(streams_of[9], part), 10)
    return {
        "inputs": draw_inputs(jax.random.fold_in(jax.random.fold_in(streams_of[9], part), 71), part),
        "cotangent": gaussian(part_keys[1], (FEATURE_CHANNELS, PADDED_VIEWS, STRIP_ROWS, IMAGE_COLUMNS), 1.0, 6.0, ((2, 4), (3, 4))),
        "keep": draw_keep(jax.random.fold_in(jax.random.fold_in(streams_of[9], part), 71), part),
        "w_conv": gaussian(streams_of[3], (FEATURE_CHANNELS, FEATURE_CHANNELS, 3, 3), (9 * FEATURE_CHANNELS) ** -0.5, 0.25),
        "gain": jnp.clip(1.0 + 0.1 * jax.random.normal(streams_of[4], (FEATURE_CHANNELS,), jnp.float32), 0.5, 1.5),
        "w_query": draw_w_query(jax.random.fold_in(streams_of[9], 71), part),
        "w_key": draw_w_key(jax.random.fold_in(streams_of[9], 71), part),
        "w_value": gaussian(streams_of[7], (FEATURE_CHANNELS, FEATURE_CHANNELS), FEATURE_CHANNELS ** -0.5, 0.75),
        "w_out": gaussian(streams_of[8], (FEATURE_CHANNELS, FEATURE_CHANNELS), FEATURE_CHANNELS ** -0.5, 0.75),
    }


def product(form, left, right):
    return jnp.einsum(form, left.astype(jnp.float32), right.astype(jnp.float32))

def convolve(padded, w_conv):
    height = padded.shape[2] - 2
    breadth = padded.shape[3] - 2
    total = jnp.zeros((w_conv.shape[0], padded.shape[1], height, breadth), jnp.float32)
    for row_tap in range(3):
        for col_tap in range(3):
            window = padded[:, :, row_tap:row_tap + height, col_tap:col_tap + breadth]
            total = total + product('oc,cvrw->ovrw', w_conv[:, :, row_tap, col_tap], window)
    return total

def input_grad(grad_pad, w_conv):
    height = grad_pad.shape[2] - 2
    breadth = grad_pad.shape[3] - 2
    total = jnp.zeros((w_conv.shape[1], grad_pad.shape[1], height, breadth), jnp.float32)
    for row_tap in range(3):
        for col_tap in range(3):
            window = grad_pad[:, :, 2 - row_tap:2 - row_tap + height, 2 - col_tap:2 - col_tap + breadth]
            total = total + product('oc,ovrw->cvrw', w_conv[:, :, row_tap, col_tap], window)
    return total

def weight_grad(grad, padded):
    height = grad.shape[2]
    breadth = grad.shape[3]
    taps = []
    for row_tap in range(3):
        for col_tap in range(3):
            window = padded[:, :, row_tap:row_tap + height, col_tap:col_tap + breadth]
            taps.append(product('ovrw,cvrw->oc', grad, window))
    stacked = jnp.stack(taps, axis=2)
    return stacked.reshape(grad.shape[0], padded.shape[0], 3, 3)

def angular(mixed_in, grad_out, keep, gain, w_query, w_key, w_value, w_out):
    scale = 1.0 / math.sqrt(FEATURE_CHANNELS)
    values = mixed_in.astype(jnp.float32)
    centred = values - lax.optimization_barrier(jnp.mean(values, axis=0, keepdims=True))
    rstd = lax.rsqrt(lax.optimization_barrier(jnp.mean(centred * centred, axis=0, keepdims=True)) + 1e-05)
    normed = centred * rstd
    normal_in = (normed * gain[:, None, None]).astype(jnp.bfloat16)
    query = product('cd,cvp->dvp', w_query, normal_in).astype(jnp.bfloat16)
    key_proj = product('cd,cvp->dvp', w_key, normal_in).astype(jnp.bfloat16)
    value_proj = product('cd,cvp->dvp', w_value, normal_in).astype(jnp.bfloat16)
    scores = product('dvp,dup->pvu', query, key_proj) * scale
    scores = jnp.where(keep[None, None, :] > 0, scores, -1e+30)
    highest = lax.optimization_barrier(jnp.max(scores, axis=2, keepdims=True))
    expo = jnp.exp(scores - highest)
    probs = expo / lax.optimization_barrier(jnp.sum(expo, axis=2, keepdims=True))
    probs_b = probs.astype(jnp.bfloat16)
    attended = product('pvu,dup->dvp', probs_b, value_proj).astype(jnp.bfloat16)
    output = (values + product('dc,dvp->cvp', w_out, attended)).astype(jnp.bfloat16)
    d_attended = product('dc,cvp->dvp', w_out, grad_out).astype(jnp.bfloat16)
    g_out = product('dvp,cvp->dc', attended, grad_out)
    d_probs = product('dvp,dup->pvu', d_attended, value_proj)
    d_value = product('pvu,dvp->dup', probs_b, d_attended).astype(jnp.bfloat16)
    inner = lax.optimization_barrier(jnp.sum(probs * d_probs, axis=2, keepdims=True))
    d_scores = (probs * (d_probs - inner) * scale).astype(jnp.bfloat16)
    d_query = product('pvu,dup->dvp', d_scores, key_proj).astype(jnp.bfloat16)
    d_key = product('pvu,dvp->dup', d_scores, query).astype(jnp.bfloat16)
    g_query = product('cvp,dvp->cd', normal_in, d_query)
    g_key = product('cvp,dvp->cd', normal_in, d_key)
    g_value = product('cvp,dvp->cd', normal_in, d_value)
    d_normal = product('cd,dvp->cvp', w_query, d_query) + product('cd,dvp->cvp', w_key, d_key) + product('cd,dvp->cvp', w_value, d_value)
    g_gain = lax.optimization_barrier(jnp.sum(d_normal * normed, axis=(1, 2)))
    scaled = d_normal * gain[:, None, None]
    back = scaled - lax.optimization_barrier(jnp.mean(scaled, axis=0, keepdims=True)) - normed * lax.optimization_barrier(jnp.mean(scaled * normed, axis=0, keepdims=True))
    d_spatial = (grad_out.astype(jnp.float32) + back * rstd).astype(jnp.bfloat16)
    return (output, d_spatial, (g_gain, g_query, g_key, g_value, g_out))

def reference(inputs, cotangent, keep, w_conv, gain, w_query, w_key, w_value, w_out):
    padded = jnp.pad(inputs, ((0, 0), (0, 0), (1, 1), (1, 1)))

    def view_conv(slab):
        return convolve(slab[:, None], w_conv)[:, 0]
    spatial_part = jnp.moveaxis(lax.map(view_conv, jnp.moveaxis(padded, 1, 0)), 0, 1)
    spatial = (inputs.astype(jnp.float32) + spatial_part).astype(jnp.bfloat16)

    def row_pass(pair):
        return angular(pair[0], pair[1], keep, gain, w_query, w_key, w_value, w_out)
    out_rows, grad_rows, grads = lax.map(row_pass, (jnp.moveaxis(spatial, 2, 0), jnp.moveaxis(cotangent, 2, 0)))
    output = jnp.moveaxis(out_rows, 0, 2)
    d_spatial = jnp.moveaxis(grad_rows, 0, 2)
    g_gain, g_query, g_key, g_value, g_out = [lax.optimization_barrier(jnp.sum(item, axis=0)) for item in grads]
    grad_pad = jnp.pad(d_spatial, ((0, 0), (0, 0), (1, 1), (1, 1)))

    def view_back(pair):
        slab_grad, slab_input = pair
        d_slab = input_grad(slab_grad[:, None], w_conv)[:, 0]
        g_slab = weight_grad(slab_grad[:, None, 1:-1, 1:-1], slab_input[:, None])
        return (d_slab, g_slab)
    d_views, g_views = lax.map(view_back, (jnp.moveaxis(grad_pad, 1, 0), jnp.moveaxis(padded, 1, 0)))
    d_input = (d_spatial.astype(jnp.float32) + jnp.moveaxis(d_views, 0, 1)).astype(jnp.bfloat16)
    g_conv = lax.optimization_barrier(jnp.sum(g_views, axis=0))
    return (output, d_input, g_conv, g_gain, g_query, g_key, g_value, g_out)
```

```python
import functools
import math

import jax
import jax.numpy as jnp
from jax import lax
from jax.experimental import pallas as pl
from jax.experimental.pallas import tpu as pltpu
from jax.sharding import PartitionSpec as P

F32 = jnp.float32
BF16 = jnp.bfloat16


def round_up(value, unit):
    return -(-value // unit) * unit


def swap(cells, axis, step):
    count = lax.axis_size(axis)
    return lax.ppermute(cells, axis, [(i, i ^ step) for i in range(count)])


def row_halo(first, last):
    count = lax.axis_size("row")
    index = lax.axis_index("row")
    even = lax.rem(index, 2) == 0
    if count % 2:
        above = lax.ppermute(last, "row", [(i, i + 1) for i in range(count - 1)])
        below = lax.ppermute(first, "row", [(i + 1, i) for i in range(count - 1)])
        return above, below
    near = lax.ppermute(
        jnp.where(even, last, first), "row", [(i, i ^ 1) for i in range(count)]
    )
    pairs = []
    for i in range(1, count - 1, 2):
        pairs += [(i, i + 1), (i + 1, i)]
    if pairs:
        far = lax.ppermute(jnp.where(even, first, last), "row", pairs)
    else:
        far = jnp.zeros_like(near)
    return jnp.where(even, far, near), jnp.where(even, near, far)


def dot(left, right, contract=(1, 0)):
    return lax.dot_general(
        left, right, (((contract[0],), (contract[1],)), ((), ())), preferred_element_type=F32
    )


def angular_kernel(
    scale,
    x_ref,
    cot_ref,
    bias_ref,
    gain_ref,
    wqkv_ref,
    wk_ref,
    wv_ref,
    wo_ref,
    wot_ref,
    wcat_ref,
    out_ref,
    ds_ref,
    g_ref,
    ggain_ref,
    e_s,
    g_s,
    gain_s,
):
    pixels, chan, lanes = x_ref.shape
    rows = bias_ref.shape[0]
    e_s[...] = jnp.zeros_like(e_s)
    g_s[...] = jnp.zeros_like(g_s)
    g_ref[...] = jnp.zeros_like(g_ref)
    gain_s[...] = jnp.zeros_like(gain_s)
    inv_chan = 1.0 / chan

    def pixel(p, carry):
        gain = gain_ref[...]
        s = x_ref[p].astype(F32)
        cen = s - jnp.sum(s, axis=0, keepdims=True) * inv_chan
        rstd = lax.rsqrt(jnp.sum(cen * cen, axis=0, keepdims=True) * inv_chan + 1e-05)
        normed = cen * rstd
        nin32 = normed * gain
        nin = nin32.astype(BF16)
        qkv = dot(wqkv_ref[...], nin)
        q = (qkv[:chan].astype(BF16).astype(F32) * scale).astype(BF16)
        k = qkv[chan : 2 * chan].astype(BF16)
        v = qkv[2 * chan :].astype(BF16)
        nin_t = jnp.transpose(nin32)[:rows].astype(BF16)
        k_t = dot(nin_t, wk_ref[...]).astype(BF16)
        v_t = dot(nin_t, wv_ref[...]).astype(BF16)
        sc = dot(k_t, q) + bias_ref[...]
        e = jnp.exp(sc - jnp.max(sc, axis=0, keepdims=True))
        e_s[:rows] = e.astype(BF16)
        v_aug = jnp.concatenate([v, jnp.ones((16, lanes), BF16)], axis=0)
        att_aug = dot(v_aug, e_s[...])
        inv = 1.0 / att_aug[chan : chan + 1]
        att = att_aug[:chan] * inv
        att_b = att.astype(BF16)
        cot = cot_ref[p]
        out_ref[p] = (s + dot(wot_ref[...], att_b)).astype(BF16)
        d_att = dot(wo_ref[...], cot).astype(BF16).astype(F32)
        d_att = (d_att * inv).astype(BF16)
        inner = jnp.sum(att * d_att.astype(F32), axis=0, keepdims=True)
        dp = dot(v_t, d_att)
        g_s[:rows] = (e * (dp - inner)).astype(BF16)
        d_v = dot(d_att, e_s[...], (1, 1)).astype(BF16)
        d_q = (dot(k, g_s[...]) * scale).astype(BF16)
        d_k = dot(q, g_s[...], (1, 1)).astype(BF16)
        d_qkv = jnp.concatenate([d_q, d_k, d_v], axis=0)
        dn = dot(wcat_ref[...], d_qkv)
        g_ref[:chan] += dot(nin, d_qkv[: 2 * chan], (1, 1))
        both = dot(
            jnp.concatenate([nin, att_b], axis=0), jnp.concatenate([d_v, cot], axis=0), (1, 1)
        )
        lane = lax.broadcasted_iota(jnp.int32, (chan, 2 * chan), 1)
        g_ref[chan:] += jnp.where(lane < chan, both[:chan], both[chan:])
        gain_s[...] += dn * normed
        scaled = dn * gain
        back = (
            scaled
            - jnp.sum(scaled, axis=0, keepdims=True) * inv_chan
            - normed * (jnp.sum(scaled * normed, axis=0, keepdims=True) * inv_chan)
        )
        ds_ref[p] = (cot.astype(F32) + back * rstd).astype(BF16)
        return carry

    lax.fori_loop(0, pixels, pixel, 0)
    ggain_ref[...] = jnp.sum(gain_s[...], axis=1, keepdims=True)


def angular(moved, cotangent, keep, gain, w_query, w_key, w_value, w_out):
    pixels, chan, lanes = moved.shape
    used = keep.shape[0]
    rows = round_up(used, 16)
    bias = jnp.where(keep > 0, 0.0, -1e30).astype(F32)
    bias = jnp.pad(bias, (0, rows - used), constant_values=-1e30)[:, None]
    vmem = pl.BlockSpec(memory_space=pltpu.VMEM)
    scale = 1.0 / math.sqrt(chan)
    return pl.pallas_call(
        functools.partial(angular_kernel, scale),
        out_shape=(
            jax.ShapeDtypeStruct((pixels, chan, lanes), BF16),
            jax.ShapeDtypeStruct((pixels, chan, lanes), BF16),
            jax.ShapeDtypeStruct((2 * chan, 2 * chan), F32),
            jax.ShapeDtypeStruct((chan, 1), F32),
        ),
        in_specs=[vmem] * 10,
        out_specs=(vmem,) * 4,
        scratch_shapes=[
            pltpu.VMEM((lanes, lanes), BF16),
            pltpu.VMEM((lanes, lanes), BF16),
            pltpu.VMEM((chan, lanes), F32),
        ],
        name="angular",
    )(
        moved,
        cotangent,
        bias,
        gain[:, None],
        jnp.concatenate([w_query, w_key, w_value], axis=1).T,
        w_key,
        w_value,
        w_out,
        w_out.T,
        jnp.concatenate([w_query, w_key, w_value], axis=1),
    )


def product(form, left, right):
    return jnp.einsum(form, left, right, preferred_element_type=F32)


def convolve(padded, w_conv):
    height = padded.shape[2] - 2
    breadth = padded.shape[3] - 2
    total = jnp.zeros((w_conv.shape[0], padded.shape[1], height, breadth), F32)
    for row_tap in range(3):
        for col_tap in range(3):
            window = padded[:, :, row_tap : row_tap + height, col_tap : col_tap + breadth]
            total = total + product("oc,cvrw->ovrw", w_conv[:, :, row_tap, col_tap], window)
    return total


def input_grad(grad_pad, w_conv):
    height = grad_pad.shape[2] - 2
    breadth = grad_pad.shape[3] - 2
    total = jnp.zeros((w_conv.shape[1], grad_pad.shape[1], height, breadth), F32)
    for row_tap in range(3):
        for col_tap in range(3):
            window = grad_pad[
                :, :, 2 - row_tap : 2 - row_tap + height, 2 - col_tap : 2 - col_tap + breadth
            ]
            total = total + product("oc,ovrw->cvrw", w_conv[:, :, row_tap, col_tap], window)
    return total


def weight_grad(grad, padded):
    height = grad.shape[2]
    breadth = grad.shape[3]
    taps = []
    for row_tap in range(3):
        for col_tap in range(3):
            window = padded[:, :, row_tap : row_tap + height, col_tap : col_tap + breadth]
            taps.append(product("ovrw,cvrw->oc", grad, window))
    return jnp.stack(taps, axis=0)


def exchange(blocks, axis):
    count = blocks.shape[0]
    if count > 8 or count & (count - 1):
        return lax.all_to_all(blocks, axis, split_axis=0, concat_axis=0, tiled=True)
    index = lax.axis_index(axis)
    got = []
    for step in range(count):
        block = lax.dynamic_index_in_dim(blocks, index ^ step, keepdims=False)
        got.append(block if step == 0 else swap(block, axis, step))
    level = 1
    while level < count:
        odd = (index & level) > 0
        got = [jnp.where(odd, got[i ^ level], got[i]) for i in range(count)]
        level *= 2
    return jnp.stack(got)


def reduce_all(part):
    rows_axis, views_axis = lax.axis_size("row"), lax.axis_size("view")
    if rows_axis != 4 or views_axis > 8 or views_axis & (views_axis - 1):
        return lax.psum(part, ("view", "row"))
    half = part.shape[0] // 2
    odd = (lax.axis_index("row") & 1) > 0
    low, high = part[:half], part[half:]
    own = jnp.where(odd, high, low) + swap(jnp.where(odd, low, high), "row", 1)
    own = own + swap(own, "row", 2)
    total = own
    for step in range(1, views_axis):
        total = total + swap(own, "view", step)
    other = swap(total, "row", 1)
    return jnp.concatenate([jnp.where(odd, other, total), jnp.where(odd, total, other)])


def body(inputs, cotangent, keep, w_conv, gain, w_query, w_key, w_value, w_out):
    chan, view_dev, row_dev, width = inputs.shape
    blocks = lax.axis_size("view")
    breadth = width // blocks
    views = view_dev * blocks
    lanes = round_up(views, 128)
    pixels = row_dev * breadth
    above, below = row_halo(inputs[:, :, :1], inputs[:, :, row_dev - 1 :])
    padded = jnp.concatenate([above, inputs, below], axis=2)
    padded = jnp.pad(padded, ((0, 0), (0, 0), (0, 0), (1, 1)))
    spatial = (inputs.astype(F32) + convolve(padded, w_conv)).astype(BF16)
    out_blocks = spatial.reshape(chan, view_dev, row_dev, blocks, breadth)
    out_blocks = jnp.transpose(out_blocks, (3, 2, 4, 0, 1))
    got = exchange(out_blocks.reshape(blocks, pixels, chan, view_dev), "view")
    moved = jnp.transpose(got, (1, 2, 0, 3)).reshape(pixels, chan, views)
    moved = jnp.pad(moved, ((0, 0), (0, 0), (0, lanes - views)))
    cot = jnp.transpose(cotangent, (2, 3, 0, 1)).reshape(pixels, chan, views)
    cot = jnp.pad(cot, ((0, 0), (0, 0), (0, lanes - views)))
    output, d_spatial, g_weights, g_gain = angular(
        moved, cot, keep, gain, w_query, w_key, w_value, w_out
    )
    output = output[:, :, :views].reshape(row_dev, breadth, chan, views)
    output = jnp.transpose(output, (2, 3, 0, 1))
    back = d_spatial[:, :, :views].reshape(pixels, chan, blocks, view_dev)
    back = exchange(jnp.transpose(back, (2, 0, 1, 3)), "view")
    back = back.reshape(blocks, row_dev, breadth, chan, view_dev)
    returned = jnp.transpose(back, (3, 4, 1, 0, 2)).reshape(chan, view_dev, row_dev, width)
    above, below = row_halo(returned[:, :, :1], returned[:, :, row_dev - 1 :])
    grad_pad = jnp.concatenate([above, returned, below], axis=2)
    grad_pad = jnp.pad(grad_pad, ((0, 0), (0, 0), (0, 0), (1, 1)))
    d_input = (returned.astype(F32) + input_grad(grad_pad, w_conv)).astype(BF16)
    packed = jnp.concatenate(
        [g_weights, jnp.pad(g_gain.reshape(1, chan), ((0, 15), (0, chan)))], axis=0
    )
    packed = reduce_all(packed)
    g_conv = weight_grad(returned, padded)
    g_conv = reduce_all(g_conv.reshape(-1, 2 * chan)).reshape(3, 3, chan, chan)
    g_conv = jnp.transpose(g_conv, (2, 3, 0, 1))
    return (
        output,
        d_input,
        g_conv,
        packed[2 * chan, :chan],
        packed[:chan, :chan],
        packed[:chan, chan:],
        packed[chan : 2 * chan, :chan],
        packed[chan : 2 * chan, chan:],
    )


def solution(mesh):
    placed = (
        P(None, "view", ("groups", "row"), None),
        P(None, None, ("groups", "row"), "view"),
        P("groups"),
        P(),
        P(),
        P(),
        P(),
        P(),
        P(),
    )
    return jax.shard_map(
        body,
        mesh=mesh,
        in_specs=placed,
        out_specs=(
            P(None, None, ("groups", "row"), "view"),
            P(None, "view", ("groups", "row"), None),
            P("groups", None, None, None),
            P("groups"),
            P("groups", None),
            P("groups", None),
            P("groups", None),
            P("groups", None),
        ),
        check_vma=False,
    )
```

```python
import functools
import math

import jax
import jax.numpy as jnp
from jax import lax
from jax.experimental import pallas as pl
from jax.experimental.pallas import tpu as pltpu
from jax.sharding import PartitionSpec as P

F32 = jnp.float32
BF16 = jnp.bfloat16


def round_up(value, unit):
    return -(-value // unit) * unit


def dot(left, right, contract=(1, 0)):
    return lax.dot_general(
        left, right, (((contract[0],), (contract[1],)), ((), ())), preferred_element_type=F32
    )


def pairwise(count):
    return count <= 8 and count & (count - 1) == 0


def swap(cells, axis, step):
    count = lax.axis_size(axis)
    return lax.ppermute(cells, axis, [(i, i ^ step) for i in range(count)])


def halo_swap(near, far):
    count = lax.axis_size("row")
    pairs = []
    for i in range(1, count - 1, 2):
        pairs += [(i, i + 1), (i + 1, i)]
    got_near = lax.ppermute(near, "row", [(i, i ^ 1) for i in range(count)])
    got_far = lax.ppermute(far, "row", pairs) if pairs else jnp.zeros_like(far)
    return got_near, got_far


def row_is_odd():
    return lax.rem(lax.axis_index("row"), 2)


def give(refs, held):
    if len(refs) == 1:
        refs[0][...] = held[...].astype(refs[0].dtype)
        return
    me = lax.axis_index("view")
    for step, ref in enumerate(refs):
        ref[...] = held[me ^ step].astype(ref.dtype)


def take(refs, held):
    if len(refs) == 1:
        held[...] = refs[0][...].astype(held.dtype)
        return
    me = lax.axis_index("view")
    for step, ref in enumerate(refs):
        held[me ^ step] = ref[...].astype(held.dtype)


def wire_shapes(blocks, chan, lanes):
    if pairwise(blocks):
        return [jax.ShapeDtypeStruct((chan, lanes), BF16)] * blocks
    return [jax.ShapeDtypeStruct((blocks, chan, lanes), BF16)]


def exchange(wires):
    if len(wires) == 1:
        return [lax.all_to_all(wires[0], "view", split_axis=0, concat_axis=0, tiled=True)]
    return [wires[0]] + [swap(wires[step], "view", step) for step in range(1, len(wires))]


def taps(w_ref, rows, forward):
    chan = w_ref.shape[2]
    blank = jnp.zeros((chan, chan), F32)
    found = {}
    for i in range(3):
        for j in range(3):
            tap = w_ref[i, j].astype(F32)
            found[i, j] = tap if forward else jnp.transpose(tap)
    bands = []
    for j in range(3):
        for r in range(rows):
            row = []
            for place in range(rows + 2):
                i = place - r if forward else r + 2 - place
                row.append(found[i, j] if 0 <= i < 3 else blank)
            bands.append(jnp.concatenate(row, axis=1))
    return jnp.concatenate(bands, axis=0).astype(BF16)


def spread(frame_ref, acc_ref, weights, rows, forward):
    width, deep, lanes = frame_ref.shape
    chan = deep // (rows + 2)
    size = rows * chan
    acc_ref[...] = jnp.zeros_like(acc_ref)

    def pair(q, carry):
        two = jnp.concatenate([frame_ref[2 * q], frame_ref[2 * q + 1]], axis=1)
        part = dot(weights, two)
        for j in range(3):
            move = 1 - j if forward else j - 1
            for side in range(2):
                acc_ref[2 * q + side + move + 1] += part[
                    j * size : (j + 1) * size, side * lanes : (side + 1) * lanes
                ]
        return carry

    lax.fori_loop(0, width // 2, pair, 0, unroll=width <= 16)


def conv_kernel(blocks, x_ref, near_ref, far_ref, w_ref, *refs):
    *wires, frame_ref, acc_s, held_s = refs
    width, own, views = x_ref.shape
    chan = near_ref.shape[1]
    rows = own // chan
    lanes = frame_ref.shape[2]
    odd = row_is_odd() > 0
    frame_ref[...] = jnp.zeros_like(frame_ref)

    def fill(w, carry):
        near, far = near_ref[w], far_ref[w]
        frame_ref[w, :chan, :views] = jnp.where(odd, near, far)
        frame_ref[w, chan : chan + own, :views] = x_ref[w]
        frame_ref[w, chan + own :, :views] = jnp.where(odd, far, near)
        return carry

    lax.fori_loop(0, width, fill, 0, unroll=width <= 16)
    weights = taps(w_ref, rows, True)
    spread(frame_ref, acc_s, weights, rows, True)
    breadth = width // blocks

    def block(b, carry):
        cells = []
        for r in range(rows):
            for k in range(breadth):
                w = b * breadth + k
                value = acc_s[w + 1, r * chan : (r + 1) * chan]
                value = value + frame_ref[w, (r + 1) * chan : (r + 2) * chan].astype(F32)
                cells.append(value[:, :views])
        cells = jnp.concatenate(cells, axis=1)
        held_s[b, :, : cells.shape[1]] = cells
        return carry

    lax.fori_loop(0, blocks, block, 0, unroll=blocks <= 4)
    give(wires, held_s)


def convolve(x, near, far, w_conv, blocks):
    width, own, views = x.shape
    chan = w_conv.shape[2]
    rows = own // chan
    lanes = round_up(views, 128)
    wire = round_up(rows * (width // blocks) * views, 128)
    vmem = pl.BlockSpec(memory_space=pltpu.VMEM)
    shapes = wire_shapes(blocks, chan, wire)
    shapes = shapes + [jax.ShapeDtypeStruct((width, own + 2 * chan, lanes), BF16)]
    *wires, frame = pl.pallas_call(
        functools.partial(conv_kernel, blocks),
        out_shape=shapes,
        in_specs=[vmem] * 4,
        out_specs=[vmem] * len(shapes),
        scratch_shapes=[
            pltpu.VMEM((width + 2, own, lanes), F32),
            pltpu.VMEM((blocks, chan, wire), F32),
        ],
        name="conv",
    )(x, near, far, w_conv)
    return wires, frame


def weight_kernel(count, pieces, *refs):
    wires = refs[:pieces]
    frame_ref, g_ref, gain_ref = refs[pieces : pieces + 3]
    near_ref, far_ref, own_ref, keep_ref, send_ref, held_s, col_s, pack_s = refs[pieces + 3 :]
    width, own, lanes = own_ref.shape
    blocks, chan, wire = held_s.shape
    rows = own // chan
    breadth = width // blocks
    views = count
    odd = row_is_odd()
    take(wires, held_s)
    col_s[0] = jnp.zeros((own, lanes), BF16)
    col_s[width + 1] = jnp.zeros((own, lanes), BF16)

    def block(b, carry):
        cells = held_s[b]
        for r in range(rows):
            for k in range(breadth):
                at = (r * breadth + k) * views
                value = cells[:, at : at + views]
                if lanes > views:
                    value = jnp.concatenate(
                        [value, jnp.zeros((chan, lanes - views), F32)], axis=1
                    )
                col_s[b * breadth + k + 1, r * chan : (r + 1) * chan] = value.astype(BF16)
        return carry

    lax.fori_loop(0, blocks, block, 0, unroll=blocks <= 4)

    def copy(w, carry):
        cells = col_s[w + 1]
        own_ref[w] = cells
        first, last = cells[:chan], cells[own - chan :]
        near_ref[w] = jnp.where(odd > 0, first, last)
        far_ref[w] = jnp.where(odd > 0, last, first)
        return carry

    lax.fori_loop(0, width, copy, 0, unroll=width <= 16)

    def pair(q, total):
        left, right = [], []
        for side in range(2):
            w = 2 * q + side
            left.append(jnp.concatenate([col_s[w], col_s[w + 1], col_s[w + 2]], axis=0))
            right.append(frame_ref[w])
        return total + dot(
            jnp.concatenate(left, axis=1), jnp.concatenate(right, axis=1), (1, 1)
        )

    total = lax.fori_loop(
        0,
        width // 2,
        pair,
        jnp.zeros((3 * own, own + 2 * chan), F32),
        unroll=width <= 16,
    )
    bands = []
    for shift in range(3):
        band = 0.0
        for r in range(rows):
            top = (shift * rows + r) * chan
            band = band + total[top : top + chan, r * chan : (r + 3) * chan]
        bands.append(band)
    g_conv = jnp.concatenate(bands, axis=0)
    edge = 2 * chan
    pack_s[...] = jnp.zeros_like(pack_s)
    pack_s[: 2 * chan] = g_ref[...]
    pack_s[2 * chan : 2 * chan + 8] = gain_ref[...]
    at = 2 * chan + 8
    pack_s[at : at + 3 * chan] = g_conv[:, :edge]
    half = 3 * chan // 2
    rest = g_conv[:, edge:]
    pack_s[at + 3 * chan : at + 3 * chan + half] = jnp.concatenate(
        [rest[:half], rest[half:]], axis=1
    )
    size = keep_ref.shape[0]
    keep_ref[...] = pack_s[pl.ds(pl.multiple_of(odd * size, 8), size)]
    send_ref[...] = pack_s[pl.ds(pl.multiple_of((1 - odd) * size, 8), size)]


def weight_grads(wires, frame, g_weights, g_gain, views, blocks):
    width, deep, lanes = frame.shape
    chan, wire = wires[0].shape[-2:]
    own = deep - 2 * chan
    size = round_up(2 * chan + 8 + 9 * chan // 2, 32) // 2
    vmem = pl.BlockSpec(memory_space=pltpu.VMEM)
    return pl.pallas_call(
        functools.partial(weight_kernel, views, len(wires)),
        out_shape=(
            jax.ShapeDtypeStruct((width, chan, lanes), BF16),
            jax.ShapeDtypeStruct((width, chan, lanes), BF16),
            jax.ShapeDtypeStruct((width, own, lanes), BF16),
            jax.ShapeDtypeStruct((size, 2 * chan), F32),
            jax.ShapeDtypeStruct((size, 2 * chan), F32),
        ),
        in_specs=[vmem] * (len(wires) + 3),
        out_specs=(vmem,) * 5,
        scratch_shapes=[
            pltpu.VMEM((blocks, chan, wire), F32),
            pltpu.VMEM((width + 2, own, lanes), BF16),
            pltpu.VMEM((2 * size, 2 * chan), F32),
        ],
        name="weights",
    )(*wires, frame, g_weights, g_gain)


def input_kernel(own_ref, near_ref, far_ref, w_ref, out_ref, frame_s, acc_s):
    width, own, lanes = own_ref.shape
    chan = near_ref.shape[1]
    rows = own // chan
    views = out_ref.shape[3]
    odd = row_is_odd() > 0

    def fill(w, carry):
        near, far = near_ref[w], far_ref[w]
        frame_s[w, :chan] = jnp.where(odd, near, far)
        frame_s[w, chan : chan + own] = own_ref[w]
        frame_s[w, chan + own :] = jnp.where(odd, far, near)
        return carry

    lax.fori_loop(0, width, fill, 0, unroll=width <= 16)
    spread(frame_s, acc_s, taps(w_ref, rows, False), rows, False)

    def column(w, carry):
        value = acc_s[w + 1] + own_ref[w].astype(F32)
        for r in range(rows):
            out_ref[r, w] = value[r * chan : (r + 1) * chan, :views].astype(BF16)
        return carry

    lax.fori_loop(0, width, column, 0, unroll=width <= 16)


def input_grad(own, near, far, w_conv, views):
    width, size, lanes = own.shape
    chan = near.shape[1]
    vmem = pl.BlockSpec(memory_space=pltpu.VMEM)
    return pl.pallas_call(
        input_kernel,
        out_shape=jax.ShapeDtypeStruct((size // chan, width, chan, views), BF16),
        in_specs=[vmem] * 4,
        out_specs=vmem,
        scratch_shapes=[
            pltpu.VMEM((width, size + 2 * chan, lanes), BF16),
            pltpu.VMEM((width + 2, size, lanes), F32),
        ],
        name="input",
    )(own, near, far, w_conv)


def unpack_kernel(mine_ref, other_ref, conv_ref, q_ref, k_ref, v_ref, o_ref, gain_ref, pack_s):
    size = mine_ref.shape[0]
    chan = q_ref.shape[0]
    odd = row_is_odd()
    pack_s[pl.ds(pl.multiple_of(odd * size, 8), size)] = mine_ref[...]
    pack_s[pl.ds(pl.multiple_of((1 - odd) * size, 8), size)] = other_ref[...]
    q_ref[...] = pack_s[:chan, :chan]
    k_ref[...] = pack_s[:chan, chan:]
    v_ref[...] = pack_s[chan : 2 * chan, :chan]
    o_ref[...] = pack_s[chan : 2 * chan, chan:]
    gain_ref[...] = pack_s[2 * chan : 2 * chan + 1, :chan]
    at = 2 * chan + 8
    half = 3 * chan // 2
    for j in range(3):
        top = (2 - j) * chan
        for i in range(2):
            conv_ref[i, j] = pack_s[at + top : at + top + chan, i * chan : (i + 1) * chan]
        for low in range(0, chan, chan // 2):
            row = top + low
            side = row // half
            start = at + 3 * chan + row - side * half
            conv_ref[2, j, low : low + chan // 2] = pack_s[
                start : start + chan // 2, side * chan : (side + 1) * chan
            ]


def unpack(mine, other, chan):
    vmem = pl.BlockSpec(memory_space=pltpu.VMEM)
    square = jax.ShapeDtypeStruct((chan, chan), F32)
    return pl.pallas_call(
        unpack_kernel,
        out_shape=(
            jax.ShapeDtypeStruct((3, 3, chan, chan), F32),
            square,
            square,
            square,
            square,
            jax.ShapeDtypeStruct((1, chan), F32),
        ),
        in_specs=[vmem] * 2,
        out_specs=(vmem,) * 6,
        scratch_shapes=[pltpu.VMEM((2 * mine.shape[0], 2 * chan), F32)],
        name="unpack",
    )(mine, other)


def angular_kernel(
    scale,
    lag,
    pieces,
    *refs,
):
    wires_in = refs[:pieces]
    cot_ref, keep_ref, gain_row, wq_ref, wkey_ref, wv_ref, wo_ref = refs[pieces : pieces + 7]
    refs = refs[pieces + 7 :]
    wires_out = refs[:pieces]
    out_ref, g_ref, ggain_ref, held_s, bias_ref, gain_ref, wqkv_ref, wk_ref, wot_ref, wcat_ref = (
        refs[pieces : pieces + 10]
    )
    give_s = refs[pieces + 10]
    scratch = refs[pieces + 11 :]
    blocks = held_s.shape[0]
    pixels, chan, lanes = cot_ref.shape
    used = keep_ref.shape[1]
    each = used // blocks
    rows = bias_ref.shape[0]
    slots = len(scratch) // 6
    inv_chan = 1.0 / chan
    take(wires_in, held_s)
    live = jnp.where(keep_ref[...] > 0, 0.0, -1e30).astype(F32)
    live = jnp.concatenate([live, jnp.full((1, lanes - used), -1e30, F32)], axis=1)
    live = jnp.transpose(jnp.broadcast_to(live, (128, lanes)))[:rows]
    lane = lax.broadcasted_iota(jnp.int32, (rows, 128), 1)
    bias_ref[...] = jnp.where(lane == chan, live, 0.0)[:, : 2 * chan]
    eye = lax.broadcasted_iota(jnp.int32, (chan, chan), 0) == lax.broadcasted_iota(
        jnp.int32, (chan, chan), 1
    )
    gain_ref[...] = jnp.sum(jnp.where(eye, gain_row[...], 0.0), axis=1, keepdims=True)
    w_q, w_k, w_v = (ref[...].astype(F32) for ref in (wq_ref, wkey_ref, wv_ref))
    wqkv_ref[...] = jnp.concatenate(
        [jnp.transpose(w_q), jnp.transpose(w_k), jnp.transpose(w_v)], axis=0
    ).astype(BF16)
    wcat_ref[...] = jnp.concatenate([w_q, w_k, w_v], axis=1).astype(BF16)
    wk_ref[...] = jnp.concatenate([w_k, jnp.zeros((chan, chan), F32)], axis=1).astype(BF16)
    wot_ref[...] = jnp.transpose(wo_ref[...].astype(F32)).astype(BF16)
    for slot in range(slots):
        s_s, e_s, g_s, n_s, t_s, x_s = scratch[6 * slot : 6 * slot + 6]
        e_s[rows:] = jnp.zeros((lanes - rows, lanes), BF16)
        g_s[rows:] = jnp.zeros((lanes - rows, lanes), BF16)
    chunks = []
    at = 0
    while at < rows:
        size = min(80, rows - at)
        chunks.append((at, size))
        at += size
    sums = {}

    def add(name, value):
        sums[name] = value if name not in sums else sums[name] + value

    def pixel(p):
        s_s, e_s, g_s, n_s, t_s, x_s = scratch[6 * (p % slots) : 6 * (p % slots) + 6]
        cells = [held_s[b, :, p * each : (p + 1) * each] for b in range(blocks)]
        if lanes > used:
            cells.append(jnp.zeros((chan, lanes - used), F32))
        s = jnp.concatenate(cells, axis=1)
        x_s[...] = s
        cen = s - jnp.sum(s, axis=0, keepdims=True) * inv_chan
        rstd = lax.rsqrt(jnp.sum(cen * cen, axis=0, keepdims=True) * inv_chan + 1e-05)
        normed = cen * rstd
        n_s[...] = normed
        nin32 = normed * gain_ref[...]
        nin = nin32.astype(BF16)
        t_s[...] = jnp.transpose(nin32).astype(BF16)
        yield
        qkv = dot(wqkv_ref[...], nin)
        q = (qkv[:chan].astype(BF16).astype(F32) * scale).astype(BF16)
        q_aug = jnp.concatenate([q, jnp.ones((16, lanes), BF16), jnp.zeros((chan - 16, lanes), BF16)], axis=0)
        k = qkv[chan : 2 * chan].astype(BF16)
        v = qkv[2 * chan :].astype(BF16)
        yield
        high = None
        for at, size in chunks:
            k_t = (dot(t_s[at : at + size], wk_ref[...]) + bias_ref[at : at + size]).astype(BF16)
            sc = dot(k_t, q_aug)
            s_s[at : at + size] = sc
            top = jnp.max(sc.reshape(size // 8, 8, lanes), axis=0)
            high = top if high is None else jnp.maximum(high, top)
            yield
        high = jnp.max(high, axis=0, keepdims=True)
        cot = cot_ref[p]
        d_att32 = dot(wo_ref[...], cot).astype(BF16).astype(F32)
        for at, size in chunks:
            e_s[at : at + size] = jnp.exp(s_s[at : at + size] - high).astype(BF16)
            yield
        v_aug = jnp.concatenate([v, jnp.ones((16, lanes), BF16)], axis=0)
        att_aug = dot(v_aug, e_s[...])
        inv = 1.0 / att_aug[chan : chan + 1]
        att = att_aug[:chan] * inv
        att_b = att.astype(BF16)
        d_att = (d_att32 * inv).astype(BF16)
        inner = jnp.sum(att * d_att.astype(F32), axis=0, keepdims=True)
        yield
        for at, size in chunks:
            v_t = dot(t_s[at : at + size], wv_ref[...]).astype(BF16)
            dp = dot(v_t, d_att)
            g_s[at : at + size] = e_s[at : at + size] * (dp - inner).astype(BF16)
            yield
        out_ref[p] = (x_s[...] + dot(wot_ref[...], att_b)).astype(BF16)[:, :used]
        d_v = dot(d_att, e_s[...], (1, 1)).astype(BF16)
        yield
        d_q = (dot(k, g_s[...]) * scale).astype(BF16)
        yield
        d_k = dot(q, g_s[...], (1, 1)).astype(BF16)
        d_qkv = jnp.concatenate([d_q, d_k, d_v], axis=0)
        yield
        dn = dot(wcat_ref[...], d_qkv)
        normed = n_s[...]
        nin = (normed * gain_ref[...]).astype(BF16)
        both = dot(
            jnp.concatenate([nin, att_b], axis=0),
            jnp.concatenate([d_q, d_k, d_v, cot], axis=0),
            (1, 1),
        )
        add("qkv", both[:chan, : 2 * chan])
        lane = lax.broadcasted_iota(jnp.int32, (chan, 2 * chan), 1)
        add("vo", jnp.where(lane < chan, both[:chan, 2 * chan :], both[chan:, 2 * chan :]))
        yield
        dnn = dn * normed
        add("gain", dnn)
        scaled = dn * gain_ref[...]
        back = (
            scaled
            - jnp.sum(scaled, axis=0, keepdims=True) * inv_chan
            - normed * (jnp.sum(dnn * gain_ref[...], axis=0, keepdims=True) * inv_chan)
        )
        done = cot.astype(F32) + back * rstd
        for b in range(blocks):
            give_s[b, :, p * each : (p + 1) * each] = done[:, b * each : (b + 1) * each]
        yield

    waiting = [pixel(p) for p in range(pixels)]
    active = []
    step = 0
    while waiting or active:
        if waiting and step % lag == 0:
            active.append(waiting.pop(0))
        for run in list(active):
            try:
                next(run)
            except StopIteration:
                active.remove(run)
        step += 1
    g_ref[:chan] = sums["qkv"]
    g_ref[chan:] = sums["vo"]
    g_gain = jnp.sum(sums["gain"], axis=1, keepdims=True)
    g_gain = jnp.sum(jnp.where(eye, g_gain, 0.0), axis=0, keepdims=True)
    g_gain = jnp.concatenate([g_gain, jnp.zeros((1, chan), F32)], axis=1)
    ggain_ref[...] = jnp.broadcast_to(g_gain, ggain_ref.shape)
    give(wires_out, give_s)


def angular(wires, cotangent, keep, gain, w_query, w_key, w_value, w_out, blocks):
    pixels, chan, lanes = cotangent.shape
    used = keep.shape[0]
    rows = round_up(used, 16)
    wire = wires[0].shape[-1]
    vmem = pl.BlockSpec(memory_space=pltpu.VMEM)
    scale = 1.0 / math.sqrt(chan)
    shapes = wire_shapes(blocks, chan, wire) + [
        jax.ShapeDtypeStruct((pixels, chan, used), BF16),
        jax.ShapeDtypeStruct((2 * chan, 2 * chan), F32),
        jax.ShapeDtypeStruct((8, 2 * chan), F32),
    ]
    *out, output, g_weights, g_gain = pl.pallas_call(
        functools.partial(angular_kernel, scale, 10, len(wires)),
        out_shape=shapes,
        in_specs=[vmem] * (len(wires) + 7),
        out_specs=[vmem] * len(shapes),
        scratch_shapes=[
            pltpu.VMEM((blocks, chan, wire), F32),
            pltpu.VMEM((rows, 2 * chan), F32),
            pltpu.VMEM((chan, 1), F32),
            pltpu.VMEM((3 * chan, chan), BF16),
            pltpu.VMEM((chan, 2 * chan), BF16),
            pltpu.VMEM((chan, chan), BF16),
            pltpu.VMEM((chan, 3 * chan), BF16),
            pltpu.VMEM((blocks, chan, wire), F32),
        ]
        + [
            pltpu.VMEM((rows, lanes), F32),
            pltpu.VMEM((lanes, lanes), BF16),
            pltpu.VMEM((lanes, lanes), BF16),
            pltpu.VMEM((chan, lanes), F32),
            pltpu.VMEM((lanes, chan), BF16),
            pltpu.VMEM((chan, lanes), F32),
        ]
        * 2,
        name="angular",
    )(*wires, cotangent, keep[None, :], gain[None, :], w_query, w_key, w_value, w_out)
    return out, output, g_weights, g_gain


def reduce_views(own):
    count = lax.axis_size("view")
    if not pairwise(count):
        return lax.psum(own, "view")
    own = own.astype(BF16)
    parts = [own] + [swap(own, "view", step) for step in range(1, count)]
    total = 0.0
    for part in parts:
        total = total + part.astype(F32)
    return total


def reduce_rows(own):
    count = lax.axis_size("row")
    step = 2
    while step < count:
        own = own + swap(own, "row", step)
        step *= 2
    return own


def body(inputs, cotangent, keep, w_conv, gain, w_query, w_key, w_value, w_out):
    chan, view_dev, row_dev, width = inputs.shape
    blocks = lax.axis_size("view")
    breadth = width // blocks
    views = view_dev * blocks
    lanes = round_up(views, 128)
    pixels = row_dev * breadth
    odd = row_is_odd() > 0
    x = jnp.transpose(inputs, (3, 2, 0, 1))
    first, last = x[:, 0], x[:, row_dev - 1]
    near, far = halo_swap(jnp.where(odd, first, last), jnp.where(odd, last, first))
    w_conv = jnp.transpose(w_conv, (2, 3, 0, 1))
    x = x.reshape(width, row_dev * chan, view_dev)
    wires, frame = convolve(x, near, far, w_conv, blocks)
    wires = exchange(wires)
    cot = jnp.transpose(cotangent, (2, 3, 0, 1)).reshape(pixels, chan, views)
    cot = jnp.pad(cot, ((0, 0), (0, 0), (0, lanes - views)))
    wires, output, g_weights, g_gain = angular(
        wires, cot, keep, gain, w_query, w_key, w_value, w_out, blocks
    )
    wires = exchange(wires)
    output = jnp.transpose(output.reshape(row_dev, breadth, chan, views), (2, 3, 0, 1))
    near, far, own, kept, sent = weight_grads(wires, frame, g_weights, g_gain, view_dev, blocks)
    near, far = halo_swap(near, far)
    part = reduce_rows(kept + swap(sent, "row", 1))
    part = reduce_views(part)
    g_conv, g_query, g_key, g_value, g_out, g_gain = unpack(part, swap(part, "row", 1), chan)
    d_input = input_grad(own, near, far, w_conv, view_dev)
    d_input = jnp.transpose(d_input, (2, 3, 0, 1))
    g_conv = jnp.transpose(g_conv, (2, 3, 0, 1))
    return (output, d_input, g_conv, g_gain[0], g_query, g_key, g_value, g_out)


def solution(mesh):
    placed = (
        P(None, "view", ("groups", "row"), None),
        P(None, None, ("groups", "row"), "view"),
        P("groups"),
        P(),
        P(),
        P(),
        P(),
        P(),
        P(),
    )
    return jax.shard_map(
        body,
        mesh=mesh,
        in_specs=placed,
        out_specs=(
            P(None, None, ("groups", "row"), "view"),
            P(None, "view", ("groups", "row"), None),
            P("groups", None, None, None),
            P("groups"),
            P("groups", None),
            P("groups", None),
            P("groups", None),
            P("groups", None),
        ),
        check_vma=False,
    )
```

```python
import functools
import math

import jax
import jax.numpy as jnp
from jax import lax
from jax.experimental import pallas as pl
from jax.experimental.pallas import tpu as pltpu
from jax.sharding import PartitionSpec as P

F32 = jnp.float32
BF16 = jnp.bfloat16


def round_up(value, unit):
    return -(-value // unit) * unit


def dot(left, right, contract=(1, 0)):
    return lax.dot_general(
        left, right, (((contract[0],), (contract[1],)), ((), ())), preferred_element_type=F32
    )


def pairwise(count):
    return count <= 8 and count & (count - 1) == 0


def swap(cells, axis, step):
    count = lax.axis_size(axis)
    return lax.ppermute(cells, axis, [(i, i ^ step) for i in range(count)])


def halo_swap(near, far):
    count = lax.axis_size("row")
    pairs = []
    for i in range(1, count - 1, 2):
        pairs += [(i, i + 1), (i + 1, i)]
    got_near = lax.ppermute(near, "row", [(i, i ^ 1) for i in range(count)])
    got_far = lax.ppermute(far, "row", pairs) if pairs else jnp.zeros_like(far)
    return got_near, got_far


def row_is_odd():
    return lax.rem(lax.axis_index("row"), 2)


def give(refs, held):
    if len(refs) == 1:
        refs[0][...] = held[...].astype(refs[0].dtype)
        return
    me = lax.axis_index("view")
    for step, ref in enumerate(refs):
        ref[...] = held[me ^ step].astype(ref.dtype)


def take(refs, held):
    if len(refs) == 1:
        held[...] = refs[0][...].astype(held.dtype)
        return
    me = lax.axis_index("view")
    for step, ref in enumerate(refs):
        held[me ^ step] = ref[...].astype(held.dtype)


def here(blocks, *arrays):
    if not pairwise(blocks):
        return arrays
    return [pltpu.with_memory_space_constraint(array, pltpu.VMEM) for array in arrays]


def grant(blocks):
    return pltpu.CompilerParams(vmem_limit_bytes=(24 << 20) if pairwise(blocks) else None)


def held(blocks, shape, dtype):
    return (pltpu.VMEM if pairwise(blocks) else jax.ShapeDtypeStruct)(shape, dtype)


def wire_shapes(blocks, chan, lanes):
    if pairwise(blocks):
        return [held(blocks, (chan, lanes), BF16)] * blocks
    return [held(blocks, (blocks, chan, lanes), BF16)]


def exchange(wires):
    if len(wires) == 1:
        return [lax.all_to_all(wires[0], "view", split_axis=0, concat_axis=0, tiled=True)]
    return [wires[0]] + [swap(wires[step], "view", step) for step in range(1, len(wires))]


def taps(w_ref, rows, forward):
    chan = w_ref.shape[2]
    blank = jnp.zeros((chan, chan), F32)
    found = {}
    for i in range(3):
        for j in range(3):
            tap = w_ref[i, j].astype(F32)
            found[i, j] = tap if forward else jnp.transpose(tap)
    bands = []
    for j in range(3):
        for r in range(rows):
            row = []
            for place in range(rows + 2):
                i = place - r if forward else r + 2 - place
                row.append(found[i, j] if 0 <= i < 3 else blank)
            bands.append(jnp.concatenate(row, axis=1))
    return jnp.concatenate(bands, axis=0).astype(BF16)


def spread(frame_ref, acc_ref, weights, rows, forward):
    width, deep, lanes = frame_ref.shape
    chan = deep // (rows + 2)
    size = rows * chan
    acc_ref[...] = jnp.zeros_like(acc_ref)

    def pair(q, carry):
        two = jnp.concatenate([frame_ref[2 * q], frame_ref[2 * q + 1]], axis=1)
        part = dot(weights, two)
        for j in range(3):
            move = 1 - j if forward else j - 1
            for side in range(2):
                acc_ref[2 * q + side + move + 1] += part[
                    j * size : (j + 1) * size, side * lanes : (side + 1) * lanes
                ]
        return carry

    lax.fori_loop(0, width // 2, pair, 0, unroll=width <= 16)


def conv_kernel(blocks, x_ref, near_ref, far_ref, w_ref, *refs):
    *wires, frame_ref, acc_s, held_s = refs
    rows, width, chan, views = x_ref.shape
    own = rows * chan
    lanes = frame_ref.shape[2]
    odd = row_is_odd() > 0
    frame_ref[...] = jnp.zeros_like(frame_ref)

    def fill(w, carry):
        near, far = near_ref[w], far_ref[w]
        frame_ref[w, :chan, :views] = jnp.where(odd, near, far)
        for r in range(rows):
            frame_ref[w, (r + 1) * chan : (r + 2) * chan, :views] = x_ref[r, w]
        frame_ref[w, chan + own :, :views] = jnp.where(odd, far, near)
        return carry

    lax.fori_loop(0, width, fill, 0, unroll=width <= 16)
    weights = taps(w_ref, rows, True)
    spread(frame_ref, acc_s, weights, rows, True)
    breadth = width // blocks

    def block(b, carry):
        cells = []
        for r in range(rows):
            for k in range(breadth):
                w = b * breadth + k
                value = acc_s[w + 1, r * chan : (r + 1) * chan]
                value = value + frame_ref[w, (r + 1) * chan : (r + 2) * chan].astype(F32)
                cells.append(value[:, :views])
        cells = jnp.concatenate(cells, axis=1)
        held_s[b, :, : cells.shape[1]] = cells
        return carry

    lax.fori_loop(0, blocks, block, 0, unroll=blocks <= 4)
    give(wires, held_s)


def convolve(x, near, far, w_conv, blocks):
    rows, width, chan, views = x.shape
    own = rows * chan
    lanes = round_up(views, 128)
    wire = round_up(rows * (width // blocks) * views, 128)
    vmem = pl.BlockSpec(memory_space=pltpu.VMEM)
    shapes = wire_shapes(blocks, chan, wire)
    shapes = shapes + [held(blocks, (width, own + 2 * chan, lanes), BF16)]
    *wires, frame = pl.pallas_call(
        functools.partial(conv_kernel, blocks),
        out_shape=shapes,
        in_specs=[vmem] * 4,
        out_specs=[vmem] * len(shapes),
        scratch_shapes=[
            pltpu.VMEM((width + 2, own, lanes), F32),
            pltpu.VMEM((blocks, chan, wire), F32),
        ],
        name="conv",
        compiler_params=grant(blocks),
    )(*here(blocks, x, near, far), w_conv)
    return wires, frame


def weight_kernel(count, pieces, *refs):
    wires = refs[:pieces]
    frame_ref, g_ref, gain_ref = refs[pieces : pieces + 3]
    near_ref, far_ref, own_ref, keep_ref, send_ref, held_s, col_s, pack_s = refs[pieces + 3 :]
    width, own, lanes = own_ref.shape
    blocks, chan, wire = held_s.shape
    rows = own // chan
    breadth = width // blocks
    views = count
    odd = row_is_odd()
    take(wires, held_s)
    col_s[0] = jnp.zeros((own, lanes), BF16)
    col_s[width + 1] = jnp.zeros((own, lanes), BF16)

    def block(b, carry):
        cells = held_s[b]
        for r in range(rows):
            for k in range(breadth):
                at = (r * breadth + k) * views
                value = cells[:, at : at + views]
                if lanes > views:
                    value = jnp.concatenate(
                        [value, jnp.zeros((chan, lanes - views), F32)], axis=1
                    )
                col_s[b * breadth + k + 1, r * chan : (r + 1) * chan] = value.astype(BF16)
        return carry

    lax.fori_loop(0, blocks, block, 0, unroll=blocks <= 4)

    def copy(w, carry):
        cells = col_s[w + 1]
        own_ref[w] = cells
        first, last = cells[:chan], cells[own - chan :]
        near_ref[w] = jnp.where(odd > 0, first, last)
        far_ref[w] = jnp.where(odd > 0, last, first)
        return carry

    lax.fori_loop(0, width, copy, 0, unroll=width <= 16)

    def pair(q, total):
        left, right = [], []
        for side in range(2):
            w = 2 * q + side
            left.append(jnp.concatenate([col_s[w], col_s[w + 1], col_s[w + 2]], axis=0))
            right.append(frame_ref[w])
        return total + dot(
            jnp.concatenate(left, axis=1), jnp.concatenate(right, axis=1), (1, 1)
        )

    total = lax.fori_loop(
        0,
        width // 2,
        pair,
        jnp.zeros((3 * own, own + 2 * chan), F32),
        unroll=width <= 16,
    )
    bands = []
    for shift in range(3):
        band = 0.0
        for r in range(rows):
            top = (shift * rows + r) * chan
            band = band + total[top : top + chan, r * chan : (r + 3) * chan]
        bands.append(band)
    g_conv = jnp.concatenate(bands, axis=0)
    edge = 2 * chan
    pack_s[...] = jnp.zeros_like(pack_s)
    pack_s[: 2 * chan] = g_ref[...]
    pack_s[2 * chan : 2 * chan + 8] = gain_ref[...]
    at = 2 * chan + 8
    pack_s[at : at + 3 * chan] = g_conv[:, :edge]
    half = 3 * chan // 2
    rest = g_conv[:, edge:]
    pack_s[at + 3 * chan : at + 3 * chan + half] = jnp.concatenate(
        [rest[:half], rest[half:]], axis=1
    )
    size = keep_ref.shape[0]
    keep_ref[...] = pack_s[pl.ds(pl.multiple_of(odd * size, 8), size)]
    send_ref[...] = pack_s[pl.ds(pl.multiple_of((1 - odd) * size, 8), size)]


def weight_grads(wires, frame, g_weights, g_gain, views, blocks):
    width, deep, lanes = frame.shape
    chan, wire = wires[0].shape[-2:]
    own = deep - 2 * chan
    size = round_up(2 * chan + 8 + 9 * chan // 2, 32) // 2
    vmem = pl.BlockSpec(memory_space=pltpu.VMEM)
    return pl.pallas_call(
        functools.partial(weight_kernel, views, len(wires)),
        out_shape=(
            held(blocks, (width, chan, lanes), BF16),
            held(blocks, (width, chan, lanes), BF16),
            held(blocks, (width, own, lanes), BF16),
            held(blocks, (size, 2 * chan), F32),
            held(blocks, (size, 2 * chan), F32),
        ),
        in_specs=[vmem] * (len(wires) + 3),
        out_specs=(vmem,) * 5,
        scratch_shapes=[
            pltpu.VMEM((blocks, chan, wire), F32),
            pltpu.VMEM((width + 2, own, lanes), BF16),
            pltpu.VMEM((2 * size, 2 * chan), F32),
        ],
        name="weights",
        compiler_params=grant(blocks),
    )(*here(blocks, *wires, frame, g_weights, g_gain))


def input_kernel(own_ref, near_ref, far_ref, w_ref, out_ref, frame_s, acc_s):
    width, own, lanes = own_ref.shape
    chan = near_ref.shape[1]
    rows = own // chan
    views = out_ref.shape[3]
    odd = row_is_odd() > 0

    def fill(w, carry):
        near, far = near_ref[w], far_ref[w]
        frame_s[w, :chan] = jnp.where(odd, near, far)
        frame_s[w, chan : chan + own] = own_ref[w]
        frame_s[w, chan + own :] = jnp.where(odd, far, near)
        return carry

    lax.fori_loop(0, width, fill, 0, unroll=width <= 16)
    spread(frame_s, acc_s, taps(w_ref, rows, False), rows, False)

    def columns(q, carry):
        at = pl.multiple_of(16 * q, 16)
        cells = []
        for k in range(16):
            cells.append(acc_s[at + k + 1] + own_ref[at + k].astype(F32))
        cells = jnp.swapaxes(jnp.stack(cells), 0, 1).astype(BF16)
        for r in range(rows):
            out_ref[:, r, pl.ds(at, 16), :] = cells[r * chan : (r + 1) * chan, :, :views]
        return carry

    lax.fori_loop(0, width // 16, columns, 0)


def input_grad(own, near, far, w_conv, views, blocks):
    width, size, lanes = own.shape
    chan = near.shape[1]
    vmem = pl.BlockSpec(memory_space=pltpu.VMEM)
    return pl.pallas_call(
        input_kernel,
        out_shape=jax.ShapeDtypeStruct((chan, size // chan, width, views), BF16),
        in_specs=[vmem] * 4,
        out_specs=vmem,
        scratch_shapes=[
            pltpu.VMEM((width, size + 2 * chan, lanes), BF16),
            pltpu.VMEM((width + 2, size, lanes), F32),
        ],
        name="input",
        compiler_params=grant(blocks),
    )(*here(blocks, own, near, far), w_conv)


def unpack_kernel(mine_ref, other_ref, conv_ref, q_ref, k_ref, v_ref, o_ref, gain_ref, pack_s):
    size = mine_ref.shape[0]
    chan = q_ref.shape[0]
    odd = row_is_odd()
    pack_s[pl.ds(pl.multiple_of(odd * size, 8), size)] = mine_ref[...]
    pack_s[pl.ds(pl.multiple_of((1 - odd) * size, 8), size)] = other_ref[...]
    q_ref[...] = pack_s[:chan, :chan]
    k_ref[...] = pack_s[:chan, chan:]
    v_ref[...] = pack_s[chan : 2 * chan, :chan]
    o_ref[...] = pack_s[chan : 2 * chan, chan:]
    gain_ref[...] = pack_s[2 * chan : 2 * chan + 1, :chan]
    at = 2 * chan + 8
    half = 3 * chan // 2
    for j in range(3):
        top = (2 - j) * chan
        for i in range(2):
            conv_ref[i, j] = pack_s[at + top : at + top + chan, i * chan : (i + 1) * chan]
        for low in range(0, chan, chan // 2):
            row = top + low
            side = row // half
            start = at + 3 * chan + row - side * half
            conv_ref[2, j, low : low + chan // 2] = pack_s[
                start : start + chan // 2, side * chan : (side + 1) * chan
            ]


def unpack(mine, other, chan, blocks):
    vmem = pl.BlockSpec(memory_space=pltpu.VMEM)
    square = jax.ShapeDtypeStruct((chan, chan), F32)
    return pl.pallas_call(
        unpack_kernel,
        out_shape=(
            jax.ShapeDtypeStruct((3, 3, chan, chan), F32),
            square,
            square,
            square,
            square,
            jax.ShapeDtypeStruct((1, chan), F32),
        ),
        in_specs=[vmem] * 2,
        out_specs=(vmem,) * 6,
        scratch_shapes=[pltpu.VMEM((2 * mine.shape[0], 2 * chan), F32)],
        name="unpack",
        compiler_params=grant(blocks),
    )(*here(blocks, mine, other))


def angular_kernel(
    scale,
    lag,
    pieces,
    *refs,
):
    wires_in = refs[:pieces]
    cot_ref, keep_ref, gain_row, wq_ref, wkey_ref, wv_ref, wo_ref = refs[pieces : pieces + 7]
    refs = refs[pieces + 7 :]
    wires_out = refs[:pieces]
    out_ref, g_ref, ggain_ref, held_s, bias_ref, gain_ref, wqkv_ref, wk_ref, wot_ref, wcat_ref = (
        refs[pieces : pieces + 10]
    )
    give_s = refs[pieces + 10]
    scratch = refs[pieces + 11 :]
    blocks = held_s.shape[0]
    pixels, chan, lanes = cot_ref.shape
    used = keep_ref.shape[1]
    each = used // blocks
    rows = bias_ref.shape[0]
    slots = len(scratch) // 6
    inv_chan = 1.0 / chan
    take(wires_in, held_s)
    live = jnp.where(keep_ref[...] > 0, 0.0, -1e30).astype(F32)
    live = jnp.concatenate([live, jnp.full((1, lanes - used), -1e30, F32)], axis=1)
    live = jnp.transpose(jnp.broadcast_to(live, (128, lanes)))[:rows]
    lane = lax.broadcasted_iota(jnp.int32, (rows, 128), 1)
    bias_ref[...] = jnp.where(lane == chan, live, 0.0)[:, : 2 * chan]
    eye = lax.broadcasted_iota(jnp.int32, (chan, chan), 0) == lax.broadcasted_iota(
        jnp.int32, (chan, chan), 1
    )
    gain_ref[...] = jnp.sum(jnp.where(eye, gain_row[...], 0.0), axis=1, keepdims=True)
    w_q, w_k, w_v = (ref[...].astype(F32) for ref in (wq_ref, wkey_ref, wv_ref))
    wqkv_ref[...] = jnp.concatenate(
        [jnp.transpose(w_q), jnp.transpose(w_k), jnp.transpose(w_v)], axis=0
    ).astype(BF16)
    wcat_ref[...] = jnp.concatenate([w_q, w_k, w_v], axis=1).astype(BF16)
    wk_ref[...] = jnp.concatenate([w_k, jnp.zeros((chan, chan), F32)], axis=1).astype(BF16)
    wot_ref[...] = jnp.transpose(wo_ref[...].astype(F32)).astype(BF16)
    for slot in range(slots):
        s_s, e_s, g_s, n_s, t_s, x_s = scratch[6 * slot : 6 * slot + 6]
        e_s[rows:] = jnp.zeros((lanes - rows, lanes), BF16)
        g_s[rows:] = jnp.zeros((lanes - rows, lanes), BF16)
    chunks = []
    at = 0
    while at < rows:
        size = min(80, rows - at)
        chunks.append((at, size))
        at += size
    sums = {}

    def add(name, value):
        sums[name] = value if name not in sums else sums[name] + value

    def pixel(p):
        s_s, e_s, g_s, n_s, t_s, x_s = scratch[6 * (p % slots) : 6 * (p % slots) + 6]
        cells = [held_s[b, :, p * each : (p + 1) * each] for b in range(blocks)]
        if lanes > used:
            cells.append(jnp.zeros((chan, lanes - used), F32))
        s = jnp.concatenate(cells, axis=1)
        x_s[...] = s
        cen = s - jnp.sum(s, axis=0, keepdims=True) * inv_chan
        rstd = lax.rsqrt(jnp.sum(cen * cen, axis=0, keepdims=True) * inv_chan + 1e-05)
        normed = cen * rstd
        n_s[...] = normed
        nin32 = normed * gain_ref[...]
        nin = nin32.astype(BF16)
        t_s[...] = jnp.transpose(nin32).astype(BF16)
        yield
        qkv = dot(wqkv_ref[...], nin)
        q = (qkv[:chan].astype(BF16).astype(F32) * scale).astype(BF16)
        q_aug = jnp.concatenate([q, jnp.ones((16, lanes), BF16), jnp.zeros((chan - 16, lanes), BF16)], axis=0)
        k = qkv[chan : 2 * chan].astype(BF16)
        v = qkv[2 * chan :].astype(BF16)
        yield
        high = None
        for at, size in chunks:
            k_t = (dot(t_s[at : at + size], wk_ref[...]) + bias_ref[at : at + size]).astype(BF16)
            sc = dot(k_t, q_aug)
            s_s[at : at + size] = sc
            top = jnp.max(sc.reshape(size // 8, 8, lanes), axis=0)
            high = top if high is None else jnp.maximum(high, top)
            yield
        high = jnp.max(high, axis=0, keepdims=True)
        cot = cot_ref[p]
        d_att32 = dot(wo_ref[...], cot).astype(BF16).astype(F32)
        for at, size in chunks:
            e_s[at : at + size] = jnp.exp(s_s[at : at + size] - high).astype(BF16)
            yield
        v_aug = jnp.concatenate([v, jnp.ones((16, lanes), BF16)], axis=0)
        att_aug = dot(v_aug, e_s[...])
        inv = 1.0 / att_aug[chan : chan + 1]
        att = att_aug[:chan] * inv
        att_b = att.astype(BF16)
        d_att = (d_att32 * inv).astype(BF16)
        inner = jnp.sum(att * d_att.astype(F32), axis=0, keepdims=True)
        yield
        for at, size in chunks:
            v_t = dot(t_s[at : at + size], wv_ref[...]).astype(BF16)
            dp = dot(v_t, d_att)
            g_s[at : at + size] = e_s[at : at + size] * (dp - inner).astype(BF16)
            yield
        out_ref[p] = (x_s[...] + dot(wot_ref[...], att_b)).astype(BF16)[:, :used]
        d_v = dot(d_att, e_s[...], (1, 1)).astype(BF16)
        yield
        d_q = (dot(k, g_s[...]) * scale).astype(BF16)
        yield
        d_k = dot(q, g_s[...], (1, 1)).astype(BF16)
        d_qkv = jnp.concatenate([d_q, d_k, d_v], axis=0)
        yield
        dn = dot(wcat_ref[...], d_qkv)
        normed = n_s[...]
        nin = (normed * gain_ref[...]).astype(BF16)
        both = dot(
            jnp.concatenate([nin, att_b], axis=0),
            jnp.concatenate([d_q, d_k, d_v, cot], axis=0),
            (1, 1),
        )
        add("qkv", both[:chan, : 2 * chan])
        lane = lax.broadcasted_iota(jnp.int32, (chan, 2 * chan), 1)
        add("vo", jnp.where(lane < chan, both[:chan, 2 * chan :], both[chan:, 2 * chan :]))
        yield
        dnn = dn * normed
        add("gain", dnn)
        scaled = dn * gain_ref[...]
        back = (
            scaled
            - jnp.sum(scaled, axis=0, keepdims=True) * inv_chan
            - normed * (jnp.sum(dnn * gain_ref[...], axis=0, keepdims=True) * inv_chan)
        )
        done = cot.astype(F32) + back * rstd
        for b in range(blocks):
            give_s[b, :, p * each : (p + 1) * each] = done[:, b * each : (b + 1) * each]
        yield

    waiting = [pixel(p) for p in range(pixels)]
    active = []
    step = 0
    while waiting or active:
        if waiting and step % lag == 0:
            active.append(waiting.pop(0))
        for run in list(active):
            try:
                next(run)
            except StopIteration:
                active.remove(run)
        step += 1
    g_ref[:chan] = sums["qkv"]
    g_ref[chan:] = sums["vo"]
    g_gain = jnp.sum(sums["gain"], axis=1, keepdims=True)
    g_gain = jnp.sum(jnp.where(eye, g_gain, 0.0), axis=0, keepdims=True)
    g_gain = jnp.concatenate([g_gain, jnp.zeros((1, chan), F32)], axis=1)
    ggain_ref[...] = jnp.broadcast_to(g_gain, ggain_ref.shape)
    give(wires_out, give_s)


def angular(wires, cotangent, keep, gain, w_query, w_key, w_value, w_out, blocks):
    pixels, chan, lanes = cotangent.shape
    used = keep.shape[0]
    rows = round_up(used, 16)
    wire = wires[0].shape[-1]
    vmem = pl.BlockSpec(memory_space=pltpu.VMEM)
    scale = 1.0 / math.sqrt(chan)
    shapes = wire_shapes(blocks, chan, wire) + [
        jax.ShapeDtypeStruct((pixels, chan, used), BF16),
        held(blocks, (2 * chan, 2 * chan), F32),
        held(blocks, (8, 2 * chan), F32),
    ]
    *out, output, g_weights, g_gain = pl.pallas_call(
        functools.partial(angular_kernel, scale, 10, len(wires)),
        out_shape=shapes,
        in_specs=[vmem] * (len(wires) + 7),
        out_specs=[vmem] * len(shapes),
        scratch_shapes=[
            pltpu.VMEM((blocks, chan, wire), F32),
            pltpu.VMEM((rows, 2 * chan), F32),
            pltpu.VMEM((chan, 1), F32),
            pltpu.VMEM((3 * chan, chan), BF16),
            pltpu.VMEM((chan, 2 * chan), BF16),
            pltpu.VMEM((chan, chan), BF16),
            pltpu.VMEM((chan, 3 * chan), BF16),
            pltpu.VMEM((blocks, chan, wire), F32),
        ]
        + [
            pltpu.VMEM((rows, lanes), F32),
            pltpu.VMEM((lanes, lanes), BF16),
            pltpu.VMEM((lanes, lanes), BF16),
            pltpu.VMEM((chan, lanes), F32),
            pltpu.VMEM((lanes, chan), BF16),
            pltpu.VMEM((chan, lanes), F32),
        ]
        * 2,
        name="angular",
        compiler_params=grant(blocks),
    )(*here(blocks, *wires, cotangent), keep[None, :], gain[None, :], w_query, w_key, w_value, w_out)
    return out, output, g_weights, g_gain


def reduce_views(own):
    count = lax.axis_size("view")
    if not pairwise(count):
        return lax.psum(own, "view")
    own = own.astype(BF16)
    parts = [own] + [swap(own, "view", step) for step in range(1, count)]
    total = 0.0
    for part in parts:
        total = total + part.astype(F32)
    return total


def reduce_rows(own, beside):
    count = lax.axis_size("row")
    step = 2
    while step < count:
        other = swap(own, "row", step)
        if step == 2:
            other, beside = lax.optimization_barrier((other, beside))
        own = own + other
        step *= 2
    return own, beside


def body(inputs, cotangent, keep, w_conv, gain, w_query, w_key, w_value, w_out):
    chan, view_dev, row_dev, width = inputs.shape
    blocks = lax.axis_size("view")
    breadth = width // blocks
    views = view_dev * blocks
    lanes = round_up(views, 128)
    pixels = row_dev * breadth
    odd = row_is_odd() > 0
    x = jnp.transpose(inputs, (2, 3, 0, 1))
    first, last = x[0], x[row_dev - 1]
    near, far = halo_swap(jnp.where(odd, first, last), jnp.where(odd, last, first))
    w_conv = jnp.transpose(w_conv, (2, 3, 0, 1))
    wires, frame = convolve(x, near, far, w_conv, blocks)
    wires = exchange(wires)
    cot = jnp.transpose(cotangent, (2, 3, 0, 1)).reshape(pixels, chan, views)
    cot = jnp.pad(cot, ((0, 0), (0, 0), (0, lanes - views)))
    wires, output, g_weights, g_gain = angular(
        wires, cot, keep, gain, w_query, w_key, w_value, w_out, blocks
    )
    wires = exchange(wires)
    output = jnp.transpose(output.reshape(row_dev, breadth, chan, views), (2, 3, 0, 1))
    near, far, own, kept, sent = weight_grads(wires, frame, g_weights, g_gain, view_dev, blocks)
    other = swap(sent, "row", 1)
    near, far = halo_swap(near, far)
    part = kept + other
    d_input = input_grad(own, near, far, w_conv, view_dev, blocks)
    part, d_input = reduce_rows(part, d_input)
    part = reduce_views(part)
    other = swap(part, "row", 1)
    g_conv, g_query, g_key, g_value, g_out, g_gain = unpack(part, other, chan, blocks)
    d_input = jnp.transpose(d_input, (0, 3, 1, 2))
    g_conv = jnp.transpose(g_conv, (2, 3, 0, 1))
    return (output, d_input, g_conv, g_gain[0], g_query, g_key, g_value, g_out)


def solution(mesh):
    placed = (
        P(None, "view", ("groups", "row"), None),
        P(None, None, ("groups", "row"), "view"),
        P("groups"),
        P(),
        P(),
        P(),
        P(),
        P(),
        P(),
    )
    return jax.shard_map(
        body,
        mesh=mesh,
        in_specs=placed,
        out_specs=(
            P(None, None, ("groups", "row"), "view"),
            P(None, "view", ("groups", "row"), None),
            P("groups", None, None, None),
            P("groups"),
            P("groups", None),
            P("groups", None),
            P("groups", None),
            P("groups", None),
        ),
        check_vma=False,
    )
```

```python
import functools
import math

import jax
import jax.numpy as jnp
from jax import lax
from jax.experimental import pallas as pl
from jax.experimental.pallas import tpu as pltpu
from jax.sharding import PartitionSpec as P

F32 = jnp.float32
BF16 = jnp.bfloat16


def round_up(value, unit):
    return -(-value // unit) * unit


def dot(left, right, contract=(1, 0)):
    return lax.dot_general(
        left, right, (((contract[0],), (contract[1],)), ((), ())), preferred_element_type=F32
    )


def pairwise(count):
    return count <= 8 and count & (count - 1) == 0


def swap(cells, axis, step):
    count = lax.axis_size(axis)
    return lax.ppermute(cells, axis, [(i, i ^ step) for i in range(count)])


def halo_swap(near, far):
    count = lax.axis_size("row")
    pairs = []
    for i in range(1, count - 1, 2):
        pairs += [(i, i + 1), (i + 1, i)]
    got_near = lax.ppermute(near, "row", [(i, i ^ 1) for i in range(count)])
    got_far = lax.ppermute(far, "row", pairs) if pairs else jnp.zeros_like(far)
    return got_near, got_far


def row_is_odd():
    return lax.rem(lax.axis_index("row"), 2)


def give(refs, held):
    if len(refs) == 1:
        refs[0][...] = held[...].astype(refs[0].dtype)
        return
    me = lax.axis_index("view")
    for step, ref in enumerate(refs):
        ref[...] = held[me ^ step].astype(ref.dtype)


def take(refs, held):
    if len(refs) == 1:
        held[...] = refs[0][...].astype(held.dtype)
        return
    me = lax.axis_index("view")
    for step, ref in enumerate(refs):
        held[me ^ step] = ref[...].astype(held.dtype)


def here(blocks, *arrays):
    if not pairwise(blocks):
        return arrays
    return [pltpu.with_memory_space_constraint(array, pltpu.VMEM) for array in arrays]


def grant(blocks):
    return pltpu.CompilerParams(vmem_limit_bytes=(24 << 20) if pairwise(blocks) else None)


def held(blocks, shape, dtype):
    return (pltpu.VMEM if pairwise(blocks) else jax.ShapeDtypeStruct)(shape, dtype)


def wire_shapes(blocks, chan, lanes):
    if pairwise(blocks):
        return [held(blocks, (chan, lanes), BF16)] * blocks
    return [held(blocks, (blocks, chan, lanes), BF16)]


def exchange(wires):
    if len(wires) == 1:
        return [lax.all_to_all(wires[0], "view", split_axis=0, concat_axis=0, tiled=True)]
    return [wires[0]] + [swap(wires[step], "view", step) for step in range(1, len(wires))]


def taps(w_ref, rows, forward):
    chan = w_ref.shape[2]
    blank = jnp.zeros((chan, chan), F32)
    found = {}
    for i in range(3):
        for j in range(3):
            tap = w_ref[i, j].astype(F32)
            found[i, j] = tap if forward else jnp.transpose(tap)
    bands = []
    for j in range(3):
        for r in range(rows):
            row = []
            for place in range(rows + 2):
                i = place - r if forward else r + 2 - place
                row.append(found[i, j] if 0 <= i < 3 else blank)
            bands.append(jnp.concatenate(row, axis=1))
    return jnp.concatenate(bands, axis=0).astype(BF16)


def spread(frame_ref, acc_ref, weights, rows, forward):
    width, deep, lanes = frame_ref.shape
    chan = deep // (rows + 2)
    size = rows * chan
    acc_ref[...] = jnp.zeros_like(acc_ref)

    def pair(q, carry):
        two = jnp.concatenate([frame_ref[2 * q], frame_ref[2 * q + 1]], axis=1)
        part = dot(weights, two)
        for j in range(3):
            move = 1 - j if forward else j - 1
            for side in range(2):
                acc_ref[2 * q + side + move + 1] += part[
                    j * size : (j + 1) * size, side * lanes : (side + 1) * lanes
                ]
        return carry

    lax.fori_loop(0, width // 2, pair, 0, unroll=width <= 16)


def conv_kernel(blocks, x_ref, near_ref, far_ref, w_ref, *refs):
    *wires, frame_ref, acc_s, held_s = refs
    rows, width, chan, views = x_ref.shape
    own = rows * chan
    lanes = frame_ref.shape[2]
    odd = row_is_odd() > 0
    frame_ref[...] = jnp.zeros_like(frame_ref)

    def fill(w, carry):
        near, far = near_ref[w], far_ref[w]
        frame_ref[w, :chan, :views] = jnp.where(odd, near, far)
        for r in range(rows):
            frame_ref[w, (r + 1) * chan : (r + 2) * chan, :views] = x_ref[r, w]
        frame_ref[w, chan + own :, :views] = jnp.where(odd, far, near)
        return carry

    lax.fori_loop(0, width, fill, 0, unroll=width <= 16)
    weights = taps(w_ref, rows, True)
    spread(frame_ref, acc_s, weights, rows, True)
    breadth = width // blocks

    def block(b, carry):
        cells = []
        for r in range(rows):
            for k in range(breadth):
                w = b * breadth + k
                value = acc_s[w + 1, r * chan : (r + 1) * chan]
                value = value + frame_ref[w, (r + 1) * chan : (r + 2) * chan].astype(F32)
                cells.append(value[:, :views])
        cells = jnp.concatenate(cells, axis=1)
        held_s[b, :, : cells.shape[1]] = cells
        return carry

    lax.fori_loop(0, blocks, block, 0, unroll=blocks <= 4)
    give(wires, held_s)


def convolve(x, near, far, w_conv, blocks):
    rows, width, chan, views = x.shape
    own = rows * chan
    lanes = round_up(views, 128)
    wire = round_up(rows * (width // blocks) * views, 128)
    vmem = pl.BlockSpec(memory_space=pltpu.VMEM)
    shapes = wire_shapes(blocks, chan, wire)
    shapes = shapes + [held(blocks, (width, own + 2 * chan, lanes), BF16)]
    *wires, frame = pl.pallas_call(
        functools.partial(conv_kernel, blocks),
        out_shape=shapes,
        in_specs=[vmem] * 4,
        out_specs=[vmem] * len(shapes),
        scratch_shapes=[
            pltpu.VMEM((width + 2, own, lanes), F32),
            pltpu.VMEM((blocks, chan, wire), F32),
        ],
        name="conv",
        compiler_params=grant(blocks),
    )(*here(blocks, x, near, far), w_conv)
    return wires, frame


def weight_kernel(count, pieces, *refs):
    wires = refs[:pieces]
    frame_ref, g_ref, gain_ref = refs[pieces : pieces + 3]
    near_ref, far_ref, own_ref, keep_ref, send_ref, held_s, col_s, pack_s = refs[pieces + 3 :]
    width, own, lanes = own_ref.shape
    blocks, chan, wire = held_s.shape
    rows = own // chan
    breadth = width // blocks
    views = count
    odd = row_is_odd()
    take(wires, held_s)
    col_s[0] = jnp.zeros((own, lanes), BF16)
    col_s[width + 1] = jnp.zeros((own, lanes), BF16)

    def block(b, carry):
        cells = held_s[b]
        for r in range(rows):
            for k in range(breadth):
                at = (r * breadth + k) * views
                value = cells[:, at : at + views]
                if lanes > views:
                    value = jnp.concatenate(
                        [value, jnp.zeros((chan, lanes - views), F32)], axis=1
                    )
                col_s[b * breadth + k + 1, r * chan : (r + 1) * chan] = value.astype(BF16)
        return carry

    lax.fori_loop(0, blocks, block, 0, unroll=blocks <= 4)

    def copy(w, carry):
        cells = col_s[w + 1]
        own_ref[w] = cells
        first, last = cells[:chan], cells[own - chan :]
        near_ref[w] = jnp.where(odd > 0, first, last)
        far_ref[w] = jnp.where(odd > 0, last, first)
        return carry

    lax.fori_loop(0, width, copy, 0, unroll=width <= 16)

    def pair(q, total):
        left, right = [], []
        for side in range(2):
            w = 2 * q + side
            left.append(jnp.concatenate([col_s[w], col_s[w + 1], col_s[w + 2]], axis=0))
            right.append(frame_ref[w])
        return total + dot(
            jnp.concatenate(left, axis=1), jnp.concatenate(right, axis=1), (1, 1)
        )

    total = lax.fori_loop(
        0,
        width // 2,
        pair,
        jnp.zeros((3 * own, own + 2 * chan), F32),
        unroll=width <= 16,
    )
    bands = []
    for shift in range(3):
        band = 0.0
        for r in range(rows):
            top = (shift * rows + r) * chan
            band = band + total[top : top + chan, r * chan : (r + 3) * chan]
        bands.append(band)
    g_conv = jnp.concatenate(bands, axis=0)
    edge = 2 * chan
    pack_s[...] = jnp.zeros_like(pack_s)
    pack_s[: 2 * chan] = g_ref[...]
    pack_s[2 * chan : 2 * chan + 8] = gain_ref[...]
    at = 2 * chan + 8
    pack_s[at : at + 3 * chan] = g_conv[:, :edge]
    half = 3 * chan // 2
    rest = g_conv[:, edge:]
    pack_s[at + 3 * chan : at + 3 * chan + half] = jnp.concatenate(
        [rest[:half], rest[half:]], axis=1
    )
    size = keep_ref.shape[0]
    keep_ref[...] = pack_s[pl.ds(pl.multiple_of(odd * size, 8), size)]
    send_ref[...] = pack_s[pl.ds(pl.multiple_of((1 - odd) * size, 8), size)]


def weight_grads(wires, frame, g_weights, g_gain, views, blocks):
    width, deep, lanes = frame.shape
    chan, wire = wires[0].shape[-2:]
    own = deep - 2 * chan
    size = round_up(2 * chan + 8 + 9 * chan // 2, 32) // 2
    vmem = pl.BlockSpec(memory_space=pltpu.VMEM)
    return pl.pallas_call(
        functools.partial(weight_kernel, views, len(wires)),
        out_shape=(
            held(blocks, (width, chan, lanes), BF16),
            held(blocks, (width, chan, lanes), BF16),
            held(blocks, (width, own, lanes), BF16),
            held(blocks, (size, 2 * chan), F32),
            held(blocks, (size, 2 * chan), F32),
        ),
        in_specs=[vmem] * (len(wires) + 3),
        out_specs=(vmem,) * 5,
        scratch_shapes=[
            pltpu.VMEM((blocks, chan, wire), F32),
            pltpu.VMEM((width + 2, own, lanes), BF16),
            pltpu.VMEM((2 * size, 2 * chan), F32),
        ],
        name="weights",
        compiler_params=grant(blocks),
    )(*here(blocks, *wires, frame, g_weights, g_gain))


def input_kernel(own_ref, near_ref, far_ref, w_ref, out_ref, frame_s, acc_s):
    width, own, lanes = own_ref.shape
    chan = near_ref.shape[1]
    rows = own // chan
    views = out_ref.shape[3]
    odd = row_is_odd() > 0

    def fill(w, carry):
        near, far = near_ref[w], far_ref[w]
        frame_s[w, :chan] = jnp.where(odd, near, far)
        frame_s[w, chan : chan + own] = own_ref[w]
        frame_s[w, chan + own :] = jnp.where(odd, far, near)
        return carry

    lax.fori_loop(0, width, fill, 0, unroll=width <= 16)
    spread(frame_s, acc_s, taps(w_ref, rows, False), rows, False)

    def columns(q, carry):
        at = pl.multiple_of(16 * q, 16)
        cells = []
        for k in range(16):
            cells.append(acc_s[at + k + 1] + own_ref[at + k].astype(F32))
        cells = jnp.swapaxes(jnp.stack(cells), 0, 1).astype(BF16)
        for r in range(rows):
            out_ref[:, r, pl.ds(at, 16), :] = cells[r * chan : (r + 1) * chan, :, :views]
        return carry

    lax.fori_loop(0, width // 16, columns, 0)


def input_grad(own, near, far, w_conv, views, blocks):
    width, size, lanes = own.shape
    chan = near.shape[1]
    vmem = pl.BlockSpec(memory_space=pltpu.VMEM)
    return pl.pallas_call(
        input_kernel,
        out_shape=jax.ShapeDtypeStruct((chan, size // chan, width, views), BF16),
        in_specs=[vmem] * 4,
        out_specs=vmem,
        scratch_shapes=[
            pltpu.VMEM((width, size + 2 * chan, lanes), BF16),
            pltpu.VMEM((width + 2, size, lanes), F32),
        ],
        name="input",
        compiler_params=grant(blocks),
    )(*here(blocks, own, near, far), w_conv)


def unpack_kernel(mine_ref, other_ref, conv_ref, q_ref, k_ref, v_ref, o_ref, gain_ref, pack_s):
    size = mine_ref.shape[0]
    chan = q_ref.shape[0]
    odd = row_is_odd()
    pack_s[pl.ds(pl.multiple_of(odd * size, 8), size)] = mine_ref[...]
    pack_s[pl.ds(pl.multiple_of((1 - odd) * size, 8), size)] = other_ref[...]
    q_ref[...] = pack_s[:chan, :chan]
    k_ref[...] = pack_s[:chan, chan:]
    v_ref[...] = pack_s[chan : 2 * chan, :chan]
    o_ref[...] = pack_s[chan : 2 * chan, chan:]
    gain_ref[...] = pack_s[2 * chan : 2 * chan + 1, :chan]
    at = 2 * chan + 8
    half = 3 * chan // 2
    for j in range(3):
        top = (2 - j) * chan
        for i in range(2):
            conv_ref[i, j] = pack_s[at + top : at + top + chan, i * chan : (i + 1) * chan]
        for low in range(0, chan, chan // 2):
            row = top + low
            side = row // half
            start = at + 3 * chan + row - side * half
            conv_ref[2, j, low : low + chan // 2] = pack_s[
                start : start + chan // 2, side * chan : (side + 1) * chan
            ]


def unpack(mine, other, chan, blocks):
    vmem = pl.BlockSpec(memory_space=pltpu.VMEM)
    square = jax.ShapeDtypeStruct((chan, chan), F32)
    return pl.pallas_call(
        unpack_kernel,
        out_shape=(
            jax.ShapeDtypeStruct((3, 3, chan, chan), F32),
            square,
            square,
            square,
            square,
            jax.ShapeDtypeStruct((1, chan), F32),
        ),
        in_specs=[vmem] * 2,
        out_specs=(vmem,) * 6,
        scratch_shapes=[pltpu.VMEM((2 * mine.shape[0], 2 * chan), F32)],
        name="unpack",
        compiler_params=grant(blocks),
    )(*here(blocks, mine, other))


def angular_kernel(
    scale,
    lag,
    pieces,
    *refs,
):
    wires_in = refs[:pieces]
    cot_ref, keep_ref, gain_row, wq_ref, wkey_ref, wv_ref, wo_ref = refs[pieces : pieces + 7]
    refs = refs[pieces + 7 :]
    wires_out = refs[:pieces]
    out_ref, g_ref, ggain_ref, held_s, bias_ref, gain_ref, wqkv_ref, wk_ref, wot_ref, wcat_ref = (
        refs[pieces : pieces + 10]
    )
    give_s = refs[pieces + 10]
    scratch = refs[pieces + 11 :]
    blocks = held_s.shape[0]
    pixels, chan, lanes = cot_ref.shape
    used = keep_ref.shape[1]
    each = used // blocks
    rows = bias_ref.shape[0]
    slots = len(scratch) // 6
    inv_chan = 1.0 / chan
    take(wires_in, held_s)
    live = jnp.where(keep_ref[...] > 0, 0.0, -1e30).astype(F32)
    live = jnp.concatenate([live, jnp.full((1, lanes - used), -1e30, F32)], axis=1)
    live = jnp.transpose(jnp.broadcast_to(live, (128, lanes)))[:rows]
    lane = lax.broadcasted_iota(jnp.int32, (rows, 128), 1)
    bias_ref[...] = jnp.where(lane == chan, live, 0.0)[:, : 2 * chan]
    eye = lax.broadcasted_iota(jnp.int32, (chan, chan), 0) == lax.broadcasted_iota(
        jnp.int32, (chan, chan), 1
    )
    gain_ref[...] = jnp.sum(jnp.where(eye, gain_row[...], 0.0), axis=1, keepdims=True)
    w_q, w_k, w_v = (ref[...].astype(F32) for ref in (wq_ref, wkey_ref, wv_ref))
    wqkv_ref[...] = jnp.concatenate(
        [jnp.transpose(w_q), jnp.transpose(w_k), jnp.transpose(w_v)], axis=0
    ).astype(BF16)
    wcat_ref[...] = jnp.concatenate([w_q, w_k, w_v], axis=1).astype(BF16)
    wk_ref[...] = jnp.concatenate([w_k, jnp.zeros((chan, chan), F32)], axis=1).astype(BF16)
    wot_ref[...] = jnp.transpose(wo_ref[...].astype(F32)).astype(BF16)
    for slot in range(slots):
        s_s, e_s, g_s, n_s, t_s, x_s = scratch[6 * slot : 6 * slot + 6]
        e_s[rows:] = jnp.zeros((lanes - rows, lanes), BF16)
        g_s[rows:] = jnp.zeros((lanes - rows, lanes), BF16)
    chunks = []
    at = 0
    while at < rows:
        size = min(80, rows - at)
        chunks.append((at, size))
        at += size
    sums = {}

    def add(name, value):
        sums[name] = value if name not in sums else sums[name] + value

    def pixel(p):
        s_s, e_s, g_s, n_s, t_s, x_s = scratch[6 * (p % slots) : 6 * (p % slots) + 6]
        cells = [held_s[b, :, p * each : (p + 1) * each] for b in range(blocks)]
        if lanes > used:
            cells.append(jnp.zeros((chan, lanes - used), F32))
        s = jnp.concatenate(cells, axis=1)
        x_s[...] = s
        cen = s - jnp.sum(s, axis=0, keepdims=True) * inv_chan
        rstd = lax.rsqrt(jnp.sum(cen * cen, axis=0, keepdims=True) * inv_chan + 1e-05)
        normed = cen * rstd
        n_s[...] = normed
        nin32 = normed * gain_ref[...]
        nin = nin32.astype(BF16)
        t_s[...] = jnp.transpose(nin32).astype(BF16)
        yield
        qkv = dot(wqkv_ref[...], nin)
        q = (qkv[:chan].astype(BF16).astype(F32) * scale).astype(BF16)
        q_aug = jnp.concatenate([q, jnp.ones((16, lanes), BF16), jnp.zeros((chan - 16, lanes), BF16)], axis=0)
        k = qkv[chan : 2 * chan].astype(BF16)
        v = qkv[2 * chan :].astype(BF16)
        yield
        high = None
        for at, size in chunks:
            k_t = (dot(t_s[at : at + size], wk_ref[...]) + bias_ref[at : at + size]).astype(BF16)
            sc = dot(k_t, q_aug)
            s_s[at : at + size] = sc
            top = jnp.max(sc.reshape(size // 8, 8, lanes), axis=0)
            high = top if high is None else jnp.maximum(high, top)
            yield
        high = jnp.max(high, axis=0, keepdims=True)
        cot = cot_ref[p]
        d_att32 = dot(wo_ref[...], cot).astype(BF16).astype(F32)
        for at, size in chunks:
            e_s[at : at + size] = jnp.exp(s_s[at : at + size] - high).astype(BF16)
            yield
        v_aug = jnp.concatenate([v, jnp.ones((16, lanes), BF16)], axis=0)
        att_aug = dot(v_aug, e_s[...])
        inv = 1.0 / att_aug[chan : chan + 1]
        att = att_aug[:chan] * inv
        att_b = att.astype(BF16)
        d_att = (d_att32 * inv).astype(BF16)
        inner = jnp.sum(att * d_att.astype(F32), axis=0, keepdims=True)
        yield
        for at, size in chunks:
            v_t = dot(t_s[at : at + size], wv_ref[...]).astype(BF16)
            dp = dot(v_t, d_att)
            g_s[at : at + size] = e_s[at : at + size] * (dp - inner).astype(BF16)
            yield
        out_ref[p] = (x_s[...] + dot(wot_ref[...], att_b)).astype(BF16)[:, :used]
        d_v = dot(d_att, e_s[...], (1, 1)).astype(BF16)
        yield
        d_q = (dot(k, g_s[...]) * scale).astype(BF16)
        yield
        d_k = dot(q, g_s[...], (1, 1)).astype(BF16)
        d_qkv = jnp.concatenate([d_q, d_k, d_v], axis=0)
        yield
        dn = dot(wcat_ref[...], d_qkv)
        normed = n_s[...]
        nin = (normed * gain_ref[...]).astype(BF16)
        both = dot(
            jnp.concatenate([nin, att_b], axis=0),
            jnp.concatenate([d_q, d_k, d_v, cot], axis=0),
            (1, 1),
        )
        add("qkv", both[:chan, : 2 * chan])
        lane = lax.broadcasted_iota(jnp.int32, (chan, 2 * chan), 1)
        add("vo", jnp.where(lane < chan, both[:chan, 2 * chan :], both[chan:, 2 * chan :]))
        yield
        dnn = dn * normed
        add("gain", dnn)
        scaled = dn * gain_ref[...]
        back = (
            scaled
            - jnp.sum(scaled, axis=0, keepdims=True) * inv_chan
            - normed * (jnp.sum(dnn * gain_ref[...], axis=0, keepdims=True) * inv_chan)
        )
        done = cot.astype(F32) + back * rstd
        for b in range(blocks):
            give_s[b, :, p * each : (p + 1) * each] = done[:, b * each : (b + 1) * each]
        yield

    waiting = [pixel(p) for p in range(pixels)]
    active = []
    step = 0
    while waiting or active:
        if waiting and step % lag == 0:
            active.append(waiting.pop(0))
        for run in list(active):
            try:
                next(run)
            except StopIteration:
                active.remove(run)
        step += 1
    g_ref[:chan] = sums["qkv"]
    g_ref[chan:] = sums["vo"]
    g_gain = jnp.sum(sums["gain"], axis=1, keepdims=True)
    g_gain = jnp.sum(jnp.where(eye, g_gain, 0.0), axis=0, keepdims=True)
    g_gain = jnp.concatenate([g_gain, jnp.zeros((1, chan), F32)], axis=1)
    ggain_ref[...] = jnp.broadcast_to(g_gain, ggain_ref.shape)
    give(wires_out, give_s)


def angular(wires, cotangent, keep, gain, w_query, w_key, w_value, w_out, blocks):
    pixels, chan, lanes = cotangent.shape
    used = keep.shape[0]
    rows = round_up(used, 16)
    wire = wires[0].shape[-1]
    vmem = pl.BlockSpec(memory_space=pltpu.VMEM)
    scale = 1.0 / math.sqrt(chan)
    shapes = wire_shapes(blocks, chan, wire) + [
        jax.ShapeDtypeStruct((pixels, chan, used), BF16),
        held(blocks, (2 * chan, 2 * chan), F32),
        held(blocks, (8, 2 * chan), F32),
    ]
    *out, output, g_weights, g_gain = pl.pallas_call(
        functools.partial(angular_kernel, scale, 10, len(wires)),
        out_shape=shapes,
        in_specs=[vmem] * (len(wires) + 7),
        out_specs=[vmem] * len(shapes),
        scratch_shapes=[
            pltpu.VMEM((blocks, chan, wire), F32),
            pltpu.VMEM((rows, 2 * chan), F32),
            pltpu.VMEM((chan, 1), F32),
            pltpu.VMEM((3 * chan, chan), BF16),
            pltpu.VMEM((chan, 2 * chan), BF16),
            pltpu.VMEM((chan, chan), BF16),
            pltpu.VMEM((chan, 3 * chan), BF16),
            pltpu.VMEM((blocks, chan, wire), F32),
        ]
        + [
            pltpu.VMEM((rows, lanes), F32),
            pltpu.VMEM((lanes, lanes), BF16),
            pltpu.VMEM((lanes, lanes), BF16),
            pltpu.VMEM((chan, lanes), F32),
            pltpu.VMEM((lanes, chan), BF16),
            pltpu.VMEM((chan, lanes), F32),
        ]
        * 2,
        name="angular",
        compiler_params=grant(blocks),
    )(*here(blocks, *wires, cotangent), keep[None, :], gain[None, :], w_query, w_key, w_value, w_out)
    return out, output, g_weights, g_gain


def reduce_views(own, beside):
    count = lax.axis_size("view")
    if not pairwise(count):
        return lax.psum(own, "view"), beside
    own = own.astype(BF16)
    parts = [swap(own, "view", step) for step in range(1, count)]
    parts, beside = lax.optimization_barrier((parts, beside))
    total = own.astype(F32)
    for part in parts:
        total = total + part.astype(F32)
    return total, beside


def reduce_rows(own):
    count = lax.axis_size("row")
    step = 2
    while step < count:
        own = own.astype(BF16)
        own = own.astype(F32) + swap(own, "row", step).astype(F32)
        step *= 2
    return own


def body(inputs, cotangent, keep, w_conv, gain, w_query, w_key, w_value, w_out):
    chan, view_dev, row_dev, width = inputs.shape
    blocks = lax.axis_size("view")
    breadth = width // blocks
    views = view_dev * blocks
    lanes = round_up(views, 128)
    pixels = row_dev * breadth
    odd = row_is_odd() > 0
    x = jnp.transpose(inputs, (2, 3, 0, 1))
    first, last = x[0], x[row_dev - 1]
    near, far = halo_swap(jnp.where(odd, first, last), jnp.where(odd, last, first))
    w_conv = jnp.transpose(w_conv, (2, 3, 0, 1))
    wires, frame = convolve(x, near, far, w_conv, blocks)
    wires = exchange(wires)
    cot = jnp.transpose(cotangent, (2, 3, 0, 1)).reshape(pixels, chan, views)
    cot = jnp.pad(cot, ((0, 0), (0, 0), (0, lanes - views)))
    wires, output, g_weights, g_gain = angular(
        wires, cot, keep, gain, w_query, w_key, w_value, w_out, blocks
    )
    output = jnp.transpose(output.reshape(row_dev, breadth, chan, views), (2, 3, 0, 1))
    wires, output = lax.optimization_barrier((exchange(wires), output))
    near, far, own, kept, sent = weight_grads(wires, frame, g_weights, g_gain, view_dev, blocks)
    other = swap(sent, "row", 1)
    other, near, far = lax.optimization_barrier((other, near, far))
    part = reduce_rows(kept + other)
    near, far = halo_swap(near, far)
    d_input = input_grad(own, near, far, w_conv, view_dev, blocks)
    part, d_input = reduce_views(part, d_input)
    other = swap(part, "row", 1)
    g_conv, g_query, g_key, g_value, g_out, g_gain = unpack(part, other, chan, blocks)
    d_input = jnp.transpose(d_input, (0, 3, 1, 2))
    g_conv = jnp.transpose(g_conv, (2, 3, 0, 1))
    return (output, d_input, g_conv, g_gain[0], g_query, g_key, g_value, g_out)


def solution(mesh):
    placed = (
        P(None, "view", ("groups", "row"), None),
        P(None, None, ("groups", "row"), "view"),
        P("groups"),
        P(),
        P(),
        P(),
        P(),
        P(),
        P(),
    )
    return jax.shard_map(
        body,
        mesh=mesh,
        in_specs=placed,
        out_specs=(
            P(None, None, ("groups", "row"), "view"),
            P(None, "view", ("groups", "row"), None),
            P("groups", None, None, None),
            P("groups"),
            P("groups", None),
            P("groups", None),
            P("groups", None),
            P("groups", None),
        ),
        check_vma=False,
    )
```

```python
import functools
import math

import jax
import jax.numpy as jnp
from jax import lax
from jax.experimental import pallas as pl
from jax.experimental.pallas import tpu as pltpu
from jax.sharding import PartitionSpec as P

F32 = jnp.float32
BF16 = jnp.bfloat16


def round_up(value, unit):
    return -(-value // unit) * unit


def dot(left, right, contract=(1, 0)):
    return lax.dot_general(
        left, right, (((contract[0],), (contract[1],)), ((), ())), preferred_element_type=F32
    )


def pairwise(count):
    return count <= 8 and count & (count - 1) == 0


def swap(cells, axis, step):
    count = lax.axis_size(axis)
    return lax.ppermute(cells, axis, [(i, i ^ step) for i in range(count)])


def halo_swap(near, far):
    count = lax.axis_size("row")
    pairs = []
    for i in range(1, count - 1, 2):
        pairs += [(i, i + 1), (i + 1, i)]
    got_near = lax.ppermute(near, "row", [(i, i ^ 1) for i in range(count)])
    got_far = lax.ppermute(far, "row", pairs) if pairs else jnp.zeros_like(far)
    return got_near, got_far


def row_is_odd():
    return lax.rem(lax.axis_index("row"), 2)


def give(refs, held):
    if len(refs) == 1:
        refs[0][...] = held[...].astype(refs[0].dtype)
        return
    me = lax.axis_index("view")
    for step, ref in enumerate(refs):
        ref[...] = held[me ^ step].astype(ref.dtype)


def take(refs, held):
    if len(refs) == 1:
        held[...] = refs[0][...].astype(held.dtype)
        return
    me = lax.axis_index("view")
    for step, ref in enumerate(refs):
        held[me ^ step] = ref[...].astype(held.dtype)


def here(blocks, *arrays):
    if not pairwise(blocks):
        return arrays
    return [pltpu.with_memory_space_constraint(array, pltpu.VMEM) for array in arrays]


def grant(blocks):
    return pltpu.CompilerParams(vmem_limit_bytes=(24 << 20) if pairwise(blocks) else None)


def held(blocks, shape, dtype):
    return (pltpu.VMEM if pairwise(blocks) else jax.ShapeDtypeStruct)(shape, dtype)


def wire_shapes(blocks, chan, lanes):
    if pairwise(blocks):
        return [held(blocks, (chan, lanes), BF16)] * blocks
    return [held(blocks, (blocks, chan, lanes), BF16)]


def exchange(wires):
    if len(wires) == 1:
        return [lax.all_to_all(wires[0], "view", split_axis=0, concat_axis=0, tiled=True)]
    return [wires[0]] + [swap(wires[step], "view", step) for step in range(1, len(wires))]


def taps(w_ref, rows, forward):
    chan = w_ref.shape[2]
    blank = jnp.zeros((chan, chan), F32)
    found = {}
    for i in range(3):
        for j in range(3):
            tap = w_ref[i, j].astype(F32)
            found[i, j] = tap if forward else jnp.transpose(tap)
    bands = []
    for j in range(3):
        for r in range(rows):
            row = []
            for place in range(rows + 2):
                i = place - r if forward else r + 2 - place
                row.append(found[i, j] if 0 <= i < 3 else blank)
            bands.append(jnp.concatenate(row, axis=1))
    return jnp.concatenate(bands, axis=0).astype(BF16)


def spread(frame_ref, acc_ref, weights, rows, forward):
    width, deep, lanes = frame_ref.shape
    chan = deep // (rows + 2)
    size = rows * chan
    acc_ref[...] = jnp.zeros_like(acc_ref)

    def pair(q, carry):
        two = jnp.concatenate([frame_ref[2 * q], frame_ref[2 * q + 1]], axis=1)
        part = dot(weights, two)
        for j in range(3):
            move = 1 - j if forward else j - 1
            for side in range(2):
                acc_ref[2 * q + side + move + 1] += part[
                    j * size : (j + 1) * size, side * lanes : (side + 1) * lanes
                ]
        return carry

    lax.fori_loop(0, width // 2, pair, 0, unroll=width <= 16)


def conv_kernel(blocks, x_ref, near_ref, far_ref, w_ref, *refs):
    *wires, frame_ref, acc_s, held_s = refs
    rows, width, chan, views = x_ref.shape
    own = rows * chan
    lanes = frame_ref.shape[2]
    odd = row_is_odd() > 0
    frame_ref[...] = jnp.zeros_like(frame_ref)

    def fill(w, carry):
        near, far = near_ref[w], far_ref[w]
        frame_ref[w, :chan, :views] = jnp.where(odd, near, far)
        for r in range(rows):
            frame_ref[w, (r + 1) * chan : (r + 2) * chan, :views] = x_ref[r, w]
        frame_ref[w, chan + own :, :views] = jnp.where(odd, far, near)
        return carry

    lax.fori_loop(0, width, fill, 0, unroll=width <= 16)
    weights = taps(w_ref, rows, True)
    spread(frame_ref, acc_s, weights, rows, True)
    breadth = width // blocks

    def block(b, carry):
        cells = []
        for r in range(rows):
            for k in range(breadth):
                w = b * breadth + k
                value = acc_s[w + 1, r * chan : (r + 1) * chan]
                value = value + frame_ref[w, (r + 1) * chan : (r + 2) * chan].astype(F32)
                cells.append(value[:, :views])
        cells = jnp.concatenate(cells, axis=1)
        held_s[b, :, : cells.shape[1]] = cells
        return carry

    lax.fori_loop(0, blocks, block, 0, unroll=blocks <= 4)
    give(wires, held_s)


def convolve(x, near, far, w_conv, blocks):
    rows, width, chan, views = x.shape
    own = rows * chan
    lanes = round_up(views, 128)
    wire = round_up(rows * (width // blocks) * views, 128)
    vmem = pl.BlockSpec(memory_space=pltpu.VMEM)
    shapes = wire_shapes(blocks, chan, wire)
    shapes = shapes + [held(blocks, (width, own + 2 * chan, lanes), BF16)]
    *wires, frame = pl.pallas_call(
        functools.partial(conv_kernel, blocks),
        out_shape=shapes,
        in_specs=[vmem] * 4,
        out_specs=[vmem] * len(shapes),
        scratch_shapes=[
            pltpu.VMEM((width + 2, own, lanes), F32),
            pltpu.VMEM((blocks, chan, wire), F32),
        ],
        name="conv",
        compiler_params=grant(blocks),
    )(*here(blocks, x, near, far), w_conv)
    return wires, frame


def weight_kernel(count, pieces, *refs):
    wires = refs[:pieces]
    frame_ref, g_ref, gain_ref = refs[pieces : pieces + 3]
    near_ref, far_ref, own_ref, keep_ref, send_ref, held_s, col_s, pack_s = refs[pieces + 3 :]
    width, own, lanes = own_ref.shape
    blocks, chan, wire = held_s.shape
    rows = own // chan
    breadth = width // blocks
    views = count
    odd = row_is_odd()
    take(wires, held_s)
    col_s[0] = jnp.zeros((own, lanes), BF16)
    col_s[width + 1] = jnp.zeros((own, lanes), BF16)

    def block(b, carry):
        cells = held_s[b]
        for r in range(rows):
            for k in range(breadth):
                at = (r * breadth + k) * views
                value = cells[:, at : at + views]
                if lanes > views:
                    value = jnp.concatenate(
                        [value, jnp.zeros((chan, lanes - views), F32)], axis=1
                    )
                col_s[b * breadth + k + 1, r * chan : (r + 1) * chan] = value.astype(BF16)
        return carry

    lax.fori_loop(0, blocks, block, 0, unroll=blocks <= 4)

    def copy(w, carry):
        cells = col_s[w + 1]
        own_ref[w] = cells
        first, last = cells[:chan], cells[own - chan :]
        near_ref[w] = jnp.where(odd > 0, first, last)
        far_ref[w] = jnp.where(odd > 0, last, first)
        return carry

    lax.fori_loop(0, width, copy, 0, unroll=width <= 16)

    def pair(q, total):
        left, right = [], []
        for side in range(2):
            w = 2 * q + side
            left.append(jnp.concatenate([col_s[w], col_s[w + 1], col_s[w + 2]], axis=0))
            right.append(frame_ref[w])
        return total + dot(
            jnp.concatenate(left, axis=1), jnp.concatenate(right, axis=1), (1, 1)
        )

    total = lax.fori_loop(
        0,
        width // 2,
        pair,
        jnp.zeros((3 * own, own + 2 * chan), F32),
        unroll=width <= 16,
    )
    bands = []
    for shift in range(3):
        band = 0.0
        for r in range(rows):
            top = (shift * rows + r) * chan
            band = band + total[top : top + chan, r * chan : (r + 3) * chan]
        bands.append(band)
    g_conv = jnp.concatenate(bands, axis=0)
    edge = 2 * chan
    pack_s[...] = jnp.zeros_like(pack_s)
    pack_s[: 2 * chan] = g_ref[...]
    pack_s[2 * chan : 2 * chan + 8] = gain_ref[...]
    at = 2 * chan + 8
    pack_s[at : at + 3 * chan] = g_conv[:, :edge]
    half = 3 * chan // 2
    rest = g_conv[:, edge:]
    pack_s[at + 3 * chan : at + 3 * chan + half] = jnp.concatenate(
        [rest[:half], rest[half:]], axis=1
    )
    size = keep_ref.shape[0]
    keep_ref[...] = pack_s[pl.ds(pl.multiple_of(odd * size, 8), size)]
    send_ref[...] = pack_s[pl.ds(pl.multiple_of((1 - odd) * size, 8), size)]


def weight_grads(wires, frame, g_weights, g_gain, views, blocks):
    width, deep, lanes = frame.shape
    chan, wire = wires[0].shape[-2:]
    own = deep - 2 * chan
    size = round_up(2 * chan + 8 + 9 * chan // 2, 32) // 2
    vmem = pl.BlockSpec(memory_space=pltpu.VMEM)
    return pl.pallas_call(
        functools.partial(weight_kernel, views, len(wires)),
        out_shape=(
            held(blocks, (width, chan, lanes), BF16),
            held(blocks, (width, chan, lanes), BF16),
            held(blocks, (width, own, lanes), BF16),
            held(blocks, (size, 2 * chan), F32),
            held(blocks, (size, 2 * chan), F32),
        ),
        in_specs=[vmem] * (len(wires) + 3),
        out_specs=(vmem,) * 5,
        scratch_shapes=[
            pltpu.VMEM((blocks, chan, wire), F32),
            pltpu.VMEM((width + 2, own, lanes), BF16),
            pltpu.VMEM((2 * size, 2 * chan), F32),
        ],
        name="weights",
        compiler_params=grant(blocks),
    )(*here(blocks, *wires, frame, g_weights, g_gain))


def input_kernel(own_ref, near_ref, far_ref, w_ref, out_ref, frame_s, acc_s):
    width, own, lanes = own_ref.shape
    chan = near_ref.shape[1]
    rows = own // chan
    views = out_ref.shape[3]
    odd = row_is_odd() > 0

    def fill(w, carry):
        near, far = near_ref[w], far_ref[w]
        frame_s[w, :chan] = jnp.where(odd, near, far)
        frame_s[w, chan : chan + own] = own_ref[w]
        frame_s[w, chan + own :] = jnp.where(odd, far, near)
        return carry

    lax.fori_loop(0, width, fill, 0, unroll=width <= 16)
    spread(frame_s, acc_s, taps(w_ref, rows, False), rows, False)

    def columns(q, carry):
        at = pl.multiple_of(16 * q, 16)
        cells = []
        for k in range(16):
            cells.append(acc_s[at + k + 1] + own_ref[at + k].astype(F32))
        cells = jnp.swapaxes(jnp.stack(cells), 0, 1).astype(BF16)
        for r in range(rows):
            out_ref[:, r, pl.ds(at, 16), :] = cells[r * chan : (r + 1) * chan, :, :views]
        return carry

    lax.fori_loop(0, width // 16, columns, 0)


def input_grad(own, near, far, w_conv, views, blocks):
    width, size, lanes = own.shape
    chan = near.shape[1]
    vmem = pl.BlockSpec(memory_space=pltpu.VMEM)
    return pl.pallas_call(
        input_kernel,
        out_shape=jax.ShapeDtypeStruct((chan, size // chan, width, views), BF16),
        in_specs=[vmem] * 4,
        out_specs=vmem,
        scratch_shapes=[
            pltpu.VMEM((width, size + 2 * chan, lanes), BF16),
            pltpu.VMEM((width + 2, size, lanes), F32),
        ],
        name="input",
        compiler_params=grant(blocks),
    )(*here(blocks, own, near, far), w_conv)


def unpack_kernel(mine_ref, other_ref, conv_ref, q_ref, k_ref, v_ref, o_ref, gain_ref, pack_s):
    size = mine_ref.shape[0]
    chan = q_ref.shape[0]
    odd = row_is_odd()
    pack_s[pl.ds(pl.multiple_of(odd * size, 8), size)] = mine_ref[...]
    pack_s[pl.ds(pl.multiple_of((1 - odd) * size, 8), size)] = other_ref[...]
    k_ref[...] = pack_s[:chan, :chan]
    v_ref[...] = pack_s[:chan, chan:]
    q_ref[...] = pack_s[chan : 2 * chan, :chan]
    o_ref[...] = pack_s[chan : 2 * chan, chan:]
    gain_ref[...] = pack_s[2 * chan : 2 * chan + 1, :chan]
    at = 2 * chan + 8
    half = 3 * chan // 2
    for j in range(3):
        top = (2 - j) * chan
        for i in range(2):
            conv_ref[i, j] = pack_s[at + top : at + top + chan, i * chan : (i + 1) * chan]
        for low in range(0, chan, chan // 2):
            row = top + low
            side = row // half
            start = at + 3 * chan + row - side * half
            conv_ref[2, j, low : low + chan // 2] = pack_s[
                start : start + chan // 2, side * chan : (side + 1) * chan
            ]


def unpack(mine, other, chan, blocks):
    vmem = pl.BlockSpec(memory_space=pltpu.VMEM)
    square = jax.ShapeDtypeStruct((chan, chan), F32)
    return pl.pallas_call(
        unpack_kernel,
        out_shape=(
            jax.ShapeDtypeStruct((3, 3, chan, chan), F32),
            square,
            square,
            square,
            square,
            jax.ShapeDtypeStruct((1, chan), F32),
        ),
        in_specs=[vmem] * 2,
        out_specs=(vmem,) * 6,
        scratch_shapes=[pltpu.VMEM((2 * mine.shape[0], 2 * chan), F32)],
        name="unpack",
        compiler_params=grant(blocks),
    )(*here(blocks, mine, other))


def angular_kernel(
    scale,
    lag,
    pieces,
    *refs,
):
    wires_in = refs[:pieces]
    cot_ref, keep_ref, gain_row, wq_ref, wkey_ref, wv_ref, wo_ref = refs[pieces : pieces + 7]
    refs = refs[pieces + 7 :]
    wires_out = refs[:pieces]
    out_ref, g_ref, ggain_ref = refs[pieces : pieces + 3]
    refs = refs[pieces + 3 :]
    held_s, give_s, bias_ref, gain_ref, wqkv_ref, wkv_ref, wot_ref, wkv2_ref, gain_s = refs[:9]
    scratch = refs[9:]
    blocks = held_s.shape[0]
    pixels, chan, lanes = cot_ref.shape
    used = keep_ref.shape[1]
    each = used // blocks
    rows = bias_ref.shape[0]
    per = 7
    slots = len(scratch) // per
    inv_chan = 1.0 / chan
    take(wires_in, held_s)
    live = jnp.where(keep_ref[...] > 0, 0.0, -1e30).astype(F32)
    live = jnp.concatenate([live, jnp.full((1, lanes - used), -1e30, F32)], axis=1)
    live = jnp.transpose(jnp.broadcast_to(live, (128, lanes)))[:rows]
    lane = lax.broadcasted_iota(jnp.int32, (rows, 128), 1)
    bias_ref[...] = jnp.where(lane == chan, live, 0.0)[:, : 2 * chan]
    eye = lax.broadcasted_iota(jnp.int32, (chan, chan), 0) == lax.broadcasted_iota(
        jnp.int32, (chan, chan), 1
    )
    gain_ref[...] = jnp.sum(jnp.where(eye, gain_row[...], 0.0), axis=1, keepdims=True)
    w_q, w_k, w_v = (ref[...].astype(F32) for ref in (wq_ref, wkey_ref, wv_ref))
    wqkv_ref[...] = jnp.concatenate(
        [jnp.transpose(w_q), jnp.transpose(w_k), jnp.transpose(w_v)], axis=0
    ).astype(BF16)
    blank = jnp.zeros((chan, chan), F32)
    wkv_ref[...] = jnp.concatenate([w_k, blank, w_v, blank], axis=1).astype(BF16)
    wkv2_ref[...] = jnp.concatenate([w_k, w_v], axis=1).astype(BF16)
    wot_ref[...] = jnp.transpose(wo_ref[...].astype(F32)).astype(BF16)
    g_ref[...] = jnp.zeros_like(g_ref)
    gain_s[...] = jnp.zeros_like(gain_s)
    for slot in range(slots):
        d_s = scratch[per * slot + 5]
        d_s[rows:] = jnp.zeros((lanes - rows, 2 * chan), BF16)
    chunks = []
    at = 0
    while at < rows:
        size = min(80, rows - at)
        chunks.append((at, size))
        at += size
    half_lane = lax.broadcasted_iota(jnp.int32, (chan, 2 * chan), 1) < chan

    def pixel(p):
        start = per * (p % slots)
        s_s, e_s, n_s, x_s, kv_s, d_s, nb_s = scratch[start : start + per]
        cells = [held_s[b, :, p * each : (p + 1) * each] for b in range(blocks)]
        if lanes > used:
            cells.append(jnp.zeros((chan, lanes - used), held_s.dtype))
        s = jnp.concatenate(cells, axis=1).astype(F32)
        x_s[...] = s
        cen = s - jnp.sum(s, axis=0, keepdims=True) * inv_chan
        rstd = lax.rsqrt(jnp.sum(cen * cen, axis=0, keepdims=True) * inv_chan + 1e-05)
        normed = cen * rstd
        n_s[...] = normed
        nin32 = normed * gain_ref[...]
        nin = nin32.astype(BF16)
        nb_s[...] = nin
        nin_t = jnp.transpose(nin32)[:rows].astype(BF16)
        yield
        kv = dot(nin_t, wkv_ref[...])
        kv_s[:, : 2 * chan] = (kv[:, : 2 * chan] + bias_ref[...]).astype(BF16)
        kv_s[:, 2 * chan :] = kv[:, 2 * chan :].astype(BF16)
        yield
        qkv = dot(wqkv_ref[...], nin)
        q = (qkv[:chan].astype(BF16).astype(F32) * scale).astype(BF16)
        k = qkv[chan : 2 * chan, :rows].astype(BF16)
        v = qkv[2 * chan :, :rows].astype(BF16)
        zero = jnp.zeros((chan, lanes), BF16)
        q_aug = jnp.concatenate([q, jnp.ones((16, lanes), BF16), zero[16:]], axis=0)
        yield
        s_s[...] = dot(kv_s[:, : 2 * chan], q_aug)
        yield
        high = None
        for at, size in chunks:
            top = jnp.max(s_s[at : at + size].reshape(size // 8, 8, lanes), axis=0)
            high = top if high is None else jnp.maximum(high, top)
        high = jnp.max(high, axis=0, keepdims=True)
        yield
        for at, size in chunks:
            e_s[at : at + size, :lanes] = jnp.exp(s_s[at : at + size] - high).astype(BF16)
            yield
        v_aug = jnp.concatenate([v, jnp.ones((16, rows), BF16)], axis=0)
        att_aug = dot(v_aug, e_s[:, :lanes])
        yield
        cot = cot_ref[p]
        d_att32 = dot(wo_ref[...], cot).astype(BF16).astype(F32)
        inv = 1.0 / att_aug[chan : chan + 1]
        att = att_aug[:chan] * inv
        att_b = att.astype(BF16)
        d_att = (d_att32 * inv).astype(BF16)
        inner = jnp.sum(att * d_att.astype(F32), axis=0, keepdims=True)
        yield
        d_aug = jnp.concatenate([d_att, zero], axis=0)
        s_s[...] = dot(kv_s[:, 2 * chan :], d_aug)
        yield
        for at, size in chunks:
            e_s[at : at + size, lanes:] = e_s[at : at + size, :lanes] * (s_s[at : at + size] - inner).astype(BF16)
            yield
        low = jnp.concatenate(
            [jnp.concatenate([zero, d_att], axis=0), jnp.concatenate([q, zero], axis=0)], axis=1
        )
        d_s[:rows] = dot(e_s[...], low, (1, 1)).astype(BF16)
        yield
        d_q = (dot(k, e_s[:, lanes:]) * scale).astype(BF16)
        yield
        out_ref[p] = (x_s[...] + dot(wot_ref[...], att_b)).astype(BF16)[:, :used]
        yield
        dn = dot(wq_ref[...], d_q) + dot(wkv2_ref[...], d_s[...], (1, 1))
        nin = nb_s[...]
        g_ref[:chan] += dot(nin, d_s[...])
        both = dot(
            jnp.concatenate([nin, att_b], axis=0), jnp.concatenate([d_q, cot], axis=0), (1, 1)
        )
        g_ref[chan:] += jnp.where(half_lane, both[:chan], both[chan:])
        yield
        normed = n_s[...]
        dnn = dn * normed
        gain_s[...] += dnn
        scaled = dn * gain_ref[...]
        back = (
            scaled
            - jnp.sum(scaled, axis=0, keepdims=True) * inv_chan
            - normed * (jnp.sum(dnn * gain_ref[...], axis=0, keepdims=True) * inv_chan)
        )
        done = (cot.astype(F32) + back * rstd).astype(give_s.dtype)
        for b in range(blocks):
            give_s[b, :, p * each : (p + 1) * each] = done[:, b * each : (b + 1) * each]
        yield

    waiting = [pixel(p) for p in range(pixels)]
    active = []
    step = 0
    while waiting or active:
        if waiting and step % lag == 0:
            active += waiting[:2]
            waiting = waiting[2:]
        for run in list(active):
            try:
                next(run)
            except StopIteration:
                active.remove(run)
        step += 1
    g_gain = jnp.sum(gain_s[...], axis=1, keepdims=True)
    g_gain = jnp.sum(jnp.where(eye, g_gain, 0.0), axis=0, keepdims=True)
    g_gain = jnp.concatenate([g_gain, jnp.zeros((1, chan), F32)], axis=1)
    ggain_ref[...] = jnp.broadcast_to(g_gain, ggain_ref.shape)
    give(wires_out, give_s)


def angular(wires, cotangent, keep, gain, w_query, w_key, w_value, w_out, blocks):
    pixels, chan, lanes = cotangent.shape
    used = keep.shape[0]
    rows = round_up(used, 16)
    wire = wires[0].shape[-1]
    vmem = pl.BlockSpec(memory_space=pltpu.VMEM)
    scale = 1.0 / math.sqrt(chan)
    shapes = wire_shapes(blocks, chan, wire) + [
        jax.ShapeDtypeStruct((pixels, chan, used), BF16),
        held(blocks, (2 * chan, 2 * chan), F32),
        held(blocks, (8, 2 * chan), F32),
    ]
    *out, output, g_weights, g_gain = pl.pallas_call(
        functools.partial(angular_kernel, scale, 8, len(wires)),
        out_shape=shapes,
        in_specs=[vmem] * (len(wires) + 7),
        out_specs=[vmem] * len(shapes),
        scratch_shapes=[
            pltpu.VMEM((blocks, chan, wire), BF16),
            pltpu.VMEM((blocks, chan, wire), BF16),
            pltpu.VMEM((rows, 2 * chan), F32),
            pltpu.VMEM((chan, 1), F32),
            pltpu.VMEM((3 * chan, chan), BF16),
            pltpu.VMEM((chan, 4 * chan), BF16),
            pltpu.VMEM((chan, chan), BF16),
            pltpu.VMEM((chan, 2 * chan), BF16),
            pltpu.VMEM((chan, lanes), F32),
        ]
        + [
            pltpu.VMEM((rows, lanes), F32),
            pltpu.VMEM((rows, 2 * lanes), BF16),
            pltpu.VMEM((chan, lanes), F32),
            pltpu.VMEM((chan, lanes), F32),
            pltpu.VMEM((rows, 4 * chan), BF16),
            pltpu.VMEM((lanes, 2 * chan), BF16),
            pltpu.VMEM((chan, lanes), BF16),
        ]
        * 6,
        name="angular",
        compiler_params=grant(blocks),
    )(*here(blocks, *wires, cotangent), keep[None, :], gain[None, :], w_query, w_key, w_value, w_out)
    return out, output, g_weights, g_gain


def reduce_views(own, beside):
    count = lax.axis_size("view")
    if not pairwise(count):
        return lax.psum(own, "view"), beside
    own = own.astype(BF16)
    parts = [swap(own, "view", step) for step in range(1, count)]
    parts, beside = lax.optimization_barrier((parts, beside))
    total = own.astype(F32)
    for part in parts:
        total = total + part.astype(F32)
    return total, beside


def reduce_rows(own):
    count = lax.axis_size("row")
    step = 2
    while step < count:
        own = own.astype(BF16)
        own = own.astype(F32) + swap(own, "row", step).astype(F32)
        step *= 2
    return own


def body(inputs, cotangent, keep, w_conv, gain, w_query, w_key, w_value, w_out):
    chan, view_dev, row_dev, width = inputs.shape
    blocks = lax.axis_size("view")
    breadth = width // blocks
    views = view_dev * blocks
    lanes = round_up(views, 128)
    pixels = row_dev * breadth
    odd = row_is_odd() > 0
    x = jnp.transpose(inputs, (2, 3, 0, 1))
    first, last = x[0], x[row_dev - 1]
    near, far = halo_swap(jnp.where(odd, first, last), jnp.where(odd, last, first))
    w_conv = jnp.transpose(w_conv, (2, 3, 0, 1))
    wires, frame = convolve(x, near, far, w_conv, blocks)
    wires = exchange(wires)
    cot = jnp.transpose(cotangent, (2, 3, 0, 1)).reshape(pixels, chan, views)
    cot = jnp.pad(cot, ((0, 0), (0, 0), (0, lanes - views)))
    wires, output, g_weights, g_gain = angular(
        wires, cot, keep, gain, w_query, w_key, w_value, w_out, blocks
    )
    output = jnp.transpose(output.reshape(row_dev, breadth, chan, views), (2, 3, 0, 1))
    wires, output = lax.optimization_barrier((exchange(wires), output))
    near, far, own, kept, sent = weight_grads(wires, frame, g_weights, g_gain, view_dev, blocks)
    other = swap(sent, "row", 1)
    other, near, far = lax.optimization_barrier((other, near, far))
    part = reduce_rows(kept + other)
    near, far = halo_swap(near, far)
    d_input = input_grad(own, near, far, w_conv, view_dev, blocks)
    part, d_input = reduce_views(part, d_input)
    other = swap(part, "row", 1)
    g_conv, g_query, g_key, g_value, g_out, g_gain = unpack(part, other, chan, blocks)
    d_input = jnp.transpose(d_input, (0, 3, 1, 2))
    g_conv = jnp.transpose(g_conv, (2, 3, 0, 1))
    return (output, d_input, g_conv, g_gain[0], g_query, g_key, g_value, g_out)


def solution(mesh):
    placed = (
        P(None, "view", ("groups", "row"), None),
        P(None, None, ("groups", "row"), "view"),
        P("groups"),
        P(),
        P(),
        P(),
        P(),
        P(),
        P(),
    )
    return jax.shard_map(
        body,
        mesh=mesh,
        in_specs=placed,
        out_specs=(
            P(None, None, ("groups", "row"), "view"),
            P(None, "view", ("groups", "row"), None),
            P("groups", None, None, None),
            P("groups"),
            P("groups", None),
            P("groups", None),
            P("groups", None),
            P("groups", None),
        ),
        check_vma=False,
    )
```

```python
import functools
import math

import jax
import jax.numpy as jnp
from jax import lax
from jax.experimental import pallas as pl
from jax.experimental.pallas import tpu as pltpu
from jax.sharding import PartitionSpec as P

F32 = jnp.float32
BF16 = jnp.bfloat16


def round_up(value, unit):
    return -(-value // unit) * unit


def dot(left, right, contract=(1, 0)):
    return lax.dot_general(
        left, right, (((contract[0],), (contract[1],)), ((), ())), preferred_element_type=F32
    )


def pairwise(count):
    return count <= 8 and count & (count - 1) == 0


def swap(cells, axis, step):
    count = lax.axis_size(axis)
    return lax.ppermute(cells, axis, [(i, i ^ step) for i in range(count)])


def halo_swap(near, far):
    count = lax.axis_size("row")
    pairs = []
    for i in range(1, count - 1, 2):
        pairs += [(i, i + 1), (i + 1, i)]
    got_near = lax.ppermute(near, "row", [(i, i ^ 1) for i in range(count)])
    got_far = lax.ppermute(far, "row", pairs) if pairs else jnp.zeros_like(far)
    return got_near, got_far


def row_is_odd():
    return lax.rem(lax.axis_index("row"), 2)


def plan(pixels, views, blocks):
    tiles = round_up(pixels * views, 128) // 128
    early = (tiles + 1) // 2
    count = min(early * 128 // views, pixels)
    late = pixels - count
    if not pairwise(blocks) or late == 0 or late * views > (tiles - early) * 128:
        return [(0, pixels, 0, 128 * tiles)]
    return [(0, count, 0, 128 * early), (count, late, 128 * early, 128 * (tiles - early))]


def give(refs, held, start=0):
    lanes = refs[0].shape[-1]
    if len(refs) == 1:
        refs[0][...] = held[:, :, start : start + lanes].astype(refs[0].dtype)
        return
    me = lax.axis_index("view")
    for step, ref in enumerate(refs):
        ref[...] = held[me ^ step, :, start : start + lanes].astype(ref.dtype)


def take(refs, held, start=0):
    lanes = refs[0].shape[-1]
    if len(refs) == 1:
        held[:, :, start : start + lanes] = refs[0][...].astype(held.dtype)
        return
    me = lax.axis_index("view")
    for step, ref in enumerate(refs):
        held[me ^ step, :, start : start + lanes] = ref[...].astype(held.dtype)


def here(blocks, *arrays):
    if not pairwise(blocks):
        return arrays
    return [pltpu.with_memory_space_constraint(array, pltpu.VMEM) for array in arrays]


def grant(blocks):
    return pltpu.CompilerParams(vmem_limit_bytes=(24 << 20) if pairwise(blocks) else None)


def held(blocks, shape, dtype):
    return (pltpu.VMEM if pairwise(blocks) else jax.ShapeDtypeStruct)(shape, dtype)


def wire_shapes(blocks, chan, lanes):
    if pairwise(blocks):
        return [held(blocks, (chan, lanes), BF16)] * blocks
    return [held(blocks, (blocks, chan, lanes), BF16)]


def exchange(wires):
    if len(wires) == 1:
        return [lax.all_to_all(wires[0], "view", split_axis=0, concat_axis=0, tiled=True)]
    return [wires[0]] + [swap(wires[step], "view", step) for step in range(1, len(wires))]


def taps(w_ref, rows, forward):
    chan = w_ref.shape[2]
    blank = jnp.zeros((chan, chan), F32)
    found = {}
    for i in range(3):
        for j in range(3):
            tap = w_ref[i, j].astype(F32)
            found[i, j] = tap if forward else jnp.transpose(tap)
    bands = []
    for j in range(3):
        for r in range(rows):
            row = []
            for place in range(rows + 2):
                i = place - r if forward else r + 2 - place
                row.append(found[i, j] if 0 <= i < 3 else blank)
            bands.append(jnp.concatenate(row, axis=1))
    return jnp.concatenate(bands, axis=0).astype(BF16)


def spread(frame_ref, acc_ref, weights, rows, forward):
    width, deep, lanes = frame_ref.shape
    chan = deep // (rows + 2)
    size = rows * chan
    acc_ref[...] = jnp.zeros_like(acc_ref)

    def pair(q, carry):
        two = jnp.concatenate([frame_ref[2 * q], frame_ref[2 * q + 1]], axis=1)
        part = dot(weights, two)
        for j in range(3):
            move = 1 - j if forward else j - 1
            for side in range(2):
                acc_ref[2 * q + side + move + 1] += part[
                    j * size : (j + 1) * size, side * lanes : (side + 1) * lanes
                ]
        return carry

    lax.fori_loop(0, width // 2, pair, 0, unroll=width <= 16)


def conv_kernel(blocks, x_ref, near_ref, far_ref, w_ref, *refs):
    *wires, frame_ref, acc_s, held_s = refs
    rows, width, chan, views = x_ref.shape
    own = rows * chan
    lanes = frame_ref.shape[2]
    odd = row_is_odd() > 0
    frame_ref[...] = jnp.zeros_like(frame_ref)

    def fill(w, carry):
        near, far = near_ref[w], far_ref[w]
        frame_ref[w, :chan, :views] = jnp.where(odd, near, far)
        for r in range(rows):
            frame_ref[w, (r + 1) * chan : (r + 2) * chan, :views] = x_ref[r, w]
        frame_ref[w, chan + own :, :views] = jnp.where(odd, far, near)
        return carry

    lax.fori_loop(0, width, fill, 0, unroll=width <= 16)
    weights = taps(w_ref, rows, True)
    spread(frame_ref, acc_s, weights, rows, True)
    breadth = width // blocks
    chunks = plan(rows * breadth, views, blocks)

    def block(b, carry):
        cells = []
        for r in range(rows):
            for k in range(breadth):
                w = b * breadth + k
                value = acc_s[w + 1, r * chan : (r + 1) * chan]
                value = value + frame_ref[w, (r + 1) * chan : (r + 2) * chan].astype(F32)
                cells.append(value[:, :views])
        for first, count, at, _ in chunks:
            some = jnp.concatenate(cells[first : first + count], axis=1)
            held_s[b, :, at : at + count * views] = some
        return carry

    lax.fori_loop(0, blocks, block, 0, unroll=blocks <= 4)
    pieces = len(wires) // len(chunks)
    for c, (_, _, at, _) in enumerate(chunks):
        give(wires[c * pieces : (c + 1) * pieces], held_s, at)


def convolve(x, near, far, w_conv, blocks):
    rows, width, chan, views = x.shape
    own = rows * chan
    lanes = round_up(views, 128)
    wire = round_up(rows * (width // blocks) * views, 128)
    vmem = pl.BlockSpec(memory_space=pltpu.VMEM)
    shapes = []
    for _, _, _, size in plan(rows * (width // blocks), views, blocks):
        shapes += wire_shapes(blocks, chan, size)
    shapes = shapes + [held(blocks, (width, own + 2 * chan, lanes), BF16)]
    *wires, frame = pl.pallas_call(
        functools.partial(conv_kernel, blocks),
        out_shape=shapes,
        in_specs=[vmem] * 4,
        out_specs=[vmem] * len(shapes),
        scratch_shapes=[
            pltpu.VMEM((width + 2, own, lanes), F32),
            pltpu.VMEM((blocks, chan, wire), F32),
        ],
        name="conv",
        compiler_params=grant(blocks),
    )(*here(blocks, x, near, far), w_conv)
    return wires, frame


def weight_kernel(count, pieces, parts, *refs):
    wires = refs[:pieces]
    frame_ref = refs[pieces]
    g_refs = refs[pieces + 1 : pieces + 1 + parts]
    gain_refs = refs[pieces + 1 + parts : pieces + 1 + 2 * parts]
    near_ref, far_ref, own_ref, keep_ref, send_ref, held_s, col_s, pack_s = refs[
        pieces + 1 + 2 * parts :
    ]
    width, own, lanes = own_ref.shape
    blocks, chan, wire = held_s.shape
    rows = own // chan
    breadth = width // blocks
    views = count
    odd = row_is_odd()
    chunks = plan(rows * breadth, views, blocks)
    each = pieces // len(chunks)
    places = {}
    for c, (first, pixels, start, _) in enumerate(chunks):
        take(wires[c * each : (c + 1) * each], held_s, start)
        for p in range(pixels):
            places[first + p] = start + p * views
    col_s[0] = jnp.zeros((own, lanes), BF16)
    col_s[width + 1] = jnp.zeros((own, lanes), BF16)

    def block(b, carry):
        cells = held_s[b]
        for r in range(rows):
            for k in range(breadth):
                at = places[r * breadth + k]
                value = cells[:, at : at + views]
                if lanes > views:
                    value = jnp.concatenate(
                        [value, jnp.zeros((chan, lanes - views), F32)], axis=1
                    )
                col_s[b * breadth + k + 1, r * chan : (r + 1) * chan] = value.astype(BF16)
        return carry

    lax.fori_loop(0, blocks, block, 0, unroll=blocks <= 4)

    def copy(w, carry):
        cells = col_s[w + 1]
        own_ref[w] = cells
        first, last = cells[:chan], cells[own - chan :]
        near_ref[w] = jnp.where(odd > 0, first, last)
        far_ref[w] = jnp.where(odd > 0, last, first)
        return carry

    lax.fori_loop(0, width, copy, 0, unroll=width <= 16)

    def pair(q, total):
        left, right = [], []
        for side in range(2):
            w = 2 * q + side
            left.append(jnp.concatenate([col_s[w], col_s[w + 1], col_s[w + 2]], axis=0))
            right.append(frame_ref[w])
        return total + dot(
            jnp.concatenate(left, axis=1), jnp.concatenate(right, axis=1), (1, 1)
        )

    total = lax.fori_loop(
        0,
        width // 2,
        pair,
        jnp.zeros((3 * own, own + 2 * chan), F32),
        unroll=width <= 16,
    )
    bands = []
    for shift in range(3):
        band = 0.0
        for r in range(rows):
            top = (shift * rows + r) * chan
            band = band + total[top : top + chan, r * chan : (r + 3) * chan]
        bands.append(band)
    g_conv = jnp.concatenate(bands, axis=0)
    edge = 2 * chan
    pack_s[...] = jnp.zeros_like(pack_s)
    pack_s[: 2 * chan] = sum(ref[...] for ref in g_refs)
    pack_s[2 * chan : 2 * chan + 8] = sum(ref[...] for ref in gain_refs)
    at = 2 * chan + 8
    pack_s[at : at + 3 * chan] = g_conv[:, :edge]
    half = 3 * chan // 2
    rest = g_conv[:, edge:]
    pack_s[at + 3 * chan : at + 3 * chan + half] = jnp.concatenate(
        [rest[:half], rest[half:]], axis=1
    )
    size = keep_ref.shape[0]
    keep_ref[...] = pack_s[pl.ds(pl.multiple_of(odd * size, 8), size)]
    send_ref[...] = pack_s[pl.ds(pl.multiple_of((1 - odd) * size, 8), size)]


def weight_grads(wires, frame, g_weights, g_gain, views, blocks):
    width, deep, lanes = frame.shape
    chan = wires[0].shape[-2]
    own = deep - 2 * chan
    wire = round_up(own // chan * (width // blocks) * views, 128)
    parts = len(g_weights)
    size = round_up(2 * chan + 8 + 9 * chan // 2, 32) // 2
    vmem = pl.BlockSpec(memory_space=pltpu.VMEM)
    return pl.pallas_call(
        functools.partial(weight_kernel, views, len(wires), parts),
        out_shape=(
            held(blocks, (width, chan, lanes), BF16),
            held(blocks, (width, chan, lanes), BF16),
            held(blocks, (width, own, lanes), BF16),
            held(blocks, (size, 2 * chan), F32),
            held(blocks, (size, 2 * chan), F32),
        ),
        in_specs=[vmem] * (len(wires) + 1 + 2 * parts),
        out_specs=(vmem,) * 5,
        scratch_shapes=[
            pltpu.VMEM((blocks, chan, wire), F32),
            pltpu.VMEM((width + 2, own, lanes), BF16),
            pltpu.VMEM((2 * size, 2 * chan), F32),
        ],
        name="weights",
        compiler_params=grant(blocks),
    )(*here(blocks, *wires, frame, *g_weights, *g_gain))


def input_kernel(own_ref, near_ref, far_ref, w_ref, out_ref, frame_s, acc_s):
    width, own, lanes = own_ref.shape
    chan = near_ref.shape[1]
    rows = own // chan
    views = out_ref.shape[3]
    odd = row_is_odd() > 0

    def fill(w, carry):
        near, far = near_ref[w], far_ref[w]
        frame_s[w, :chan] = jnp.where(odd, near, far)
        frame_s[w, chan : chan + own] = own_ref[w]
        frame_s[w, chan + own :] = jnp.where(odd, far, near)
        return carry

    lax.fori_loop(0, width, fill, 0, unroll=width <= 16)
    spread(frame_s, acc_s, taps(w_ref, rows, False), rows, False)

    def columns(q, carry):
        at = pl.multiple_of(16 * q, 16)
        cells = []
        for k in range(16):
            cells.append(acc_s[at + k + 1] + own_ref[at + k].astype(F32))
        cells = jnp.swapaxes(jnp.stack(cells), 0, 1).astype(BF16)
        for r in range(rows):
            out_ref[:, r, pl.ds(at, 16), :] = cells[r * chan : (r + 1) * chan, :, :views]
        return carry

    lax.fori_loop(0, width // 16, columns, 0)


def input_grad(own, near, far, w_conv, views, blocks):
    width, size, lanes = own.shape
    chan = near.shape[1]
    vmem = pl.BlockSpec(memory_space=pltpu.VMEM)
    return pl.pallas_call(
        input_kernel,
        out_shape=jax.ShapeDtypeStruct((chan, size // chan, width, views), BF16),
        in_specs=[vmem] * 4,
        out_specs=vmem,
        scratch_shapes=[
            pltpu.VMEM((width, size + 2 * chan, lanes), BF16),
            pltpu.VMEM((width + 2, size, lanes), F32),
        ],
        name="input",
        compiler_params=grant(blocks),
    )(*here(blocks, own, near, far), w_conv)


def unpack_kernel(mine_ref, other_ref, conv_ref, q_ref, k_ref, v_ref, o_ref, gain_ref, pack_s):
    size = mine_ref.shape[0]
    chan = q_ref.shape[0]
    odd = row_is_odd()
    pack_s[pl.ds(pl.multiple_of(odd * size, 8), size)] = mine_ref[...]
    pack_s[pl.ds(pl.multiple_of((1 - odd) * size, 8), size)] = other_ref[...]
    k_ref[...] = pack_s[:chan, :chan]
    v_ref[...] = pack_s[:chan, chan:]
    q_ref[...] = pack_s[chan : 2 * chan, :chan]
    o_ref[...] = pack_s[chan : 2 * chan, chan:]
    gain_ref[...] = pack_s[2 * chan : 2 * chan + 1, :chan]
    at = 2 * chan + 8
    half = 3 * chan // 2
    for j in range(3):
        top = (2 - j) * chan
        for i in range(2):
            conv_ref[i, j] = pack_s[at + top : at + top + chan, i * chan : (i + 1) * chan]
        for low in range(0, chan, chan // 2):
            row = top + low
            side = row // half
            start = at + 3 * chan + row - side * half
            conv_ref[2, j, low : low + chan // 2] = pack_s[
                start : start + chan // 2, side * chan : (side + 1) * chan
            ]


def unpack(mine, other, chan, blocks):
    vmem = pl.BlockSpec(memory_space=pltpu.VMEM)
    square = jax.ShapeDtypeStruct((chan, chan), F32)
    return pl.pallas_call(
        unpack_kernel,
        out_shape=(
            jax.ShapeDtypeStruct((3, 3, chan, chan), F32),
            square,
            square,
            square,
            square,
            jax.ShapeDtypeStruct((1, chan), F32),
        ),
        in_specs=[vmem] * 2,
        out_specs=(vmem,) * 6,
        scratch_shapes=[pltpu.VMEM((2 * mine.shape[0], 2 * chan), F32)],
        name="unpack",
        compiler_params=grant(blocks),
    )(*here(blocks, mine, other))


def angular_kernel(
    scale,
    lag,
    first,
    pieces,
    *refs,
):
    wires_in = refs[:pieces]
    cot_ref, keep_ref, gain_row, wq_ref, wkey_ref, wv_ref, wo_ref = refs[pieces : pieces + 7]
    refs = refs[pieces + 7 :]
    wires_out = refs[:pieces]
    out_ref, g_ref, ggain_ref = refs[pieces : pieces + 3]
    refs = refs[pieces + 3 :]
    held_s, give_s, bias_ref, gain_ref, wqkv_ref, wkv_ref, wot_ref, wkv2_ref, gain_s = refs[:9]
    scratch = refs[9:]
    blocks = held_s.shape[0]
    _, chan, lanes = cot_ref.shape
    pixels = out_ref.shape[0]
    used = keep_ref.shape[1]
    each = used // blocks
    rows = bias_ref.shape[0]
    per = 7
    slots = len(scratch) // per
    inv_chan = 1.0 / chan
    take(wires_in, held_s)
    live = jnp.where(keep_ref[...] > 0, 0.0, -1e30).astype(F32)
    live = jnp.concatenate([live, jnp.full((1, lanes - used), -1e30, F32)], axis=1)
    live = jnp.transpose(jnp.broadcast_to(live, (128, lanes)))[:rows]
    lane = lax.broadcasted_iota(jnp.int32, (rows, 128), 1)
    bias_ref[...] = jnp.where(lane == chan, live, 0.0)[:, : 2 * chan]
    eye = lax.broadcasted_iota(jnp.int32, (chan, chan), 0) == lax.broadcasted_iota(
        jnp.int32, (chan, chan), 1
    )
    gain_ref[...] = jnp.sum(jnp.where(eye, gain_row[...], 0.0), axis=1, keepdims=True)
    w_q, w_k, w_v = (ref[...].astype(F32) for ref in (wq_ref, wkey_ref, wv_ref))
    wqkv_ref[...] = jnp.concatenate(
        [jnp.transpose(w_q), jnp.transpose(w_k), jnp.transpose(w_v)], axis=0
    ).astype(BF16)
    blank = jnp.zeros((chan, chan), F32)
    wkv_ref[...] = jnp.concatenate([w_k, blank, w_v, blank], axis=1).astype(BF16)
    wkv2_ref[...] = jnp.concatenate([w_k, w_v], axis=1).astype(BF16)
    wot_ref[...] = jnp.transpose(wo_ref[...].astype(F32)).astype(BF16)
    g_ref[...] = jnp.zeros_like(g_ref)
    gain_s[...] = jnp.zeros_like(gain_s)
    for slot in range(slots):
        d_s = scratch[per * slot + 5]
        d_s[rows:] = jnp.zeros((lanes - rows, 2 * chan), BF16)
    chunks = []
    at = 0
    while at < rows:
        size = min(80, rows - at)
        chunks.append((at, size))
        at += size
    half_lane = lax.broadcasted_iota(jnp.int32, (chan, 2 * chan), 1) < chan

    def pixel(p):
        start = per * (p % slots)
        s_s, e_s, n_s, x_s, kv_s, d_s, nb_s = scratch[start : start + per]
        cells = [held_s[b, :, p * each : (p + 1) * each] for b in range(blocks)]
        if lanes > used:
            cells.append(jnp.zeros((chan, lanes - used), held_s.dtype))
        s = jnp.concatenate(cells, axis=1).astype(F32)
        x_s[...] = s
        cen = s - jnp.sum(s, axis=0, keepdims=True) * inv_chan
        rstd = lax.rsqrt(jnp.sum(cen * cen, axis=0, keepdims=True) * inv_chan + 1e-05)
        normed = cen * rstd
        n_s[...] = normed
        nin32 = normed * gain_ref[...]
        nin = nin32.astype(BF16)
        nb_s[...] = nin
        nin_t = jnp.transpose(nin32)[:rows].astype(BF16)
        yield
        kv = dot(nin_t, wkv_ref[...])
        kv_s[:, : 2 * chan] = (kv[:, : 2 * chan] + bias_ref[...]).astype(BF16)
        kv_s[:, 2 * chan :] = kv[:, 2 * chan :].astype(BF16)
        yield
        qkv = dot(wqkv_ref[...], nin)
        q = (qkv[:chan].astype(BF16).astype(F32) * scale).astype(BF16)
        k = qkv[chan : 2 * chan, :rows].astype(BF16)
        v = qkv[2 * chan :, :rows].astype(BF16)
        zero = jnp.zeros((chan, lanes), BF16)
        q_aug = jnp.concatenate([q, jnp.ones((16, lanes), BF16), zero[16:]], axis=0)
        yield
        s_s[...] = dot(kv_s[:, : 2 * chan], q_aug)
        yield
        high = None
        for at, size in chunks:
            top = jnp.max(s_s[at : at + size].reshape(size // 8, 8, lanes), axis=0)
            high = top if high is None else jnp.maximum(high, top)
        high = jnp.max(high, axis=0, keepdims=True)
        yield
        for at, size in chunks:
            e_s[at : at + size, :lanes] = jnp.exp(s_s[at : at + size] - high).astype(BF16)
            yield
        v_aug = jnp.concatenate([v, jnp.ones((16, rows), BF16)], axis=0)
        att_aug = dot(v_aug, e_s[:, :lanes])
        yield
        cot = cot_ref[first + p]
        d_att32 = dot(wo_ref[...], cot).astype(BF16).astype(F32)
        inv = 1.0 / att_aug[chan : chan + 1]
        att = att_aug[:chan] * inv
        att_b = att.astype(BF16)
        d_att = (d_att32 * inv).astype(BF16)
        inner = jnp.sum(att * d_att.astype(F32), axis=0, keepdims=True)
        yield
        d_aug = jnp.concatenate([d_att, zero], axis=0)
        s_s[...] = dot(kv_s[:, 2 * chan :], d_aug)
        yield
        for at, size in chunks:
            e_s[at : at + size, lanes:] = e_s[at : at + size, :lanes] * (s_s[at : at + size] - inner).astype(BF16)
            yield
        low = jnp.concatenate(
            [jnp.concatenate([zero, d_att], axis=0), jnp.concatenate([q, zero], axis=0)], axis=1
        )
        d_s[:rows] = dot(e_s[...], low, (1, 1)).astype(BF16)
        yield
        d_q = (dot(k, e_s[:, lanes:]) * scale).astype(BF16)
        yield
        out_ref[p] = (x_s[...] + dot(wot_ref[...], att_b)).astype(BF16)[:, :used]
        yield
        dn = dot(wq_ref[...], d_q) + dot(wkv2_ref[...], d_s[...], (1, 1))
        nin = nb_s[...]
        g_ref[:chan] += dot(nin, d_s[...])
        both = dot(
            jnp.concatenate([nin, att_b], axis=0), jnp.concatenate([d_q, cot], axis=0), (1, 1)
        )
        g_ref[chan:] += jnp.where(half_lane, both[:chan], both[chan:])
        yield
        normed = n_s[...]
        dnn = dn * normed
        gain_s[...] += dnn
        scaled = dn * gain_ref[...]
        back = (
            scaled
            - jnp.sum(scaled, axis=0, keepdims=True) * inv_chan
            - normed * (jnp.sum(dnn * gain_ref[...], axis=0, keepdims=True) * inv_chan)
        )
        done = (cot.astype(F32) + back * rstd).astype(give_s.dtype)
        for b in range(blocks):
            give_s[b, :, p * each : (p + 1) * each] = done[:, b * each : (b + 1) * each]
        yield

    waiting = [pixel(p) for p in range(pixels)]
    active = []
    step = 0
    while waiting or active:
        if waiting and step % lag == 0:
            active += waiting[:2]
            waiting = waiting[2:]
        for run in list(active):
            try:
                next(run)
            except StopIteration:
                active.remove(run)
        step += 1
    g_gain = jnp.sum(gain_s[...], axis=1, keepdims=True)
    g_gain = jnp.sum(jnp.where(eye, g_gain, 0.0), axis=0, keepdims=True)
    g_gain = jnp.concatenate([g_gain, jnp.zeros((1, chan), F32)], axis=1)
    ggain_ref[...] = jnp.broadcast_to(g_gain, ggain_ref.shape)
    give(wires_out, give_s)


def angular(
    wires, first, pixels, cotangent, keep, gain, w_query, w_key, w_value, w_out, blocks
):
    _, chan, lanes = cotangent.shape
    used = keep.shape[0]
    rows = round_up(used, 16)
    wire = wires[0].shape[-1]
    vmem = pl.BlockSpec(memory_space=pltpu.VMEM)
    scale = 1.0 / math.sqrt(chan)
    shapes = wire_shapes(blocks, chan, wire) + [
        jax.ShapeDtypeStruct((pixels, chan, used), BF16),
        held(blocks, (2 * chan, 2 * chan), F32),
        held(blocks, (8, 2 * chan), F32),
    ]
    *out, output, g_weights, g_gain = pl.pallas_call(
        functools.partial(angular_kernel, scale, 8, first, len(wires)),
        out_shape=shapes,
        in_specs=[vmem] * (len(wires) + 7),
        out_specs=[vmem] * len(shapes),
        scratch_shapes=[
            pltpu.VMEM((blocks, chan, wire), BF16),
            pltpu.VMEM((blocks, chan, wire), BF16),
            pltpu.VMEM((rows, 2 * chan), F32),
            pltpu.VMEM((chan, 1), F32),
            pltpu.VMEM((3 * chan, chan), BF16),
            pltpu.VMEM((chan, 4 * chan), BF16),
            pltpu.VMEM((chan, chan), BF16),
            pltpu.VMEM((chan, 2 * chan), BF16),
            pltpu.VMEM((chan, lanes), F32),
        ]
        + [
            pltpu.VMEM((rows, lanes), F32),
            pltpu.VMEM((rows, 2 * lanes), BF16),
            pltpu.VMEM((chan, lanes), F32),
            pltpu.VMEM((chan, lanes), F32),
            pltpu.VMEM((rows, 4 * chan), BF16),
            pltpu.VMEM((lanes, 2 * chan), BF16),
            pltpu.VMEM((chan, lanes), BF16),
        ]
        * 6,
        name="angular",
        compiler_params=grant(blocks),
    )(*here(blocks, *wires, cotangent), keep[None, :], gain[None, :], w_query, w_key, w_value, w_out)
    return out, output, g_weights, g_gain


def reduce_views(own, beside):
    count = lax.axis_size("view")
    if not pairwise(count):
        return lax.psum(own, "view"), beside
    own = own.astype(BF16)
    parts = [swap(own, "view", step) for step in range(1, count)]
    parts, beside = lax.optimization_barrier((parts, beside))
    total = own.astype(F32)
    for part in parts:
        total = total + part.astype(F32)
    return total, beside


def reduce_rows(own):
    count = lax.axis_size("row")
    step = 2
    while step < count:
        own = own.astype(BF16)
        own = own.astype(F32) + swap(own, "row", step).astype(F32)
        step *= 2
    return own


def body(inputs, cotangent, keep, w_conv, gain, w_query, w_key, w_value, w_out):
    chan, view_dev, row_dev, width = inputs.shape
    blocks = lax.axis_size("view")
    breadth = width // blocks
    views = view_dev * blocks
    lanes = round_up(views, 128)
    pixels = row_dev * breadth
    odd = row_is_odd() > 0
    x = jnp.transpose(inputs, (2, 3, 0, 1))
    first, last = x[0], x[row_dev - 1]
    near, far = halo_swap(jnp.where(odd, first, last), jnp.where(odd, last, first))
    w_conv = jnp.transpose(w_conv, (2, 3, 0, 1))
    wires, frame = convolve(x, near, far, w_conv, blocks)
    chunks = plan(pixels, view_dev, blocks)
    pieces = len(wires) // len(chunks)
    arrived = [exchange(wires[c * pieces : (c + 1) * pieces]) for c in range(len(chunks))]
    cot = jnp.transpose(cotangent, (2, 3, 0, 1)).reshape(pixels, chan, views)
    cot = jnp.pad(cot, ((0, 0), (0, 0), (0, lanes - views)))
    weights = (gain, w_query, w_key, w_value, w_out)
    wires, output, g_weights, g_gain = [], [], [], []
    for (first, count, _, _), got in zip(chunks, arrived):
        out, result, g_part, gain_part = angular(got, first, count, cot, keep, *weights, blocks)
        wires += exchange(out)
        output.append(result)
        g_weights.append(g_part)
        g_gain.append(gain_part)
    output = jnp.concatenate(output, axis=0) if len(output) > 1 else output[0]
    output = jnp.transpose(output.reshape(row_dev, breadth, chan, views), (2, 3, 0, 1))
    wires, output = lax.optimization_barrier((wires, output))
    near, far, own, kept, sent = weight_grads(wires, frame, g_weights, g_gain, view_dev, blocks)
    other = swap(sent, "row", 1)
    other, near, far = lax.optimization_barrier((other, near, far))
    part = reduce_rows(kept + other)
    near, far = halo_swap(near, far)
    d_input = input_grad(own, near, far, w_conv, view_dev, blocks)
    part, d_input = reduce_views(part, d_input)
    other = swap(part, "row", 1)
    g_conv, g_query, g_key, g_value, g_out, g_gain = unpack(part, other, chan, blocks)
    d_input = jnp.transpose(d_input, (0, 3, 1, 2))
    g_conv = jnp.transpose(g_conv, (2, 3, 0, 1))
    return (output, d_input, g_conv, g_gain[0], g_query, g_key, g_value, g_out)


def solution(mesh):
    placed = (
        P(None, "view", ("groups", "row"), None),
        P(None, None, ("groups", "row"), "view"),
        P("groups"),
        P(),
        P(),
        P(),
        P(),
        P(),
        P(),
    )
    return jax.shard_map(
        body,
        mesh=mesh,
        in_specs=placed,
        out_specs=(
            P(None, None, ("groups", "row"), "view"),
            P(None, "view", ("groups", "row"), None),
            P("groups", None, None, None),
            P("groups"),
            P("groups", None),
            P("groups", None),
            P("groups", None),
            P("groups", None),
        ),
        check_vma=False,
    )
```

```python
import functools
import math

import jax
import jax.numpy as jnp
from jax import lax
from jax.experimental import pallas as pl
from jax.experimental.pallas import tpu as pltpu
from jax.sharding import PartitionSpec as P

F32 = jnp.float32
BF16 = jnp.bfloat16


def round_up(value, unit):
    return -(-value // unit) * unit


def dot(left, right, contract=(1, 0)):
    return lax.dot_general(
        left, right, (((contract[0],), (contract[1],)), ((), ())), preferred_element_type=F32
    )


def pairwise(count):
    return count <= 8 and count & (count - 1) == 0


def swap(cells, axis, step):
    count = lax.axis_size(axis)
    return lax.ppermute(cells, axis, [(i, i ^ step) for i in range(count)])


def halo_swap(near, far):
    count = lax.axis_size("row")
    pairs = []
    for i in range(1, count - 1, 2):
        pairs += [(i, i + 1), (i + 1, i)]
    got_near = lax.ppermute(near, "row", [(i, i ^ 1) for i in range(count)])
    got_far = lax.ppermute(far, "row", pairs) if pairs else jnp.zeros_like(far)
    return got_near, got_far


def row_is_odd():
    return lax.rem(lax.axis_index("row"), 2)


def give(refs, held):
    if len(refs) == 1:
        refs[0][...] = held[...].astype(refs[0].dtype)
        return
    me = lax.axis_index("view")
    for step, ref in enumerate(refs):
        ref[...] = held[me ^ step].astype(ref.dtype)


def take(refs, held):
    if len(refs) == 1:
        held[...] = refs[0][...].astype(held.dtype)
        return
    me = lax.axis_index("view")
    for step, ref in enumerate(refs):
        held[me ^ step] = ref[...].astype(held.dtype)


def here(blocks, *arrays):
    if not pairwise(blocks):
        return arrays
    return [pltpu.with_memory_space_constraint(array, pltpu.VMEM) for array in arrays]


def grant(blocks):
    return pltpu.CompilerParams(vmem_limit_bytes=(24 << 20) if pairwise(blocks) else None)


def held(blocks, shape, dtype):
    return (pltpu.VMEM if pairwise(blocks) else jax.ShapeDtypeStruct)(shape, dtype)


def wire_shapes(blocks, chan, lanes):
    if pairwise(blocks):
        return [held(blocks, (chan, lanes), BF16)] * blocks
    return [held(blocks, (blocks, chan, lanes), BF16)]


def exchange(wires):
    if len(wires) == 1:
        return [lax.all_to_all(wires[0], "view", split_axis=0, concat_axis=0, tiled=True)]
    return [wires[0]] + [swap(wires[step], "view", step) for step in range(1, len(wires))]


def taps(w_ref, rows, forward):
    chan = w_ref.shape[2]
    blank = jnp.zeros((chan, chan), F32)
    found = {}
    for i in range(3):
        for j in range(3):
            tap = w_ref[i, j].astype(F32)
            found[i, j] = tap if forward else jnp.transpose(tap)
    bands = []
    for j in range(3):
        for r in range(rows):
            row = []
            for place in range(rows + 2):
                i = place - r if forward else r + 2 - place
                row.append(found[i, j] if 0 <= i < 3 else blank)
            bands.append(jnp.concatenate(row, axis=1))
    return jnp.concatenate(bands, axis=0).astype(BF16)


def spread(frame_ref, acc_ref, weights, rows, forward):
    width, deep, lanes = frame_ref.shape
    chan = deep // (rows + 2)
    size = rows * chan
    acc_ref[...] = jnp.zeros_like(acc_ref)

    def pair(q, carry):
        two = jnp.concatenate([frame_ref[2 * q], frame_ref[2 * q + 1]], axis=1)
        part = dot(weights, two)
        for j in range(3):
            move = 1 - j if forward else j - 1
            for side in range(2):
                acc_ref[2 * q + side + move + 1] += part[
                    j * size : (j + 1) * size, side * lanes : (side + 1) * lanes
                ]
        return carry

    lax.fori_loop(0, width // 2, pair, 0, unroll=width <= 16)


def conv_kernel(blocks, x_ref, near_ref, far_ref, w_ref, *refs):
    *wires, frame_ref, acc_s, held_s = refs
    rows, width, chan, views = x_ref.shape
    own = rows * chan
    lanes = frame_ref.shape[2]
    odd = row_is_odd() > 0
    frame_ref[...] = jnp.zeros_like(frame_ref)

    def fill(w, carry):
        near, far = near_ref[w], far_ref[w]
        frame_ref[w, :chan, :views] = jnp.where(odd, near, far)
        for r in range(rows):
            frame_ref[w, (r + 1) * chan : (r + 2) * chan, :views] = x_ref[r, w]
        frame_ref[w, chan + own :, :views] = jnp.where(odd, far, near)
        return carry

    lax.fori_loop(0, width, fill, 0, unroll=width <= 16)
    weights = taps(w_ref, rows, True)
    spread(frame_ref, acc_s, weights, rows, True)
    breadth = width // blocks

    def block(b, carry):
        cells = []
        for r in range(rows):
            for k in range(breadth):
                w = b * breadth + k
                value = acc_s[w + 1, r * chan : (r + 1) * chan]
                value = value + frame_ref[w, (r + 1) * chan : (r + 2) * chan].astype(F32)
                cells.append(value[:, :views])
        cells = jnp.concatenate(cells, axis=1)
        held_s[b, :, : cells.shape[1]] = cells
        return carry

    lax.fori_loop(0, blocks, block, 0, unroll=blocks <= 4)
    give(wires, held_s)


def convolve(x, near, far, w_conv, blocks):
    rows, width, chan, views = x.shape
    own = rows * chan
    lanes = round_up(views, 128)
    wire = round_up(rows * (width // blocks) * views, 128)
    vmem = pl.BlockSpec(memory_space=pltpu.VMEM)
    shapes = wire_shapes(blocks, chan, wire)
    shapes = shapes + [held(blocks, (width, own + 2 * chan, lanes), BF16)]
    *wires, frame = pl.pallas_call(
        functools.partial(conv_kernel, blocks),
        out_shape=shapes,
        in_specs=[vmem] * 4,
        out_specs=[vmem] * len(shapes),
        scratch_shapes=[
            pltpu.VMEM((width + 2, own, lanes), F32),
            pltpu.VMEM((blocks, chan, wire), F32),
        ],
        name="conv",
        compiler_params=grant(blocks),
    )(*here(blocks, x, near, far), w_conv)
    return wires, frame


def weight_kernel(count, pieces, *refs):
    wires = refs[:pieces]
    frame_ref, g_ref, gain_ref = refs[pieces : pieces + 3]
    near_ref, far_ref, own_ref, *part_refs, held_s, col_s, pack_s = refs[pieces + 3 :]
    width, own, lanes = own_ref.shape
    blocks, chan, wire = held_s.shape
    rows = own // chan
    breadth = width // blocks
    views = count
    odd = row_is_odd()
    take(wires, held_s)
    col_s[0] = jnp.zeros((own, lanes), BF16)
    col_s[width + 1] = jnp.zeros((own, lanes), BF16)

    def block(b, carry):
        cells = held_s[b]
        for r in range(rows):
            for k in range(breadth):
                at = (r * breadth + k) * views
                value = cells[:, at : at + views]
                if lanes > views:
                    value = jnp.concatenate(
                        [value, jnp.zeros((chan, lanes - views), F32)], axis=1
                    )
                col_s[b * breadth + k + 1, r * chan : (r + 1) * chan] = value.astype(BF16)
        return carry

    lax.fori_loop(0, blocks, block, 0, unroll=blocks <= 4)

    def copy(w, carry):
        cells = col_s[w + 1]
        own_ref[w] = cells
        first, last = cells[:chan], cells[own - chan :]
        near_ref[w] = jnp.where(odd > 0, first, last)
        far_ref[w] = jnp.where(odd > 0, last, first)
        return carry

    lax.fori_loop(0, width, copy, 0, unroll=width <= 16)

    def pair(q, total):
        left, right = [], []
        for side in range(2):
            w = 2 * q + side
            left.append(jnp.concatenate([col_s[w], col_s[w + 1], col_s[w + 2]], axis=0))
            right.append(frame_ref[w])
        return total + dot(
            jnp.concatenate(left, axis=1), jnp.concatenate(right, axis=1), (1, 1)
        )

    total = lax.fori_loop(
        0,
        width // 2,
        pair,
        jnp.zeros((3 * own, own + 2 * chan), F32),
        unroll=width <= 16,
    )
    bands = []
    for shift in range(3):
        band = 0.0
        for r in range(rows):
            top = (shift * rows + r) * chan
            band = band + total[top : top + chan, r * chan : (r + 3) * chan]
        bands.append(band)
    g_conv = jnp.concatenate(bands, axis=0)
    edge = 2 * chan
    pack_s[...] = jnp.zeros_like(pack_s)
    pack_s[: 2 * chan] = g_ref[...]
    pack_s[2 * chan : 2 * chan + 8] = gain_ref[...]
    at = 2 * chan + 8
    pack_s[at : at + 3 * chan] = g_conv[:, :edge]
    half = 3 * chan // 2
    rest = g_conv[:, edge:]
    pack_s[at + 3 * chan : at + 3 * chan + half] = jnp.concatenate(
        [rest[:half], rest[half:]], axis=1
    )
    size = part_refs[0].shape[0]
    for step, ref in enumerate(part_refs):
        turn = lax.axis_index("row") ^ step if len(part_refs) > 1 else 0
        ref[...] = pack_s[pl.ds(pl.multiple_of(turn * size, 16), size)].astype(ref.dtype)


def weight_grads(wires, frame, g_weights, g_gain, views, blocks):
    width, deep, lanes = frame.shape
    chan, wire = wires[0].shape[-2:]
    own = deep - 2 * chan
    count = lax.axis_size("row")
    parts = count if pairwise(count) else 1
    size = round_up(2 * chan + 8 + 9 * chan // 2, 16 * parts) // parts
    vmem = pl.BlockSpec(memory_space=pltpu.VMEM)
    return pl.pallas_call(
        functools.partial(weight_kernel, views, len(wires)),
        out_shape=(
            held(blocks, (width, chan, lanes), BF16),
            held(blocks, (width, chan, lanes), BF16),
            held(blocks, (width, own, lanes), BF16),
        )
        + (held(blocks, (size, 2 * chan), BF16 if parts > 1 else F32),) * parts,
        in_specs=[vmem] * (len(wires) + 3),
        out_specs=(vmem,) * (3 + parts),
        scratch_shapes=[
            pltpu.VMEM((blocks, chan, wire), F32),
            pltpu.VMEM((width + 2, own, lanes), BF16),
            pltpu.VMEM((parts * size, 2 * chan), F32),
        ],
        name="weights",
        compiler_params=grant(blocks),
    )(*here(blocks, *wires, frame, g_weights, g_gain))


def input_kernel(own_ref, near_ref, far_ref, w_ref, out_ref, frame_s, acc_s):
    width, own, lanes = own_ref.shape
    chan = near_ref.shape[1]
    rows = own // chan
    views = out_ref.shape[3]
    odd = row_is_odd() > 0

    def fill(w, carry):
        near, far = near_ref[w], far_ref[w]
        frame_s[w, :chan] = jnp.where(odd, near, far)
        frame_s[w, chan : chan + own] = own_ref[w]
        frame_s[w, chan + own :] = jnp.where(odd, far, near)
        return carry

    lax.fori_loop(0, width, fill, 0, unroll=width <= 16)
    spread(frame_s, acc_s, taps(w_ref, rows, False), rows, False)

    def columns(q, carry):
        at = pl.multiple_of(16 * q, 16)
        cells = []
        for k in range(16):
            cells.append(acc_s[at + k + 1] + own_ref[at + k].astype(F32))
        cells = jnp.swapaxes(jnp.stack(cells), 0, 1).astype(BF16)
        for r in range(rows):
            out_ref[:, r, pl.ds(at, 16), :] = cells[r * chan : (r + 1) * chan, :, :views]
        return carry

    lax.fori_loop(0, width // 16, columns, 0)


def input_grad(own, near, far, w_conv, views, blocks):
    width, size, lanes = own.shape
    chan = near.shape[1]
    vmem = pl.BlockSpec(memory_space=pltpu.VMEM)
    return pl.pallas_call(
        input_kernel,
        out_shape=jax.ShapeDtypeStruct((chan, size // chan, width, views), BF16),
        in_specs=[vmem] * 4,
        out_specs=vmem,
        scratch_shapes=[
            pltpu.VMEM((width, size + 2 * chan, lanes), BF16),
            pltpu.VMEM((width + 2, size, lanes), F32),
        ],
        name="input",
        compiler_params=grant(blocks),
    )(*here(blocks, own, near, far), w_conv)


def unpack_kernel(parts, *refs):
    conv_ref, q_ref, k_ref, v_ref, o_ref, gain_ref, pack_s = refs[parts:]
    size = refs[0].shape[0]
    chan = q_ref.shape[0]
    for step in range(parts):
        turn = lax.axis_index("row") ^ step if parts > 1 else 0
        pack_s[pl.ds(pl.multiple_of(turn * size, 16), size)] = refs[step][...].astype(F32)
    k_ref[...] = pack_s[:chan, :chan]
    v_ref[...] = pack_s[:chan, chan:]
    q_ref[...] = pack_s[chan : 2 * chan, :chan]
    o_ref[...] = pack_s[chan : 2 * chan, chan:]
    gain_ref[...] = pack_s[2 * chan : 2 * chan + 1, :chan]
    at = 2 * chan + 8
    half = 3 * chan // 2
    for j in range(3):
        top = (2 - j) * chan
        for i in range(2):
            conv_ref[i, j] = pack_s[at + top : at + top + chan, i * chan : (i + 1) * chan]
        for low in range(0, chan, chan // 2):
            row = top + low
            side = row // half
            start = at + 3 * chan + row - side * half
            conv_ref[2, j, low : low + chan // 2] = pack_s[
                start : start + chan // 2, side * chan : (side + 1) * chan
            ]


def unpack(parts, chan, blocks):
    vmem = pl.BlockSpec(memory_space=pltpu.VMEM)
    square = jax.ShapeDtypeStruct((chan, chan), F32)
    return pl.pallas_call(
        functools.partial(unpack_kernel, len(parts)),
        out_shape=(
            jax.ShapeDtypeStruct((3, 3, chan, chan), F32),
            square,
            square,
            square,
            square,
            jax.ShapeDtypeStruct((1, chan), F32),
        ),
        in_specs=[vmem] * len(parts),
        out_specs=(vmem,) * 6,
        scratch_shapes=[pltpu.VMEM((len(parts) * parts[0].shape[0], 2 * chan), F32)],
        name="unpack",
        compiler_params=grant(blocks),
    )(*here(blocks, *parts))


def angular_kernel(
    scale,
    lag,
    pieces,
    *refs,
):
    wires_in = refs[:pieces]
    cot_ref, keep_ref, gain_row, wq_ref, wkey_ref, wv_ref, wo_ref = refs[pieces : pieces + 7]
    refs = refs[pieces + 7 :]
    wires_out = refs[:pieces]
    out_ref, g_ref, ggain_ref = refs[pieces : pieces + 3]
    refs = refs[pieces + 3 :]
    held_s, give_s, bias_ref, gain_ref, wqkv_ref, wkv_ref, wot_ref, wkv2_ref, gain_s = refs[:9]
    scratch = refs[9:]
    blocks = held_s.shape[0]
    pixels, chan, lanes = cot_ref.shape
    used = keep_ref.shape[1]
    each = used // blocks
    rows = bias_ref.shape[0]
    per = 7
    slots = len(scratch) // per
    inv_chan = 1.0 / chan
    take(wires_in, held_s)
    live = jnp.where(keep_ref[...] > 0, 0.0, -1e30).astype(F32)
    live = jnp.concatenate([live, jnp.full((1, lanes - used), -1e30, F32)], axis=1)
    live = jnp.transpose(jnp.broadcast_to(live, (128, lanes)))[:rows]
    lane = lax.broadcasted_iota(jnp.int32, (rows, 128), 1)
    bias_ref[...] = jnp.where(lane == chan, live, 0.0)[:, : 2 * chan]
    eye = lax.broadcasted_iota(jnp.int32, (chan, chan), 0) == lax.broadcasted_iota(
        jnp.int32, (chan, chan), 1
    )
    gain_ref[...] = jnp.sum(jnp.where(eye, gain_row[...], 0.0), axis=1, keepdims=True)
    w_q, w_k, w_v = (ref[...].astype(F32) for ref in (wq_ref, wkey_ref, wv_ref))
    wqkv_ref[...] = jnp.concatenate(
        [jnp.transpose(w_q), jnp.transpose(w_k), jnp.transpose(w_v)], axis=0
    ).astype(BF16)
    blank = jnp.zeros((chan, chan), F32)
    wkv_ref[...] = jnp.concatenate([w_k, blank, w_v, blank], axis=1).astype(BF16)
    wkv2_ref[...] = jnp.concatenate([w_k, w_v], axis=1).astype(BF16)
    wot_ref[...] = jnp.transpose(wo_ref[...].astype(F32)).astype(BF16)
    g_ref[...] = jnp.zeros_like(g_ref)
    gain_s[...] = jnp.zeros_like(gain_s)
    for slot in range(slots):
        d_s = scratch[per * slot + 5]
        d_s[rows:] = jnp.zeros((lanes - rows, 2 * chan), BF16)
    chunks = []
    at = 0
    while at < rows:
        size = min(80, rows - at)
        chunks.append((at, size))
        at += size
    half_lane = lax.broadcasted_iota(jnp.int32, (chan, 2 * chan), 1) < chan

    def pixel(p):
        start = per * (p % slots)
        s_s, e_s, n_s, x_s, kv_s, d_s, nb_s = scratch[start : start + per]
        cells = [held_s[b, :, p * each : (p + 1) * each] for b in range(blocks)]
        if lanes > used:
            cells.append(jnp.zeros((chan, lanes - used), held_s.dtype))
        s = jnp.concatenate(cells, axis=1).astype(F32)
        x_s[...] = s
        cen = s - jnp.sum(s, axis=0, keepdims=True) * inv_chan
        rstd = lax.rsqrt(jnp.sum(cen * cen, axis=0, keepdims=True) * inv_chan + 1e-05)
        normed = cen * rstd
        n_s[...] = normed
        nin32 = normed * gain_ref[...]
        nin = nin32.astype(BF16)
        nb_s[...] = nin
        nin_t = jnp.transpose(nin32)[:rows].astype(BF16)
        yield
        kv = dot(nin_t, wkv_ref[...])
        kv_s[:, : 2 * chan] = (kv[:, : 2 * chan] + bias_ref[...]).astype(BF16)
        kv_s[:, 2 * chan :] = kv[:, 2 * chan :].astype(BF16)
        yield
        qkv = dot(wqkv_ref[...], nin)
        q = (qkv[:chan].astype(BF16).astype(F32) * scale).astype(BF16)
        k = qkv[chan : 2 * chan, :rows].astype(BF16)
        v = qkv[2 * chan :, :rows].astype(BF16)
        zero = jnp.zeros((chan, lanes), BF16)
        q_aug = jnp.concatenate([q, jnp.ones((16, lanes), BF16), zero[16:]], axis=0)
        yield
        s_s[...] = dot(kv_s[:, : 2 * chan], q_aug)
        yield
        high = None
        for at, size in chunks:
            top = jnp.max(s_s[at : at + size].reshape(size // 8, 8, lanes), axis=0)
            high = top if high is None else jnp.maximum(high, top)
        high = jnp.max(high, axis=0, keepdims=True)
        yield
        for at, size in chunks:
            e_s[at : at + size, :lanes] = jnp.exp(s_s[at : at + size] - high).astype(BF16)
            yield
        v_aug = jnp.concatenate([v, jnp.ones((16, rows), BF16)], axis=0)
        att_aug = dot(v_aug, e_s[:, :lanes])
        yield
        cot = cot_ref[p]
        d_att32 = dot(wo_ref[...], cot).astype(BF16).astype(F32)
        inv = 1.0 / att_aug[chan : chan + 1]
        att = att_aug[:chan] * inv
        att_b = att.astype(BF16)
        d_att = (d_att32 * inv).astype(BF16)
        inner = jnp.sum(att * d_att.astype(F32), axis=0, keepdims=True)
        yield
        d_aug = jnp.concatenate([d_att, zero], axis=0)
        s_s[...] = dot(kv_s[:, 2 * chan :], d_aug)
        yield
        for at, size in chunks:
            e_s[at : at + size, lanes:] = e_s[at : at + size, :lanes] * (s_s[at : at + size] - inner).astype(BF16)
            yield
        low = jnp.concatenate(
            [jnp.concatenate([zero, d_att], axis=0), jnp.concatenate([q, zero], axis=0)], axis=1
        )
        d_s[:rows] = dot(e_s[...], low, (1, 1)).astype(BF16)
        yield
        d_q = (dot(k, e_s[:, lanes:]) * scale).astype(BF16)
        yield
        out_ref[p] = (x_s[...] + dot(wot_ref[...], att_b)).astype(BF16)[:, :used]
        yield
        dn = dot(wq_ref[...], d_q) + dot(wkv2_ref[...], d_s[...], (1, 1))
        nin = nb_s[...]
        g_ref[:chan] += dot(nin, d_s[...])
        both = dot(
            jnp.concatenate([nin, att_b], axis=0), jnp.concatenate([d_q, cot], axis=0), (1, 1)
        )
        g_ref[chan:] += jnp.where(half_lane, both[:chan], both[chan:])
        yield
        normed = n_s[...]
        dnn = dn * normed
        gain_s[...] += dnn
        scaled = dn * gain_ref[...]
        back = (
            scaled
            - jnp.sum(scaled, axis=0, keepdims=True) * inv_chan
            - normed * (jnp.sum(dnn * gain_ref[...], axis=0, keepdims=True) * inv_chan)
        )
        done = (cot.astype(F32) + back * rstd).astype(give_s.dtype)
        for b in range(blocks):
            give_s[b, :, p * each : (p + 1) * each] = done[:, b * each : (b + 1) * each]
        yield

    waiting = [pixel(p) for p in range(pixels)]
    active = []
    step = 0
    while waiting or active:
        if waiting and step % lag == 0:
            active += waiting[:2]
            waiting = waiting[2:]
        for run in list(active):
            try:
                next(run)
            except StopIteration:
                active.remove(run)
        step += 1
    g_gain = jnp.sum(gain_s[...], axis=1, keepdims=True)
    g_gain = jnp.sum(jnp.where(eye, g_gain, 0.0), axis=0, keepdims=True)
    g_gain = jnp.concatenate([g_gain, jnp.zeros((1, chan), F32)], axis=1)
    ggain_ref[...] = jnp.broadcast_to(g_gain, ggain_ref.shape)
    give(wires_out, give_s)


def angular(wires, cotangent, keep, gain, w_query, w_key, w_value, w_out, blocks):
    pixels, chan, lanes = cotangent.shape
    used = keep.shape[0]
    rows = round_up(used, 16)
    wire = wires[0].shape[-1]
    vmem = pl.BlockSpec(memory_space=pltpu.VMEM)
    scale = 1.0 / math.sqrt(chan)
    shapes = wire_shapes(blocks, chan, wire) + [
        jax.ShapeDtypeStruct((pixels, chan, used), BF16),
        held(blocks, (2 * chan, 2 * chan), F32),
        held(blocks, (8, 2 * chan), F32),
    ]
    *out, output, g_weights, g_gain = pl.pallas_call(
        functools.partial(angular_kernel, scale, 8, len(wires)),
        out_shape=shapes,
        in_specs=[vmem] * (len(wires) + 7),
        out_specs=[vmem] * len(shapes),
        scratch_shapes=[
            pltpu.VMEM((blocks, chan, wire), BF16),
            pltpu.VMEM((blocks, chan, wire), BF16),
            pltpu.VMEM((rows, 2 * chan), F32),
            pltpu.VMEM((chan, 1), F32),
            pltpu.VMEM((3 * chan, chan), BF16),
            pltpu.VMEM((chan, 4 * chan), BF16),
            pltpu.VMEM((chan, chan), BF16),
            pltpu.VMEM((chan, 2 * chan), BF16),
            pltpu.VMEM((chan, lanes), F32),
        ]
        + [
            pltpu.VMEM((rows, lanes), F32),
            pltpu.VMEM((rows, 2 * lanes), BF16),
            pltpu.VMEM((chan, lanes), F32),
            pltpu.VMEM((chan, lanes), F32),
            pltpu.VMEM((rows, 4 * chan), BF16),
            pltpu.VMEM((lanes, 2 * chan), BF16),
            pltpu.VMEM((chan, lanes), BF16),
        ]
        * 6,
        name="angular",
        compiler_params=grant(blocks),
    )(*here(blocks, *wires, cotangent), keep[None, :], gain[None, :], w_query, w_key, w_value, w_out)
    return out, output, g_weights, g_gain


def sum_parts(parts):
    total = parts[0].astype(F32)
    for part in parts[1:]:
        total = total + part.astype(F32)
    return total


def reduce_views(own, beside):
    count = lax.axis_size("view")
    if not pairwise(count):
        return lax.psum(own, "view"), beside
    own = own.astype(BF16)
    parts = [swap(own, "view", step) for step in range(1, count)]
    parts, beside = lax.optimization_barrier((parts, beside))
    return sum_parts([own] + parts), beside


def scatter_rows(parts):
    if len(parts) == 1:
        return lax.psum(parts[0], "row")
    return sum_parts(
        [parts[0]] + [swap(parts[step], "row", step) for step in range(1, len(parts))]
    )


def gather_rows(own, count):
    if count == 1:
        return [own]
    own = own.astype(BF16)
    return [own] + [swap(own, "row", step) for step in range(1, count)]


def body(inputs, cotangent, keep, w_conv, gain, w_query, w_key, w_value, w_out):
    chan, view_dev, row_dev, width = inputs.shape
    blocks = lax.axis_size("view")
    breadth = width // blocks
    views = view_dev * blocks
    lanes = round_up(views, 128)
    pixels = row_dev * breadth
    odd = row_is_odd() > 0
    x = jnp.transpose(inputs, (2, 3, 0, 1))
    first, last = x[0], x[row_dev - 1]
    near, far = halo_swap(jnp.where(odd, first, last), jnp.where(odd, last, first))
    w_conv = jnp.transpose(w_conv, (2, 3, 0, 1))
    wires, frame = convolve(x, near, far, w_conv, blocks)
    wires = exchange(wires)
    cot = jnp.transpose(cotangent, (2, 3, 0, 1)).reshape(pixels, chan, views)
    cot = jnp.pad(cot, ((0, 0), (0, 0), (0, lanes - views)))
    wires, output, g_weights, g_gain = angular(
        wires, cot, keep, gain, w_query, w_key, w_value, w_out, blocks
    )
    output = jnp.transpose(output.reshape(row_dev, breadth, chan, views), (2, 3, 0, 1))
    wires, output = lax.optimization_barrier((exchange(wires), output))
    near, far, own, *parts = weight_grads(wires, frame, g_weights, g_gain, view_dev, blocks)
    part = scatter_rows(parts)
    near, far = halo_swap(near, far)
    d_input = input_grad(own, near, far, w_conv, view_dev, blocks)
    part, d_input = reduce_views(part, d_input)
    parts = gather_rows(part, len(parts))
    g_conv, g_query, g_key, g_value, g_out, g_gain = unpack(parts, chan, blocks)
    d_input = jnp.transpose(d_input, (0, 3, 1, 2))
    g_conv = jnp.transpose(g_conv, (2, 3, 0, 1))
    return (output, d_input, g_conv, g_gain[0], g_query, g_key, g_value, g_out)


def solution(mesh):
    placed = (
        P(None, "view", ("groups", "row"), None),
        P(None, None, ("groups", "row"), "view"),
        P("groups"),
        P(),
        P(),
        P(),
        P(),
        P(),
        P(),
    )
    return jax.shard_map(
        body,
        mesh=mesh,
        in_specs=placed,
        out_specs=(
            P(None, None, ("groups", "row"), "view"),
            P(None, "view", ("groups", "row"), None),
            P("groups", None, None, None),
            P("groups"),
            P("groups", None),
            P("groups", None),
            P("groups", None),
            P("groups", None),
        ),
        check_vma=False,
    )
```

```python
import functools
import math

import jax
import jax.numpy as jnp
from jax import lax
from jax.experimental import pallas as pl
from jax.experimental.pallas import tpu as pltpu
from jax.sharding import PartitionSpec as P

F32 = jnp.float32
BF16 = jnp.bfloat16


def round_up(value, unit):
    return -(-value // unit) * unit


def dot(left, right, contract=(1, 0)):
    return lax.dot_general(
        left, right, (((contract[0],), (contract[1],)), ((), ())), preferred_element_type=F32
    )


def pairwise(count):
    return count <= 8 and count & (count - 1) == 0


def swap(cells, axis, step):
    count = lax.axis_size(axis)
    return lax.ppermute(cells, axis, [(i, i ^ step) for i in range(count)])


def halo_swap(near, far):
    count = lax.axis_size("row")
    pairs = []
    for i in range(1, count - 1, 2):
        pairs += [(i, i + 1), (i + 1, i)]
    got_near = lax.ppermute(near, "row", [(i, i ^ 1) for i in range(count)])
    got_far = lax.ppermute(far, "row", pairs) if pairs else jnp.zeros_like(far)
    return got_near, got_far


def row_is_odd():
    return lax.rem(lax.axis_index("row"), 2)


def give(refs, held):
    if len(refs) == 1:
        refs[0][...] = held[...].astype(refs[0].dtype)
        return
    me = lax.axis_index("view")
    for step, ref in enumerate(refs):
        ref[...] = held[me ^ step].astype(ref.dtype)


def take(refs, held):
    if len(refs) == 1:
        held[...] = refs[0][...].astype(held.dtype)
        return
    me = lax.axis_index("view")
    for step, ref in enumerate(refs):
        held[me ^ step] = ref[...].astype(held.dtype)


def here(blocks, *arrays):
    if not pairwise(blocks):
        return arrays
    return [pltpu.with_memory_space_constraint(array, pltpu.VMEM) for array in arrays]


def grant(blocks):
    return pltpu.CompilerParams(vmem_limit_bytes=(24 << 20) if pairwise(blocks) else None)


def held(blocks, shape, dtype):
    return (pltpu.VMEM if pairwise(blocks) else jax.ShapeDtypeStruct)(shape, dtype)


def wire_shapes(blocks, chan, lanes):
    if pairwise(blocks):
        return [held(blocks, (chan, lanes), BF16)] * blocks
    return [held(blocks, (blocks, chan, lanes), BF16)]


def exchange(wires):
    if len(wires) == 1:
        return [lax.all_to_all(wires[0], "view", split_axis=0, concat_axis=0, tiled=True)]
    return [wires[0]] + [swap(wires[step], "view", step) for step in range(1, len(wires))]


def taps(w_ref, rows, forward):
    chan = w_ref.shape[2]
    blank = jnp.zeros((chan, chan), F32)
    found = {}
    for i in range(3):
        for j in range(3):
            tap = w_ref[i, j].astype(F32)
            found[i, j] = tap if forward else jnp.transpose(tap)
    bands = []
    for j in range(3):
        for r in range(rows):
            row = []
            for place in range(rows + 2):
                i = place - r if forward else r + 2 - place
                row.append(found[i, j] if 0 <= i < 3 else blank)
            bands.append(jnp.concatenate(row, axis=1))
    return jnp.concatenate(bands, axis=0).astype(BF16)


def spread(frame_ref, acc_ref, weights, rows, forward):
    width, deep, lanes = frame_ref.shape
    chan = deep // (rows + 2)
    size = rows * chan
    acc_ref[...] = jnp.zeros_like(acc_ref)

    def pair(q, carry):
        two = jnp.concatenate([frame_ref[2 * q], frame_ref[2 * q + 1]], axis=1)
        part = dot(weights, two)
        for j in range(3):
            move = 1 - j if forward else j - 1
            for side in range(2):
                acc_ref[2 * q + side + move + 1] += part[
                    j * size : (j + 1) * size, side * lanes : (side + 1) * lanes
                ]
        return carry

    lax.fori_loop(0, width // 2, pair, 0, unroll=width <= 16)


def conv_kernel(blocks, x_ref, near_ref, far_ref, w_ref, *refs):
    *wires, frame_ref, acc_s, held_s = refs
    rows, width, chan, views = x_ref.shape
    own = rows * chan
    lanes = frame_ref.shape[2]
    odd = row_is_odd() > 0
    frame_ref[...] = jnp.zeros_like(frame_ref)

    def fill(w, carry):
        near, far = near_ref[w], far_ref[w]
        frame_ref[w, :chan, :views] = jnp.where(odd, near, far)
        for r in range(rows):
            frame_ref[w, (r + 1) * chan : (r + 2) * chan, :views] = x_ref[r, w]
        frame_ref[w, chan + own :, :views] = jnp.where(odd, far, near)
        return carry

    lax.fori_loop(0, width, fill, 0, unroll=width <= 16)
    weights = taps(w_ref, rows, True)
    spread(frame_ref, acc_s, weights, rows, True)
    breadth = width // blocks

    def block(b, carry):
        cells = []
        for r in range(rows):
            for k in range(breadth):
                w = b * breadth + k
                value = acc_s[w + 1, r * chan : (r + 1) * chan]
                value = value + frame_ref[w, (r + 1) * chan : (r + 2) * chan].astype(F32)
                cells.append(value[:, :views])
        cells = jnp.concatenate(cells, axis=1)
        held_s[b, :, : cells.shape[1]] = cells
        return carry

    lax.fori_loop(0, blocks, block, 0, unroll=blocks <= 4)
    give(wires, held_s)


def convolve(x, near, far, w_conv, blocks):
    rows, width, chan, views = x.shape
    own = rows * chan
    lanes = round_up(views, 128)
    wire = round_up(rows * (width // blocks) * views, 128)
    vmem = pl.BlockSpec(memory_space=pltpu.VMEM)
    shapes = wire_shapes(blocks, chan, wire)
    shapes = shapes + [held(blocks, (width, own + 2 * chan, lanes), BF16)]
    *wires, frame = pl.pallas_call(
        functools.partial(conv_kernel, blocks),
        out_shape=shapes,
        in_specs=[vmem] * 4,
        out_specs=[vmem] * len(shapes),
        scratch_shapes=[
            pltpu.VMEM((width + 2, own, lanes), F32),
            pltpu.VMEM((blocks, chan, wire), F32),
        ],
        name="conv",
        compiler_params=grant(blocks),
    )(*here(blocks, x, near, far), w_conv)
    return wires, frame


def weight_kernel(count, pieces, *refs):
    wires = refs[:pieces]
    frame_ref, g_ref, gain_ref = refs[pieces : pieces + 3]
    near_ref, far_ref, own_ref, *part_refs, held_s, col_s, pack_s = refs[pieces + 3 :]
    width, own, lanes = own_ref.shape
    blocks, chan, wire = held_s.shape
    rows = own // chan
    breadth = width // blocks
    views = count
    odd = row_is_odd()
    take(wires, held_s)
    col_s[0] = jnp.zeros((own, lanes), BF16)
    col_s[width + 1] = jnp.zeros((own, lanes), BF16)

    def block(b, carry):
        cells = held_s[b]
        for r in range(rows):
            for k in range(breadth):
                at = (r * breadth + k) * views
                value = cells[:, at : at + views]
                if lanes > views:
                    value = jnp.concatenate(
                        [value, jnp.zeros((chan, lanes - views), BF16)], axis=1
                    )
                col_s[b * breadth + k + 1, r * chan : (r + 1) * chan] = value
        return carry

    lax.fori_loop(0, blocks, block, 0, unroll=blocks <= 4)

    def copy(w, carry):
        own_ref[w] = col_s[w + 1]
        return carry

    lax.fori_loop(0, width, copy, 0, unroll=width <= 16)
    edges = []
    for r in (0, rows - 1):
        span = breadth * views
        edges.append(
            jnp.concatenate(
                [held_s[b, :, r * span : (r + 1) * span] for b in range(blocks)], axis=1
            )
        )
    near_ref[:, : width * views] = jnp.where(odd > 0, edges[0], edges[1])
    far_ref[:, : width * views] = jnp.where(odd > 0, edges[1], edges[0])

    def pair(q, total):
        left, right = [], []
        for side in range(2):
            w = 2 * q + side
            left.append(jnp.concatenate([col_s[w], col_s[w + 1], col_s[w + 2]], axis=0))
            right.append(frame_ref[w])
        return total + dot(
            jnp.concatenate(left, axis=1), jnp.concatenate(right, axis=1), (1, 1)
        )

    total = lax.fori_loop(
        0,
        width // 2,
        pair,
        jnp.zeros((3 * own, own + 2 * chan), F32),
        unroll=width <= 16,
    )
    bands = []
    for shift in range(3):
        band = 0.0
        for r in range(rows):
            top = (shift * rows + r) * chan
            band = band + total[top : top + chan, r * chan : (r + 3) * chan]
        bands.append(band)
    g_conv = jnp.concatenate(bands, axis=0)
    edge = 2 * chan
    pack_s[...] = jnp.zeros_like(pack_s)
    pack_s[: 2 * chan] = g_ref[...]
    pack_s[2 * chan : 2 * chan + 8] = gain_ref[...]
    at = 2 * chan + 8
    pack_s[at : at + 3 * chan] = g_conv[:, :edge]
    half = 3 * chan // 2
    rest = g_conv[:, edge:]
    pack_s[at + 3 * chan : at + 3 * chan + half] = jnp.concatenate(
        [rest[:half], rest[half:]], axis=1
    )
    size = part_refs[0].shape[0]
    for step, ref in enumerate(part_refs):
        turn = lax.axis_index("row") ^ step if len(part_refs) > 1 else 0
        ref[...] = pack_s[pl.ds(pl.multiple_of(turn * size, 16), size)].astype(ref.dtype)


def weight_grads(wires, frame, g_weights, g_gain, views, blocks):
    width, deep, lanes = frame.shape
    chan, wire = wires[0].shape[-2:]
    own = deep - 2 * chan
    count = lax.axis_size("row")
    parts = count if pairwise(count) else 1
    size = round_up(2 * chan + 8 + 9 * chan // 2, 16 * parts) // parts
    vmem = pl.BlockSpec(memory_space=pltpu.VMEM)
    return pl.pallas_call(
        functools.partial(weight_kernel, views, len(wires)),
        out_shape=(
            held(blocks, (chan, round_up(width * views, 128)), BF16),
            held(blocks, (chan, round_up(width * views, 128)), BF16),
            held(blocks, (width, own, lanes), BF16),
        )
        + (held(blocks, (size, 2 * chan), BF16 if parts > 1 else F32),) * parts,
        in_specs=[vmem] * (len(wires) + 3),
        out_specs=(vmem,) * (3 + parts),
        scratch_shapes=[
            pltpu.VMEM((blocks, chan, wire), BF16),
            pltpu.VMEM((width + 2, own, lanes), BF16),
            pltpu.VMEM((parts * size, 2 * chan), F32),
        ],
        name="weights",
        compiler_params=grant(blocks),
    )(*here(blocks, *wires, frame, g_weights, g_gain))


def input_kernel(own_ref, near_ref, far_ref, w_ref, out_ref, frame_s, acc_s):
    width, own, lanes = own_ref.shape
    chan = near_ref.shape[0]
    rows = own // chan
    views = out_ref.shape[3]
    odd = row_is_odd() > 0
    for w in range(width):
        near = near_ref[:, w * views : (w + 1) * views]
        far = far_ref[:, w * views : (w + 1) * views]
        frame_s[w, :chan, :views] = jnp.where(odd, near, far)
        frame_s[w, chan + own :, :views] = jnp.where(odd, far, near)

    def fill(w, carry):
        frame_s[w, chan : chan + own] = own_ref[w]
        return carry

    lax.fori_loop(0, width, fill, 0, unroll=width <= 16)
    spread(frame_s, acc_s, taps(w_ref, rows, False), rows, False)

    def columns(q, carry):
        at = pl.multiple_of(16 * q, 16)
        cells = []
        for k in range(16):
            cells.append(acc_s[at + k + 1] + own_ref[at + k].astype(F32))
        cells = jnp.swapaxes(jnp.stack(cells), 0, 1).astype(BF16)
        for r in range(rows):
            out_ref[:, r, pl.ds(at, 16), :] = cells[r * chan : (r + 1) * chan, :, :views]
        return carry

    lax.fori_loop(0, width // 16, columns, 0)


def input_grad(own, near, far, w_conv, views, blocks):
    width, size, lanes = own.shape
    chan = near.shape[0]
    vmem = pl.BlockSpec(memory_space=pltpu.VMEM)
    return pl.pallas_call(
        input_kernel,
        out_shape=jax.ShapeDtypeStruct((chan, size // chan, width, views), BF16),
        in_specs=[vmem] * 4,
        out_specs=vmem,
        scratch_shapes=[
            pltpu.VMEM((width, size + 2 * chan, lanes), BF16),
            pltpu.VMEM((width + 2, size, lanes), F32),
        ],
        name="input",
        compiler_params=grant(blocks),
    )(*here(blocks, own, near, far), w_conv)


def unpack_kernel(parts, *refs):
    conv_ref, q_ref, k_ref, v_ref, o_ref, gain_ref, pack_s = refs[parts:]
    size = refs[0].shape[0]
    chan = q_ref.shape[0]
    for step in range(parts):
        turn = lax.axis_index("row") ^ step if parts > 1 else 0
        pack_s[pl.ds(pl.multiple_of(turn * size, 16), size)] = refs[step][...].astype(F32)
    k_ref[...] = pack_s[:chan, :chan]
    v_ref[...] = pack_s[:chan, chan:]
    q_ref[...] = pack_s[chan : 2 * chan, :chan]
    o_ref[...] = pack_s[chan : 2 * chan, chan:]
    gain_ref[...] = pack_s[2 * chan : 2 * chan + 1, :chan]
    at = 2 * chan + 8
    half = 3 * chan // 2
    for j in range(3):
        top = (2 - j) * chan
        for i in range(2):
            conv_ref[i, j] = pack_s[at + top : at + top + chan, i * chan : (i + 1) * chan]
        for low in range(0, chan, chan // 2):
            row = top + low
            side = row // half
            start = at + 3 * chan + row - side * half
            conv_ref[2, j, low : low + chan // 2] = pack_s[
                start : start + chan // 2, side * chan : (side + 1) * chan
            ]


def unpack(parts, chan, blocks):
    vmem = pl.BlockSpec(memory_space=pltpu.VMEM)
    square = jax.ShapeDtypeStruct((chan, chan), F32)
    return pl.pallas_call(
        functools.partial(unpack_kernel, len(parts)),
        out_shape=(
            jax.ShapeDtypeStruct((3, 3, chan, chan), F32),
            square,
            square,
            square,
            square,
            jax.ShapeDtypeStruct((1, chan), F32),
        ),
        in_specs=[vmem] * len(parts),
        out_specs=(vmem,) * 6,
        scratch_shapes=[pltpu.VMEM((len(parts) * parts[0].shape[0], 2 * chan), F32)],
        name="unpack",
        compiler_params=grant(blocks),
    )(*here(blocks, *parts))


def angular_kernel(
    scale,
    lag,
    pieces,
    *refs,
):
    wires_in = refs[:pieces]
    cot_ref, keep_ref, gain_row, wq_ref, wkey_ref, wv_ref, wo_ref = refs[pieces : pieces + 7]
    refs = refs[pieces + 7 :]
    wires_out = refs[:pieces]
    out_ref, g_ref, ggain_ref = refs[pieces : pieces + 3]
    refs = refs[pieces + 3 :]
    held_s, give_s, bias_ref, gain_ref, wqkv_ref, wkv_ref, wot_ref, wkv2_ref, gain_s = refs[:9]
    scratch = refs[9:]
    blocks = held_s.shape[0]
    pixels, chan, lanes = cot_ref.shape
    used = keep_ref.shape[1]
    each = used // blocks
    rows = bias_ref.shape[0]
    per = 7
    slots = len(scratch) // per
    inv_chan = 1.0 / chan
    take(wires_in, held_s)
    live = jnp.where(keep_ref[...] > 0, 0.0, -1e30).astype(F32)
    live = jnp.concatenate([live, jnp.full((1, lanes - used), -1e30, F32)], axis=1)
    live = jnp.transpose(jnp.broadcast_to(live, (128, lanes)))[:rows]
    lane = lax.broadcasted_iota(jnp.int32, (rows, 128), 1)
    bias_ref[...] = jnp.where(lane == chan, live, 0.0)[:, : 2 * chan]
    eye = lax.broadcasted_iota(jnp.int32, (chan, chan), 0) == lax.broadcasted_iota(
        jnp.int32, (chan, chan), 1
    )
    gain_ref[...] = jnp.sum(jnp.where(eye, gain_row[...], 0.0), axis=1, keepdims=True)
    w_q, w_k, w_v = (ref[...].astype(F32) for ref in (wq_ref, wkey_ref, wv_ref))
    wqkv_ref[...] = jnp.concatenate(
        [jnp.transpose(w_q), jnp.transpose(w_k), jnp.transpose(w_v)], axis=0
    ).astype(BF16)
    blank = jnp.zeros((chan, chan), F32)
    wkv_ref[...] = jnp.concatenate([w_k, blank, w_v, blank], axis=1).astype(BF16)
    wkv2_ref[...] = jnp.concatenate([w_k, w_v], axis=1).astype(BF16)
    wot_ref[...] = jnp.transpose(wo_ref[...].astype(F32)).astype(BF16)
    g_ref[...] = jnp.zeros_like(g_ref)
    gain_s[...] = jnp.zeros_like(gain_s)
    for slot in range(slots):
        d_s = scratch[per * slot + 5]
        d_s[rows:] = jnp.zeros((lanes - rows, 2 * chan), BF16)
    chunks = []
    at = 0
    while at < rows:
        size = min(80, rows - at)
        chunks.append((at, size))
        at += size
    half_lane = lax.broadcasted_iota(jnp.int32, (chan, 2 * chan), 1) < chan

    def pixel(p):
        start = per * (p % slots)
        s_s, e_s, n_s, x_s, kv_s, d_s, nb_s = scratch[start : start + per]
        cells = [held_s[b, :, p * each : (p + 1) * each] for b in range(blocks)]
        if lanes > used:
            cells.append(jnp.zeros((chan, lanes - used), held_s.dtype))
        s = jnp.concatenate(cells, axis=1).astype(F32)
        x_s[...] = s
        cen = s - jnp.sum(s, axis=0, keepdims=True) * inv_chan
        rstd = lax.rsqrt(jnp.sum(cen * cen, axis=0, keepdims=True) * inv_chan + 1e-05)
        normed = cen * rstd
        n_s[...] = normed
        nin32 = normed * gain_ref[...]
        nin = nin32.astype(BF16)
        nb_s[...] = nin
        nin_t = jnp.transpose(nin32)[:rows].astype(BF16)
        yield
        kv = dot(nin_t, wkv_ref[...])
        kv_s[:, : 2 * chan] = (kv[:, : 2 * chan] + bias_ref[...]).astype(BF16)
        kv_s[:, 2 * chan :] = kv[:, 2 * chan :].astype(BF16)
        yield
        qkv = dot(wqkv_ref[...], nin)
        q = (qkv[:chan].astype(BF16).astype(F32) * scale).astype(BF16)
        k = qkv[chan : 2 * chan, :rows].astype(BF16)
        v = qkv[2 * chan :, :rows].astype(BF16)
        zero = jnp.zeros((chan, lanes), BF16)
        q_aug = jnp.concatenate([q, jnp.ones((16, lanes), BF16), zero[16:]], axis=0)
        yield
        s_s[...] = dot(kv_s[:, : 2 * chan], q_aug)
        yield
        high = None
        for at, size in chunks:
            top = jnp.max(s_s[at : at + size].reshape(size // 8, 8, lanes), axis=0)
            high = top if high is None else jnp.maximum(high, top)
        high = jnp.max(high, axis=0, keepdims=True)
        yield
        for at, size in chunks:
            e_s[at : at + size, :lanes] = jnp.exp(s_s[at : at + size] - high).astype(BF16)
            yield
        v_aug = jnp.concatenate([v, jnp.ones((16, rows), BF16)], axis=0)
        att_aug = dot(v_aug, e_s[:, :lanes])
        yield
        cot = cot_ref[p]
        d_att32 = dot(wo_ref[...], cot).astype(BF16).astype(F32)
        inv = 1.0 / att_aug[chan : chan + 1]
        att = att_aug[:chan] * inv
        att_b = att.astype(BF16)
        d_att = (d_att32 * inv).astype(BF16)
        inner = jnp.sum(att * d_att.astype(F32), axis=0, keepdims=True)
        yield
        d_aug = jnp.concatenate([d_att, zero], axis=0)
        s_s[...] = dot(kv_s[:, 2 * chan :], d_aug)
        yield
        for at, size in chunks:
            e_s[at : at + size, lanes:] = e_s[at : at + size, :lanes] * (s_s[at : at + size] - inner).astype(BF16)
            yield
        low = jnp.concatenate(
            [jnp.concatenate([zero, d_att], axis=0), jnp.concatenate([q, zero], axis=0)], axis=1
        )
        d_s[:rows] = dot(e_s[...], low, (1, 1)).astype(BF16)
        yield
        d_q = (dot(k, e_s[:, lanes:]) * scale).astype(BF16)
        yield
        out_ref[p] = (x_s[...] + dot(wot_ref[...], att_b)).astype(BF16)[:, :used]
        yield
        dn = dot(wq_ref[...], d_q) + dot(wkv2_ref[...], d_s[...], (1, 1))
        nin = nb_s[...]
        g_ref[:chan] += dot(nin, d_s[...])
        both = dot(
            jnp.concatenate([nin, att_b], axis=0), jnp.concatenate([d_q, cot], axis=0), (1, 1)
        )
        g_ref[chan:] += jnp.where(half_lane, both[:chan], both[chan:])
        yield
        normed = n_s[...]
        dnn = dn * normed
        gain_s[...] += dnn
        scaled = dn * gain_ref[...]
        back = (
            scaled
            - jnp.sum(scaled, axis=0, keepdims=True) * inv_chan
            - normed * (jnp.sum(dnn * gain_ref[...], axis=0, keepdims=True) * inv_chan)
        )
        done = (cot.astype(F32) + back * rstd).astype(give_s.dtype)
        for b in range(blocks):
            give_s[b, :, p * each : (p + 1) * each] = done[:, b * each : (b + 1) * each]
        yield

    waiting = [pixel(p) for p in range(pixels)]
    active = []
    step = 0
    while waiting or active:
        if waiting and step % lag == 0:
            active += waiting[:2]
            waiting = waiting[2:]
        for run in list(active):
            try:
                next(run)
            except StopIteration:
                active.remove(run)
        step += 1
    g_gain = jnp.sum(gain_s[...], axis=1, keepdims=True)
    g_gain = jnp.sum(jnp.where(eye, g_gain, 0.0), axis=0, keepdims=True)
    g_gain = jnp.concatenate([g_gain, jnp.zeros((1, chan), F32)], axis=1)
    ggain_ref[...] = jnp.broadcast_to(g_gain, ggain_ref.shape)
    give(wires_out, give_s)


def angular(wires, cotangent, keep, gain, w_query, w_key, w_value, w_out, blocks):
    pixels, chan, lanes = cotangent.shape
    used = keep.shape[0]
    rows = round_up(used, 16)
    wire = wires[0].shape[-1]
    vmem = pl.BlockSpec(memory_space=pltpu.VMEM)
    scale = 1.0 / math.sqrt(chan)
    shapes = wire_shapes(blocks, chan, wire) + [
        jax.ShapeDtypeStruct((pixels, chan, used), BF16),
        held(blocks, (2 * chan, 2 * chan), F32),
        held(blocks, (8, 2 * chan), F32),
    ]
    *out, output, g_weights, g_gain = pl.pallas_call(
        functools.partial(angular_kernel, scale, 8, len(wires)),
        out_shape=shapes,
        in_specs=[vmem] * (len(wires) + 7),
        out_specs=[vmem] * len(shapes),
        scratch_shapes=[
            pltpu.VMEM((blocks, chan, wire), BF16),
            pltpu.VMEM((blocks, chan, wire), BF16),
            pltpu.VMEM((rows, 2 * chan), F32),
            pltpu.VMEM((chan, 1), F32),
            pltpu.VMEM((3 * chan, chan), BF16),
            pltpu.VMEM((chan, 4 * chan), BF16),
            pltpu.VMEM((chan, chan), BF16),
            pltpu.VMEM((chan, 2 * chan), BF16),
            pltpu.VMEM((chan, lanes), F32),
        ]
        + [
            pltpu.VMEM((rows, lanes), F32),
            pltpu.VMEM((rows, 2 * lanes), BF16),
            pltpu.VMEM((chan, lanes), F32),
            pltpu.VMEM((chan, lanes), F32),
            pltpu.VMEM((rows, 4 * chan), BF16),
            pltpu.VMEM((lanes, 2 * chan), BF16),
            pltpu.VMEM((chan, lanes), BF16),
        ]
        * 6,
        name="angular",
        compiler_params=grant(blocks),
    )(*here(blocks, *wires, cotangent), keep[None, :], gain[None, :], w_query, w_key, w_value, w_out)
    return out, output, g_weights, g_gain


def sum_parts(parts):
    total = parts[0].astype(F32)
    for part in parts[1:]:
        total = total + part.astype(F32)
    return total


def reduce_views(own):
    count = lax.axis_size("view")
    if not pairwise(count):
        return lax.psum(own, "view")
    own = own.astype(BF16)
    parts = [swap(own, "view", step) for step in range(1, count)]
    return sum_parts([own] + parts).astype(BF16)


def scatter_rows(parts):
    if len(parts) == 1:
        return lax.psum(parts[0], "row")
    return sum_parts(
        [parts[0]] + [swap(parts[step], "row", step) for step in range(1, len(parts))]
    )


def gather_rows(own, count):
    if count == 1:
        return [own]
    return [own] + [swap(own, "row", step) for step in range(1, count)]


def body(inputs, cotangent, keep, w_conv, gain, w_query, w_key, w_value, w_out):
    chan, view_dev, row_dev, width = inputs.shape
    blocks = lax.axis_size("view")
    breadth = width // blocks
    views = view_dev * blocks
    lanes = round_up(views, 128)
    pixels = row_dev * breadth
    odd = row_is_odd() > 0
    x = jnp.transpose(inputs, (2, 3, 0, 1))
    first, last = x[0], x[row_dev - 1]
    near, far = halo_swap(jnp.where(odd, first, last), jnp.where(odd, last, first))
    w_conv = jnp.transpose(w_conv, (2, 3, 0, 1))
    wires, frame = convolve(x, near, far, w_conv, blocks)
    wires = exchange(wires)
    cot = jnp.transpose(cotangent, (2, 3, 0, 1)).reshape(pixels, chan, views)
    cot = jnp.pad(cot, ((0, 0), (0, 0), (0, lanes - views)))
    wires, output, g_weights, g_gain = angular(
        wires, cot, keep, gain, w_query, w_key, w_value, w_out, blocks
    )
    output = jnp.transpose(output.reshape(row_dev, breadth, chan, views), (2, 3, 0, 1))
    wires, output = lax.optimization_barrier((exchange(wires), output))
    near, far, own, *parts = weight_grads(wires, frame, g_weights, g_gain, view_dev, blocks)
    part = scatter_rows(parts)
    near, far = halo_swap(near, far)
    part, near, far = lax.optimization_barrier((reduce_views(part), near, far))
    parts = gather_rows(part, len(parts))
    d_input = input_grad(own, near, far, w_conv, view_dev, blocks)
    parts, d_input = lax.optimization_barrier((parts, d_input))
    g_conv, g_query, g_key, g_value, g_out, g_gain = unpack(parts, chan, blocks)
    d_input = jnp.transpose(d_input, (0, 3, 1, 2))
    g_conv = jnp.transpose(g_conv, (2, 3, 0, 1))
    return (output, d_input, g_conv, g_gain[0], g_query, g_key, g_value, g_out)


def solution(mesh):
    placed = (
        P(None, "view", ("groups", "row"), None),
        P(None, None, ("groups", "row"), "view"),
        P("groups"),
        P(),
        P(),
        P(),
        P(),
        P(),
        P(),
    )
    return jax.shard_map(
        body,
        mesh=mesh,
        in_specs=placed,
        out_specs=(
            P(None, None, ("groups", "row"), "view"),
            P(None, "view", ("groups", "row"), None),
            P("groups", None, None, None),
            P("groups"),
            P("groups", None),
            P("groups", None),
            P("groups", None),
            P("groups", None),
        ),
        check_vma=False,
    )
```

```python
import functools
import math

import jax
import jax.numpy as jnp
from jax import lax
from jax.experimental import pallas as pl
from jax.experimental.pallas import tpu as pltpu
from jax.sharding import PartitionSpec as P

F32 = jnp.float32
BF16 = jnp.bfloat16


def round_up(value, unit):
    return -(-value // unit) * unit


def dot(left, right, contract=(1, 0)):
    return lax.dot_general(
        left, right, (((contract[0],), (contract[1],)), ((), ())), preferred_element_type=F32
    )


def pairwise(count):
    return count <= 8 and count & (count - 1) == 0


def swap(cells, axis, step):
    count = lax.axis_size(axis)
    return lax.ppermute(cells, axis, [(i, i ^ step) for i in range(count)])


def halo_swap(near, far):
    count = lax.axis_size("row")
    pairs = []
    for i in range(1, count - 1, 2):
        pairs += [(i, i + 1), (i + 1, i)]
    got_near = lax.ppermute(near, "row", [(i, i ^ 1) for i in range(count)])
    got_far = lax.ppermute(far, "row", pairs) if pairs else jnp.zeros_like(far)
    return got_near, got_far


def row_is_odd():
    return lax.rem(lax.axis_index("row"), 2)


def give(refs, held):
    if len(refs) == 1:
        refs[0][...] = held[...].astype(refs[0].dtype)
        return
    me = lax.axis_index("view")
    for step, ref in enumerate(refs):
        ref[...] = held[me ^ step].astype(ref.dtype)


def take(refs, held):
    if len(refs) == 1:
        held[...] = refs[0][...].astype(held.dtype)
        return
    me = lax.axis_index("view")
    for step, ref in enumerate(refs):
        held[me ^ step] = ref[...].astype(held.dtype)


def here(blocks, *arrays):
    if not pairwise(blocks):
        return arrays
    return [pltpu.with_memory_space_constraint(array, pltpu.VMEM) for array in arrays]


def grant(blocks):
    return pltpu.CompilerParams(vmem_limit_bytes=(24 << 20) if pairwise(blocks) else None)


def held(blocks, shape, dtype):
    return (pltpu.VMEM if pairwise(blocks) else jax.ShapeDtypeStruct)(shape, dtype)


def wire_shapes(blocks, chan, lanes):
    if pairwise(blocks):
        return [held(blocks, (chan, lanes), BF16)] * blocks
    return [held(blocks, (blocks, chan, lanes), BF16)]


def exchange(wires):
    if len(wires) == 1:
        return [lax.all_to_all(wires[0], "view", split_axis=0, concat_axis=0, tiled=True)]
    return [wires[0]] + [swap(wires[step], "view", step) for step in range(1, len(wires))]


def taps(w_ref, rows, forward):
    chan = w_ref.shape[2]
    blank = jnp.zeros((chan, chan), F32)
    found = {}
    for i in range(3):
        for j in range(3):
            tap = w_ref[i, j].astype(F32)
            found[i, j] = tap if forward else jnp.transpose(tap)
    bands = []
    for j in range(3):
        for r in range(rows):
            row = []
            for place in range(rows + 2):
                i = place - r if forward else r + 2 - place
                row.append(found[i, j] if 0 <= i < 3 else blank)
            bands.append(jnp.concatenate(row, axis=1))
    return jnp.concatenate(bands, axis=0).astype(BF16)


def spread(frame_ref, acc_ref, weights, rows, forward):
    width, deep, lanes = frame_ref.shape
    chan = deep // (rows + 2)
    size = rows * chan
    acc_ref[...] = jnp.zeros_like(acc_ref)

    def pair(q, carry):
        two = jnp.concatenate([frame_ref[2 * q], frame_ref[2 * q + 1]], axis=1)
        part = dot(weights, two)
        for j in range(3):
            move = 1 - j if forward else j - 1
            for side in range(2):
                acc_ref[2 * q + side + move + 1] += part[
                    j * size : (j + 1) * size, side * lanes : (side + 1) * lanes
                ]
        return carry

    lax.fori_loop(0, width // 2, pair, 0, unroll=width <= 16)


def conv_kernel(blocks, x_ref, near_ref, far_ref, w_ref, *refs):
    *wires, frame_ref, acc_s, held_s = refs
    rows, width, chan, views = x_ref.shape
    own = rows * chan
    lanes = frame_ref.shape[2]
    odd = row_is_odd() > 0
    frame_ref[...] = jnp.zeros_like(frame_ref)

    def fill(w, carry):
        near, far = near_ref[w], far_ref[w]
        frame_ref[w, :chan, :views] = jnp.where(odd, near, far)
        for r in range(rows):
            frame_ref[w, (r + 1) * chan : (r + 2) * chan, :views] = x_ref[r, w]
        frame_ref[w, chan + own :, :views] = jnp.where(odd, far, near)
        return carry

    lax.fori_loop(0, width, fill, 0, unroll=width <= 16)
    weights = taps(w_ref, rows, True)
    spread(frame_ref, acc_s, weights, rows, True)
    breadth = width // blocks

    def block(b, carry):
        cells = []
        for r in range(rows):
            for k in range(breadth):
                w = b * breadth + k
                value = acc_s[w + 1, r * chan : (r + 1) * chan]
                value = value + frame_ref[w, (r + 1) * chan : (r + 2) * chan].astype(F32)
                cells.append(value[:, :views])
        cells = jnp.concatenate(cells, axis=1)
        held_s[b, :, : cells.shape[1]] = cells
        return carry

    lax.fori_loop(0, blocks, block, 0, unroll=blocks <= 4)
    give(wires, held_s)


def convolve(x, near, far, w_conv, blocks):
    rows, width, chan, views = x.shape
    own = rows * chan
    lanes = round_up(views, 128)
    wire = round_up(rows * (width // blocks) * views, 128)
    vmem = pl.BlockSpec(memory_space=pltpu.VMEM)
    shapes = wire_shapes(blocks, chan, wire)
    shapes = shapes + [held(blocks, (width, own + 2 * chan, lanes), BF16)]
    *wires, frame = pl.pallas_call(
        functools.partial(conv_kernel, blocks),
        out_shape=shapes,
        in_specs=[vmem] * 4,
        out_specs=[vmem] * len(shapes),
        scratch_shapes=[
            pltpu.VMEM((width + 2, own, lanes), F32),
            pltpu.VMEM((blocks, chan, wire), F32),
        ],
        name="conv",
        compiler_params=grant(blocks),
    )(*here(blocks, x, near, far), w_conv)
    return wires, frame


def weight_kernel(count, pieces, *refs):
    wires = refs[:pieces]
    frame_ref, g_ref, gain_ref = refs[pieces : pieces + 3]
    near_ref, far_ref, own_ref, *part_refs, held_s, col_s, pack_s = refs[pieces + 3 :]
    width, own, lanes = own_ref.shape
    blocks, chan, wire = held_s.shape
    rows = own // chan
    breadth = width // blocks
    views = count
    odd = row_is_odd()
    take(wires, held_s)
    col_s[0] = jnp.zeros((own, lanes), BF16)
    col_s[width + 1] = jnp.zeros((own, lanes), BF16)

    def block(b, carry):
        cells = held_s[b]
        for r in range(rows):
            for k in range(breadth):
                at = (r * breadth + k) * views
                value = cells[:, at : at + views]
                if lanes > views:
                    value = jnp.concatenate(
                        [value, jnp.zeros((chan, lanes - views), F32)], axis=1
                    )
                col_s[b * breadth + k + 1, r * chan : (r + 1) * chan] = value.astype(BF16)
        return carry

    lax.fori_loop(0, blocks, block, 0, unroll=blocks <= 4)

    def copy(w, carry):
        cells = col_s[w + 1]
        own_ref[w] = cells
        first, last = cells[:chan], cells[own - chan :]
        near_ref[w] = jnp.where(odd > 0, first, last)
        far_ref[w] = jnp.where(odd > 0, last, first)
        return carry

    lax.fori_loop(0, width, copy, 0, unroll=width <= 16)

    def pair(q, total):
        left, right = [], []
        for side in range(2):
            w = 2 * q + side
            left.append(jnp.concatenate([col_s[w], col_s[w + 1], col_s[w + 2]], axis=0))
            right.append(frame_ref[w])
        return total + dot(
            jnp.concatenate(left, axis=1), jnp.concatenate(right, axis=1), (1, 1)
        )

    total = lax.fori_loop(
        0,
        width // 2,
        pair,
        jnp.zeros((3 * own, own + 2 * chan), F32),
        unroll=width <= 16,
    )
    bands = []
    for shift in range(3):
        band = 0.0
        for r in range(rows):
            top = (shift * rows + r) * chan
            band = band + total[top : top + chan, r * chan : (r + 3) * chan]
        bands.append(band)
    g_conv = jnp.concatenate(bands, axis=0)
    edge = 2 * chan
    pack_s[...] = jnp.zeros_like(pack_s)
    pack_s[: 2 * chan] = g_ref[...]
    pack_s[2 * chan : 2 * chan + 8] = gain_ref[...]
    at = 2 * chan + 8
    pack_s[at : at + 3 * chan] = g_conv[:, :edge]
    half = 3 * chan // 2
    rest = g_conv[:, edge:]
    pack_s[at + 3 * chan : at + 3 * chan + half] = jnp.concatenate(
        [rest[:half], rest[half:]], axis=1
    )
    size = part_refs[0].shape[0]
    for step, ref in enumerate(part_refs):
        turn = lax.axis_index("row") ^ step if len(part_refs) > 1 else 0
        ref[...] = pack_s[pl.ds(pl.multiple_of(turn * size, 16), size)].astype(ref.dtype)


def weight_grads(wires, frame, g_weights, g_gain, views, blocks):
    width, deep, lanes = frame.shape
    chan, wire = wires[0].shape[-2:]
    own = deep - 2 * chan
    count = lax.axis_size("row")
    parts = count if pairwise(count) else 1
    size = round_up(2 * chan + 8 + 9 * chan // 2, 16 * parts) // parts
    vmem = pl.BlockSpec(memory_space=pltpu.VMEM)
    return pl.pallas_call(
        functools.partial(weight_kernel, views, len(wires)),
        out_shape=(
            held(blocks, (width, chan, lanes), BF16),
            held(blocks, (width, chan, lanes), BF16),
            held(blocks, (width, own, lanes), BF16),
        )
        + (held(blocks, (size, 2 * chan), BF16 if parts > 1 else F32),) * parts,
        in_specs=[vmem] * (len(wires) + 3),
        out_specs=(vmem,) * (3 + parts),
        scratch_shapes=[
            pltpu.VMEM((blocks, chan, wire), F32),
            pltpu.VMEM((width + 2, own, lanes), BF16),
            pltpu.VMEM((parts * size, 2 * chan), F32),
        ],
        name="weights",
        compiler_params=grant(blocks),
    )(*here(blocks, *wires, frame, g_weights, g_gain))


def input_kernel(own_ref, near_ref, far_ref, w_ref, out_ref, frame_s, acc_s):
    width, own, lanes = own_ref.shape
    chan = near_ref.shape[1]
    rows = own // chan
    views = out_ref.shape[3]
    odd = row_is_odd() > 0

    def fill(w, carry):
        near, far = near_ref[w], far_ref[w]
        frame_s[w, :chan] = jnp.where(odd, near, far)
        frame_s[w, chan : chan + own] = own_ref[w]
        frame_s[w, chan + own :] = jnp.where(odd, far, near)
        return carry

    lax.fori_loop(0, width, fill, 0, unroll=width <= 16)
    spread(frame_s, acc_s, taps(w_ref, rows, False), rows, False)

    def columns(q, carry):
        at = pl.multiple_of(16 * q, 16)
        cells = []
        for k in range(16):
            cells.append(acc_s[at + k + 1] + own_ref[at + k].astype(F32))
        cells = jnp.swapaxes(jnp.stack(cells), 0, 1).astype(BF16)
        for r in range(rows):
            out_ref[:, r, pl.ds(at, 16), :] = cells[r * chan : (r + 1) * chan, :, :views]
        return carry

    lax.fori_loop(0, width // 16, columns, 0)


def input_grad(own, near, far, w_conv, views, blocks):
    width, size, lanes = own.shape
    chan = near.shape[1]
    vmem = pl.BlockSpec(memory_space=pltpu.VMEM)
    return pl.pallas_call(
        input_kernel,
        out_shape=jax.ShapeDtypeStruct((chan, size // chan, width, views), BF16),
        in_specs=[vmem] * 4,
        out_specs=vmem,
        scratch_shapes=[
            pltpu.VMEM((width, size + 2 * chan, lanes), BF16),
            pltpu.VMEM((width + 2, size, lanes), F32),
        ],
        name="input",
        compiler_params=grant(blocks),
    )(*here(blocks, own, near, far), w_conv)


def unpack_kernel(parts, *refs):
    conv_ref, q_ref, k_ref, v_ref, o_ref, gain_ref, pack_s = refs[parts:]
    size = refs[0].shape[0]
    chan = q_ref.shape[0]
    for step in range(parts):
        turn = lax.axis_index("row") ^ step if parts > 1 else 0
        pack_s[pl.ds(pl.multiple_of(turn * size, 16), size)] = refs[step][...].astype(F32)
    k_ref[...] = pack_s[:chan, :chan]
    v_ref[...] = pack_s[:chan, chan:]
    q_ref[...] = pack_s[chan : 2 * chan, :chan]
    o_ref[...] = pack_s[chan : 2 * chan, chan:]
    gain_ref[...] = pack_s[2 * chan : 2 * chan + 1, :chan]
    at = 2 * chan + 8
    half = 3 * chan // 2
    for j in range(3):
        top = (2 - j) * chan
        for i in range(2):
            conv_ref[i, j] = pack_s[at + top : at + top + chan, i * chan : (i + 1) * chan]
        for low in range(0, chan, chan // 2):
            row = top + low
            side = row // half
            start = at + 3 * chan + row - side * half
            conv_ref[2, j, low : low + chan // 2] = pack_s[
                start : start + chan // 2, side * chan : (side + 1) * chan
            ]


def unpack(parts, chan, blocks):
    vmem = pl.BlockSpec(memory_space=pltpu.VMEM)
    square = jax.ShapeDtypeStruct((chan, chan), F32)
    return pl.pallas_call(
        functools.partial(unpack_kernel, len(parts)),
        out_shape=(
            jax.ShapeDtypeStruct((3, 3, chan, chan), F32),
            square,
            square,
            square,
            square,
            jax.ShapeDtypeStruct((1, chan), F32),
        ),
        in_specs=[vmem] * len(parts),
        out_specs=(vmem,) * 6,
        scratch_shapes=[pltpu.VMEM((len(parts) * parts[0].shape[0], 2 * chan), F32)],
        name="unpack",
        compiler_params=grant(blocks),
    )(*here(blocks, *parts))


def angular_kernel(
    scale,
    lag,
    pieces,
    *refs,
):
    wires_in = refs[:pieces]
    cot_ref, keep_ref, gain_row, wq_ref, wkey_ref, wv_ref, wo_ref = refs[pieces : pieces + 7]
    refs = refs[pieces + 7 :]
    wires_out = refs[:pieces]
    out_ref, g_ref, ggain_ref = refs[pieces : pieces + 3]
    refs = refs[pieces + 3 :]
    held_s, give_s, bias_ref, gain_ref, wqkv_ref, wkv_ref, wot_ref, wkv2_ref, gain_s = refs[:9]
    scratch = refs[9:]
    blocks = held_s.shape[0]
    pixels, chan, lanes = cot_ref.shape
    used = keep_ref.shape[1]
    each = used // blocks
    rows = bias_ref.shape[0]
    per = 7
    slots = len(scratch) // per
    inv_chan = 1.0 / chan
    take(wires_in, held_s)
    live = jnp.where(keep_ref[...] > 0, 0.0, -1e30).astype(F32)
    live = jnp.concatenate([live, jnp.full((1, lanes - used), -1e30, F32)], axis=1)
    live = jnp.transpose(jnp.broadcast_to(live, (128, lanes)))[:rows]
    lane = lax.broadcasted_iota(jnp.int32, (rows, 128), 1)
    bias_ref[...] = jnp.where(lane == chan, live, 0.0)[:, : 2 * chan]
    eye = lax.broadcasted_iota(jnp.int32, (chan, chan), 0) == lax.broadcasted_iota(
        jnp.int32, (chan, chan), 1
    )
    gain_ref[...] = jnp.sum(jnp.where(eye, gain_row[...], 0.0), axis=1, keepdims=True)
    w_q, w_k, w_v = (ref[...].astype(F32) for ref in (wq_ref, wkey_ref, wv_ref))
    wqkv_ref[...] = jnp.concatenate(
        [jnp.transpose(w_q), jnp.transpose(w_k), jnp.transpose(w_v)], axis=0
    ).astype(BF16)
    blank = jnp.zeros((chan, chan), F32)
    wkv_ref[...] = jnp.concatenate([w_k, blank, w_v, blank], axis=1).astype(BF16)
    wkv2_ref[...] = jnp.concatenate([w_k, w_v], axis=1).astype(BF16)
    wot_ref[...] = jnp.transpose(wo_ref[...].astype(F32)).astype(BF16)
    g_ref[...] = jnp.zeros_like(g_ref)
    gain_s[...] = jnp.zeros_like(gain_s)
    for slot in range(slots):
        d_s = scratch[per * slot + 5]
        d_s[rows:] = jnp.zeros((lanes - rows, 2 * chan), BF16)
    chunks = []
    at = 0
    while at < rows:
        size = min(80, rows - at)
        chunks.append((at, size))
        at += size
    half_lane = lax.broadcasted_iota(jnp.int32, (chan, 2 * chan), 1) < chan

    def pixel(p):
        start = per * (p % slots)
        s_s, e_s, n_s, x_s, kv_s, d_s, nb_s = scratch[start : start + per]
        cells = [held_s[b, :, p * each : (p + 1) * each] for b in range(blocks)]
        if lanes > used:
            cells.append(jnp.zeros((chan, lanes - used), held_s.dtype))
        s = jnp.concatenate(cells, axis=1).astype(F32)
        x_s[...] = s
        cen = s - jnp.sum(s, axis=0, keepdims=True) * inv_chan
        rstd = lax.rsqrt(jnp.sum(cen * cen, axis=0, keepdims=True) * inv_chan + 1e-05)
        normed = cen * rstd
        n_s[...] = normed
        nin32 = normed * gain_ref[...]
        nin = nin32.astype(BF16)
        nb_s[...] = nin
        nin_t = jnp.transpose(nin32)[:rows].astype(BF16)
        yield
        kv = dot(nin_t, wkv_ref[...])
        kv_s[:, : 2 * chan] = (kv[:, : 2 * chan] + bias_ref[...]).astype(BF16)
        kv_s[:, 2 * chan :] = kv[:, 2 * chan :].astype(BF16)
        yield
        qkv = dot(wqkv_ref[...], nin)
        q = (qkv[:chan].astype(BF16).astype(F32) * scale).astype(BF16)
        k = qkv[chan : 2 * chan, :rows].astype(BF16)
        v = qkv[2 * chan :, :rows].astype(BF16)
        zero = jnp.zeros((chan, lanes), BF16)
        q_aug = jnp.concatenate([q, jnp.ones((16, lanes), BF16), zero[16:]], axis=0)
        yield
        s_s[...] = dot(kv_s[:, : 2 * chan], q_aug)
        yield
        high = None
        for at, size in chunks:
            top = jnp.max(s_s[at : at + size].reshape(size // 8, 8, lanes), axis=0)
            high = top if high is None else jnp.maximum(high, top)
        high = jnp.max(high, axis=0, keepdims=True)
        yield
        for at, size in chunks:
            e_s[at : at + size, :lanes] = jnp.exp(s_s[at : at + size] - high).astype(BF16)
            yield
        v_aug = jnp.concatenate([v, jnp.ones((16, rows), BF16)], axis=0)
        att_aug = dot(v_aug, e_s[:, :lanes])
        yield
        cot = cot_ref[p]
        d_att32 = dot(wo_ref[...], cot).astype(BF16).astype(F32)
        inv = 1.0 / att_aug[chan : chan + 1]
        att = att_aug[:chan] * inv
        att_b = att.astype(BF16)
        d_att = (d_att32 * inv).astype(BF16)
        inner = jnp.sum(att * d_att.astype(F32), axis=0, keepdims=True)
        yield
        d_aug = jnp.concatenate([d_att, zero], axis=0)
        s_s[...] = dot(kv_s[:, 2 * chan :], d_aug)
        yield
        for at, size in chunks:
            e_s[at : at + size, lanes:] = e_s[at : at + size, :lanes] * (s_s[at : at + size] - inner).astype(BF16)
            yield
        low = jnp.concatenate(
            [jnp.concatenate([zero, d_att], axis=0), jnp.concatenate([q, zero], axis=0)], axis=1
        )
        d_s[:rows] = dot(e_s[...], low, (1, 1)).astype(BF16)
        yield
        d_q = (dot(k, e_s[:, lanes:]) * scale).astype(BF16)
        yield
        out_ref[p] = (x_s[...] + dot(wot_ref[...], att_b)).astype(BF16)[:, :used]
        yield
        dn = dot(wq_ref[...], d_q) + dot(wkv2_ref[...], d_s[...], (1, 1))
        nin = nb_s[...]
        g_ref[:chan] += dot(nin, d_s[...])
        both = dot(
            jnp.concatenate([nin, att_b], axis=0), jnp.concatenate([d_q, cot], axis=0), (1, 1)
        )
        g_ref[chan:] += jnp.where(half_lane, both[:chan], both[chan:])
        yield
        normed = n_s[...]
        dnn = dn * normed
        gain_s[...] += dnn
        scaled = dn * gain_ref[...]
        back = (
            scaled
            - jnp.sum(scaled, axis=0, keepdims=True) * inv_chan
            - normed * (jnp.sum(dnn * gain_ref[...], axis=0, keepdims=True) * inv_chan)
        )
        done = (cot.astype(F32) + back * rstd).astype(give_s.dtype)
        for b in range(blocks):
            give_s[b, :, p * each : (p + 1) * each] = done[:, b * each : (b + 1) * each]
        yield

    waiting = [pixel(p) for p in range(pixels)]
    active = []
    step = 0
    while waiting or active:
        if waiting and step % lag == 0:
            active += waiting[:2]
            waiting = waiting[2:]
        for run in list(active):
            try:
                next(run)
            except StopIteration:
                active.remove(run)
        step += 1
    g_gain = jnp.sum(gain_s[...], axis=1, keepdims=True)
    g_gain = jnp.sum(jnp.where(eye, g_gain, 0.0), axis=0, keepdims=True)
    g_gain = jnp.concatenate([g_gain, jnp.zeros((1, chan), F32)], axis=1)
    ggain_ref[...] = jnp.broadcast_to(g_gain, ggain_ref.shape)
    give(wires_out, give_s)


def angular(wires, cotangent, keep, gain, w_query, w_key, w_value, w_out, blocks):
    pixels, chan, lanes = cotangent.shape
    used = keep.shape[0]
    rows = round_up(used, 16)
    wire = wires[0].shape[-1]
    vmem = pl.BlockSpec(memory_space=pltpu.VMEM)
    scale = 1.0 / math.sqrt(chan)
    shapes = wire_shapes(blocks, chan, wire) + [
        jax.ShapeDtypeStruct((pixels, chan, used), BF16),
        held(blocks, (2 * chan, 2 * chan), F32),
        held(blocks, (8, 2 * chan), F32),
    ]
    *out, output, g_weights, g_gain = pl.pallas_call(
        functools.partial(angular_kernel, scale, 8, len(wires)),
        out_shape=shapes,
        in_specs=[vmem] * (len(wires) + 7),
        out_specs=[vmem] * len(shapes),
        scratch_shapes=[
            pltpu.VMEM((blocks, chan, wire), BF16),
            pltpu.VMEM((blocks, chan, wire), BF16),
            pltpu.VMEM((rows, 2 * chan), F32),
            pltpu.VMEM((chan, 1), F32),
            pltpu.VMEM((3 * chan, chan), BF16),
            pltpu.VMEM((chan, 4 * chan), BF16),
            pltpu.VMEM((chan, chan), BF16),
            pltpu.VMEM((chan, 2 * chan), BF16),
            pltpu.VMEM((chan, lanes), F32),
        ]
        + [
            pltpu.VMEM((rows, lanes), F32),
            pltpu.VMEM((rows, 2 * lanes), BF16),
            pltpu.VMEM((chan, lanes), F32),
            pltpu.VMEM((chan, lanes), F32),
            pltpu.VMEM((rows, 4 * chan), BF16),
            pltpu.VMEM((lanes, 2 * chan), BF16),
            pltpu.VMEM((chan, lanes), BF16),
        ]
        * 6,
        name="angular",
        compiler_params=grant(blocks),
    )(*here(blocks, *wires, cotangent), keep[None, :], gain[None, :], w_query, w_key, w_value, w_out)
    return out, output, g_weights, g_gain


def sum_parts(parts):
    total = parts[0].astype(F32)
    for part in parts[1:]:
        total = total + part.astype(F32)
    return total


def reduce_views(own):
    count = lax.axis_size("view")
    if not pairwise(count):
        return lax.psum(own, "view")
    own = own.astype(BF16)
    parts = [swap(own, "view", step) for step in range(1, count)]
    return sum_parts([own] + parts).astype(BF16)


def scatter_rows(parts):
    if len(parts) == 1:
        return lax.psum(parts[0], "row")
    return sum_parts(
        [parts[0]] + [swap(parts[step], "row", step) for step in range(1, len(parts))]
    )


def gather_rows(own, count):
    if count == 1:
        return [own]
    return [own] + [swap(own, "row", step) for step in range(1, count)]


def body(inputs, cotangent, keep, w_conv, gain, w_query, w_key, w_value, w_out):
    chan, view_dev, row_dev, width = inputs.shape
    blocks = lax.axis_size("view")
    breadth = width // blocks
    views = view_dev * blocks
    lanes = round_up(views, 128)
    pixels = row_dev * breadth
    odd = row_is_odd() > 0
    x = jnp.transpose(inputs, (2, 3, 0, 1))
    first, last = x[0], x[row_dev - 1]
    near, far = halo_swap(jnp.where(odd, first, last), jnp.where(odd, last, first))
    w_conv = jnp.transpose(w_conv, (2, 3, 0, 1))
    wires, frame = convolve(x, near, far, w_conv, blocks)
    wires = exchange(wires)
    cot = jnp.transpose(cotangent, (2, 3, 0, 1)).reshape(pixels, chan, views)
    cot = jnp.pad(cot, ((0, 0), (0, 0), (0, lanes - views)))
    wires, output, g_weights, g_gain = angular(
        wires, cot, keep, gain, w_query, w_key, w_value, w_out, blocks
    )
    output = jnp.transpose(output.reshape(row_dev, breadth, chan, views), (2, 3, 0, 1))
    wires, output = lax.optimization_barrier((exchange(wires), output))
    near, far, own, *parts = weight_grads(wires, frame, g_weights, g_gain, view_dev, blocks)
    part = scatter_rows(parts)
    near, far = halo_swap(near, far)
    part, near, far = lax.optimization_barrier((reduce_views(part), near, far))
    parts = gather_rows(part, len(parts))
    d_input = input_grad(own, near, far, w_conv, view_dev, blocks)
    parts, d_input = lax.optimization_barrier((parts, d_input))
    g_conv, g_query, g_key, g_value, g_out, g_gain = unpack(parts, chan, blocks)
    d_input = jnp.transpose(d_input, (0, 3, 1, 2))
    g_conv = jnp.transpose(g_conv, (2, 3, 0, 1))
    return (output, d_input, g_conv, g_gain[0], g_query, g_key, g_value, g_out)


def solution(mesh):
    placed = (
        P(None, "view", ("groups", "row"), None),
        P(None, None, ("groups", "row"), "view"),
        P("groups"),
        P(),
        P(),
        P(),
        P(),
        P(),
        P(),
    )
    return jax.shard_map(
        body,
        mesh=mesh,
        in_specs=placed,
        out_specs=(
            P(None, None, ("groups", "row"), "view"),
            P(None, "view", ("groups", "row"), None),
            P("groups", None, None, None),
            P("groups"),
            P("groups", None),
            P("groups", None),
            P("groups", None),
            P("groups", None),
        ),
        check_vma=False,
    )
```

```python
import functools
import math

import jax
import jax.numpy as jnp
from jax import lax
from jax.experimental import pallas as pl
from jax.experimental.pallas import tpu as pltpu
from jax.sharding import PartitionSpec as P

F32 = jnp.float32
BF16 = jnp.bfloat16


def round_up(value, unit):
    return -(-value // unit) * unit


def dot(left, right, contract=(1, 0)):
    return lax.dot_general(
        left, right, (((contract[0],), (contract[1],)), ((), ())), preferred_element_type=F32
    )


def pairwise(count):
    return count <= 8 and count & (count - 1) == 0


def swap(cells, axis, step):
    count = lax.axis_size(axis)
    return lax.ppermute(cells, axis, [(i, i ^ step) for i in range(count)])


def halo_swap(near, far):
    count = lax.axis_size("row")
    pairs = []
    for i in range(1, count - 1, 2):
        pairs += [(i, i + 1), (i + 1, i)]
    got_near = lax.ppermute(near, "row", [(i, i ^ 1) for i in range(count)])
    got_far = lax.ppermute(far, "row", pairs) if pairs else jnp.zeros_like(far)
    return got_near, got_far


def row_is_odd():
    return lax.rem(lax.axis_index("row"), 2)


def give(refs, held):
    if len(refs) == 1:
        refs[0][...] = held[...].astype(refs[0].dtype)
        return
    me = lax.axis_index("view")
    for step, ref in enumerate(refs):
        ref[...] = held[me ^ step].astype(ref.dtype)


def take(refs, held):
    if len(refs) == 1:
        held[...] = refs[0][...].astype(held.dtype)
        return
    me = lax.axis_index("view")
    for step, ref in enumerate(refs):
        held[me ^ step] = ref[...].astype(held.dtype)


def here(blocks, *arrays):
    if not pairwise(blocks):
        return arrays
    return [pltpu.with_memory_space_constraint(array, pltpu.VMEM) for array in arrays]


def grant(blocks):
    return pltpu.CompilerParams(vmem_limit_bytes=(24 << 20) if pairwise(blocks) else None)


def held(blocks, shape, dtype):
    return (pltpu.VMEM if pairwise(blocks) else jax.ShapeDtypeStruct)(shape, dtype)


def wire_shapes(blocks, chan, lanes):
    if pairwise(blocks):
        return [held(blocks, (chan, lanes), BF16)] * blocks
    return [held(blocks, (blocks, chan, lanes), BF16)]


def exchange(wires):
    if len(wires) == 1:
        return [lax.all_to_all(wires[0], "view", split_axis=0, concat_axis=0, tiled=True)]
    return [wires[0]] + [swap(wires[step], "view", step) for step in range(1, len(wires))]


def taps(w_ref, rows, forward):
    chan = w_ref.shape[2]
    blank = jnp.zeros((chan, chan), F32)
    found = {}
    for i in range(3):
        for j in range(3):
            tap = w_ref[i, j].astype(F32)
            found[i, j] = tap if forward else jnp.transpose(tap)
    bands = []
    for j in range(3):
        for r in range(rows):
            row = []
            for place in range(rows + 2):
                i = place - r if forward else r + 2 - place
                row.append(found[i, j] if 0 <= i < 3 else blank)
            bands.append(jnp.concatenate(row, axis=1))
    return jnp.concatenate(bands, axis=0).astype(BF16)


def spread(frame_ref, acc_ref, weights, rows, forward):
    width, deep, lanes = frame_ref.shape
    chan = deep // (rows + 2)
    size = rows * chan
    acc_ref[...] = jnp.zeros_like(acc_ref)

    def pair(q, carry):
        two = jnp.concatenate([frame_ref[2 * q], frame_ref[2 * q + 1]], axis=1)
        part = dot(weights, two)
        for j in range(3):
            move = 1 - j if forward else j - 1
            for side in range(2):
                acc_ref[2 * q + side + move + 1] += part[
                    j * size : (j + 1) * size, side * lanes : (side + 1) * lanes
                ]
        return carry

    lax.fori_loop(0, width // 2, pair, 0, unroll=width <= 16)


def conv_kernel(blocks, x_ref, near_ref, far_ref, w_ref, *refs):
    *wires, frame_ref, acc_s, held_s = refs
    rows, width, chan, views = x_ref.shape
    own = rows * chan
    lanes = frame_ref.shape[2]
    odd = row_is_odd() > 0
    frame_ref[...] = jnp.zeros_like(frame_ref)

    def fill(w, carry):
        near, far = near_ref[w], far_ref[w]
        frame_ref[w, :chan, :views] = jnp.where(odd, near, far)
        for r in range(rows):
            frame_ref[w, (r + 1) * chan : (r + 2) * chan, :views] = x_ref[r, w]
        frame_ref[w, chan + own :, :views] = jnp.where(odd, far, near)
        return carry

    lax.fori_loop(0, width, fill, 0, unroll=width <= 16)
    weights = taps(w_ref, rows, True)
    spread(frame_ref, acc_s, weights, rows, True)
    breadth = width // blocks

    def block(b, carry):
        cells = []
        for r in range(rows):
            for k in range(breadth):
                w = b * breadth + k
                value = acc_s[w + 1, r * chan : (r + 1) * chan]
                value = value + frame_ref[w, (r + 1) * chan : (r + 2) * chan].astype(F32)
                cells.append(value[:, :views])
        cells = jnp.concatenate(cells, axis=1)
        held_s[b, :, : cells.shape[1]] = cells
        return carry

    lax.fori_loop(0, blocks, block, 0, unroll=blocks <= 4)
    give(wires, held_s)


def convolve(x, near, far, w_conv, blocks):
    rows, width, chan, views = x.shape
    own = rows * chan
    lanes = round_up(views, 128)
    wire = round_up(rows * (width // blocks) * views, 128)
    vmem = pl.BlockSpec(memory_space=pltpu.VMEM)
    shapes = wire_shapes(blocks, chan, wire)
    shapes = shapes + [held(blocks, (width, own + 2 * chan, lanes), BF16)]
    *wires, frame = pl.pallas_call(
        functools.partial(conv_kernel, blocks),
        out_shape=shapes,
        in_specs=[vmem] * 4,
        out_specs=[vmem] * len(shapes),
        scratch_shapes=[
            pltpu.VMEM((width + 2, own, lanes), F32),
            pltpu.VMEM((blocks, chan, wire), F32),
        ],
        name="conv",
        compiler_params=grant(blocks),
    )(*here(blocks, x, near, far), w_conv)
    return wires, frame


def weight_kernel(count, pieces, *refs):
    wires = refs[:pieces][::-1]
    frame_ref, g_ref, gain_ref = refs[pieces : pieces + 3]
    near_ref, far_ref, own_ref, *part_refs, held_s, col_s, pack_s = refs[pieces + 3 :]
    width, own, lanes = own_ref.shape
    blocks, chan, wire = held_s.shape
    rows = own // chan
    breadth = width // blocks
    views = count
    odd = row_is_odd()
    take(wires, held_s)
    col_s[0] = jnp.zeros((own, lanes), BF16)
    col_s[width + 1] = jnp.zeros((own, lanes), BF16)

    def block(b, carry):
        cells = held_s[b]
        for r in range(rows):
            for k in range(breadth):
                at = (r * breadth + k) * views
                value = cells[:, at : at + views]
                if lanes > views:
                    value = jnp.concatenate(
                        [value, jnp.zeros((chan, lanes - views), F32)], axis=1
                    )
                col_s[b * breadth + k + 1, r * chan : (r + 1) * chan] = value.astype(BF16)
        return carry

    lax.fori_loop(0, blocks, block, 0, unroll=blocks <= 4)

    def copy(w, carry):
        cells = col_s[w + 1]
        own_ref[w] = cells
        first, last = cells[:chan], cells[own - chan :]
        near_ref[w] = jnp.where(odd > 0, first, last)
        far_ref[w] = jnp.where(odd > 0, last, first)
        return carry

    lax.fori_loop(0, width, copy, 0, unroll=width <= 16)

    def pair(q, total):
        left, right = [], []
        for side in range(2):
            w = 2 * q + side
            left.append(jnp.concatenate([col_s[w], col_s[w + 1], col_s[w + 2]], axis=0))
            right.append(frame_ref[w])
        return total + dot(
            jnp.concatenate(left, axis=1), jnp.concatenate(right, axis=1), (1, 1)
        )

    total = lax.fori_loop(
        0,
        width // 2,
        pair,
        jnp.zeros((3 * own, own + 2 * chan), F32),
        unroll=width <= 16,
    )
    bands = []
    for shift in range(3):
        band = 0.0
        for r in range(rows):
            top = (shift * rows + r) * chan
            band = band + total[top : top + chan, r * chan : (r + 3) * chan]
        bands.append(band)
    g_conv = jnp.concatenate(bands, axis=0)
    edge = 2 * chan
    pack_s[...] = jnp.zeros_like(pack_s)
    pack_s[: 2 * chan] = g_ref[...]
    pack_s[2 * chan : 2 * chan + 8] = gain_ref[...]
    at = 2 * chan + 8
    pack_s[at : at + 3 * chan] = g_conv[:, :edge]
    half = 3 * chan // 2
    rest = g_conv[:, edge:]
    pack_s[at + 3 * chan : at + 3 * chan + half] = jnp.concatenate(
        [rest[:half], rest[half:]], axis=1
    )
    size = part_refs[0].shape[0]
    for step, ref in enumerate(part_refs):
        turn = lax.axis_index("row") ^ step if len(part_refs) > 1 else 0
        ref[...] = pack_s[pl.ds(pl.multiple_of(turn * size, 16), size)].astype(ref.dtype)


def weight_grads(wires, frame, g_weights, g_gain, views, blocks):
    width, deep, lanes = frame.shape
    chan, wire = wires[0].shape[-2:]
    own = deep - 2 * chan
    count = lax.axis_size("row")
    parts = count if pairwise(count) else 1
    size = round_up(2 * chan + 8 + 9 * chan // 2, 16 * parts) // parts
    vmem = pl.BlockSpec(memory_space=pltpu.VMEM)
    return pl.pallas_call(
        functools.partial(weight_kernel, views, len(wires)),
        out_shape=(
            held(blocks, (width, chan, lanes), BF16),
            held(blocks, (width, chan, lanes), BF16),
            held(blocks, (width, own, lanes), BF16),
        )
        + (held(blocks, (size, 2 * chan), BF16 if parts > 1 else F32),) * parts,
        in_specs=[vmem] * (len(wires) + 3),
        out_specs=(vmem,) * (3 + parts),
        scratch_shapes=[
            pltpu.VMEM((blocks, chan, wire), F32),
            pltpu.VMEM((width + 2, own, lanes), BF16),
            pltpu.VMEM((parts * size, 2 * chan), F32),
        ],
        name="weights",
        compiler_params=grant(blocks),
    )(*here(blocks, *wires[::-1], frame, g_weights, g_gain))


def input_kernel(own_ref, near_ref, far_ref, w_ref, out_ref, frame_s, acc_s):
    width, own, lanes = own_ref.shape
    chan = near_ref.shape[1]
    rows = own // chan
    views = out_ref.shape[3]
    odd = row_is_odd() > 0

    def fill(w, carry):
        near, far = near_ref[w], far_ref[w]
        frame_s[w, :chan] = jnp.where(odd, near, far)
        frame_s[w, chan : chan + own] = own_ref[w]
        frame_s[w, chan + own :] = jnp.where(odd, far, near)
        return carry

    lax.fori_loop(0, width, fill, 0, unroll=width <= 16)
    spread(frame_s, acc_s, taps(w_ref, rows, False), rows, False)

    def columns(q, carry):
        at = pl.multiple_of(16 * q, 16)
        cells = []
        for k in range(16):
            cells.append(acc_s[at + k + 1] + own_ref[at + k].astype(F32))
        cells = jnp.swapaxes(jnp.stack(cells), 0, 1).astype(BF16)
        for r in range(rows):
            out_ref[:, r, pl.ds(at, 16), :] = cells[r * chan : (r + 1) * chan, :, :views]
        return carry

    lax.fori_loop(0, width // 16, columns, 0)


def input_grad(own, near, far, w_conv, views, blocks):
    width, size, lanes = own.shape
    chan = near.shape[1]
    vmem = pl.BlockSpec(memory_space=pltpu.VMEM)
    return pl.pallas_call(
        input_kernel,
        out_shape=jax.ShapeDtypeStruct((chan, size // chan, width, views), BF16),
        in_specs=[vmem] * 4,
        out_specs=vmem,
        scratch_shapes=[
            pltpu.VMEM((width, size + 2 * chan, lanes), BF16),
            pltpu.VMEM((width + 2, size, lanes), F32),
        ],
        name="input",
        compiler_params=grant(blocks),
    )(*here(blocks, own, near, far), w_conv)


def unpack_kernel(parts, *refs):
    conv_ref, q_ref, k_ref, v_ref, o_ref, gain_ref, pack_s = refs[parts:]
    size = refs[0].shape[0]
    chan = q_ref.shape[0]
    for step in range(parts):
        turn = lax.axis_index("row") ^ step if parts > 1 else 0
        pack_s[pl.ds(pl.multiple_of(turn * size, 16), size)] = refs[step][...].astype(F32)
    k_ref[...] = pack_s[:chan, :chan]
    v_ref[...] = pack_s[:chan, chan:]
    q_ref[...] = pack_s[chan : 2 * chan, :chan]
    o_ref[...] = pack_s[chan : 2 * chan, chan:]
    gain_ref[...] = pack_s[2 * chan : 2 * chan + 1, :chan]
    at = 2 * chan + 8
    half = 3 * chan // 2
    for j in range(3):
        top = (2 - j) * chan
        for i in range(2):
            conv_ref[i, j] = pack_s[at + top : at + top + chan, i * chan : (i + 1) * chan]
        for low in range(0, chan, chan // 2):
            row = top + low
            side = row // half
            start = at + 3 * chan + row - side * half
            conv_ref[2, j, low : low + chan // 2] = pack_s[
                start : start + chan // 2, side * chan : (side + 1) * chan
            ]


def unpack(parts, chan, blocks):
    vmem = pl.BlockSpec(memory_space=pltpu.VMEM)
    square = jax.ShapeDtypeStruct((chan, chan), F32)
    return pl.pallas_call(
        functools.partial(unpack_kernel, len(parts)),
        out_shape=(
            jax.ShapeDtypeStruct((3, 3, chan, chan), F32),
            square,
            square,
            square,
            square,
            jax.ShapeDtypeStruct((1, chan), F32),
        ),
        in_specs=[vmem] * len(parts),
        out_specs=(vmem,) * 6,
        scratch_shapes=[pltpu.VMEM((len(parts) * parts[0].shape[0], 2 * chan), F32)],
        name="unpack",
        compiler_params=grant(blocks),
    )(*here(blocks, *parts))


def angular_kernel(
    scale,
    lag,
    pieces,
    *refs,
):
    wires_in = refs[:pieces][::-1]
    cot_ref, keep_ref, gain_row, wq_ref, wkey_ref, wv_ref, wo_ref = refs[pieces : pieces + 7]
    refs = refs[pieces + 7 :]
    wires_out = refs[:pieces]
    out_ref, g_ref, ggain_ref = refs[pieces : pieces + 3]
    refs = refs[pieces + 3 :]
    held_s, give_s, bias_ref, gain_ref, wqkv_ref, wkv_ref, wot_ref, wkv2_ref, gain_s = refs[:9]
    scratch = refs[9:]
    blocks = held_s.shape[0]
    pixels, chan, lanes = cot_ref.shape
    used = keep_ref.shape[1]
    each = used // blocks
    rows = bias_ref.shape[0]
    per = 7
    slots = len(scratch) // per
    inv_chan = 1.0 / chan
    take(wires_in, held_s)
    live = jnp.where(keep_ref[...] > 0, 0.0, -1e30).astype(F32)
    live = jnp.concatenate([live, jnp.full((1, lanes - used), -1e30, F32)], axis=1)
    live = jnp.transpose(jnp.broadcast_to(live, (128, lanes)))[:rows]
    lane = lax.broadcasted_iota(jnp.int32, (rows, 128), 1)
    bias_ref[...] = jnp.where(lane == chan, live, 0.0)[:, : 2 * chan]
    eye = lax.broadcasted_iota(jnp.int32, (chan, chan), 0) == lax.broadcasted_iota(
        jnp.int32, (chan, chan), 1
    )
    gain_ref[...] = jnp.sum(jnp.where(eye, gain_row[...], 0.0), axis=1, keepdims=True)
    w_q, w_k, w_v = (ref[...].astype(F32) for ref in (wq_ref, wkey_ref, wv_ref))
    wqkv_ref[...] = jnp.concatenate(
        [jnp.transpose(w_q), jnp.transpose(w_k), jnp.transpose(w_v)], axis=0
    ).astype(BF16)
    blank = jnp.zeros((chan, chan), F32)
    wkv_ref[...] = jnp.concatenate([w_k, blank, w_v, blank], axis=1).astype(BF16)
    wkv2_ref[...] = jnp.concatenate([w_k, w_v], axis=1).astype(BF16)
    wot_ref[...] = jnp.transpose(wo_ref[...].astype(F32)).astype(BF16)
    g_ref[...] = jnp.zeros_like(g_ref)
    gain_s[...] = jnp.zeros_like(gain_s)
    for slot in range(slots):
        d_s = scratch[per * slot + 5]
        d_s[rows:] = jnp.zeros((lanes - rows, 2 * chan), BF16)
    chunks = []
    at = 0
    while at < rows:
        size = min(80, rows - at)
        chunks.append((at, size))
        at += size
    half_lane = lax.broadcasted_iota(jnp.int32, (chan, 2 * chan), 1) < chan

    def pixel(p):
        start = per * (p % slots)
        s_s, e_s, n_s, x_s, kv_s, d_s, nb_s = scratch[start : start + per]
        cells = [held_s[b, :, p * each : (p + 1) * each] for b in range(blocks)]
        if lanes > used:
            cells.append(jnp.zeros((chan, lanes - used), held_s.dtype))
        s = jnp.concatenate(cells, axis=1).astype(F32)
        x_s[...] = s
        cen = s - jnp.sum(s, axis=0, keepdims=True) * inv_chan
        rstd = lax.rsqrt(jnp.sum(cen * cen, axis=0, keepdims=True) * inv_chan + 1e-05)
        normed = cen * rstd
        n_s[...] = normed
        nin32 = normed * gain_ref[...]
        nin = nin32.astype(BF16)
        nb_s[...] = nin
        nin_t = jnp.transpose(nin32)[:rows].astype(BF16)
        yield
        kv = dot(nin_t, wkv_ref[...])
        kv_s[:, : 2 * chan] = (kv[:, : 2 * chan] + bias_ref[...]).astype(BF16)
        kv_s[:, 2 * chan :] = kv[:, 2 * chan :].astype(BF16)
        yield
        qkv = dot(wqkv_ref[...], nin)
        q = (qkv[:chan].astype(BF16).astype(F32) * scale).astype(BF16)
        k = qkv[chan : 2 * chan, :rows].astype(BF16)
        v = qkv[2 * chan :, :rows].astype(BF16)
        zero = jnp.zeros((chan, lanes), BF16)
        q_aug = jnp.concatenate([q, jnp.ones((16, lanes), BF16), zero[16:]], axis=0)
        yield
        s_s[...] = dot(kv_s[:, : 2 * chan], q_aug)
        yield
        high = None
        for at, size in chunks:
            top = jnp.max(s_s[at : at + size].reshape(size // 8, 8, lanes), axis=0)
            high = top if high is None else jnp.maximum(high, top)
        high = jnp.max(high, axis=0, keepdims=True)
        yield
        for at, size in chunks:
            e_s[at : at + size, :lanes] = jnp.exp(s_s[at : at + size] - high).astype(BF16)
            yield
        v_aug = jnp.concatenate([v, jnp.ones((16, rows), BF16)], axis=0)
        att_aug = dot(v_aug, e_s[:, :lanes])
        yield
        cot = cot_ref[p]
        d_att32 = dot(wo_ref[...], cot).astype(BF16).astype(F32)
        inv = 1.0 / att_aug[chan : chan + 1]
        att = att_aug[:chan] * inv
        att_b = att.astype(BF16)
        d_att = (d_att32 * inv).astype(BF16)
        inner = jnp.sum(att * d_att.astype(F32), axis=0, keepdims=True)
        yield
        d_aug = jnp.concatenate([d_att, zero], axis=0)
        s_s[...] = dot(kv_s[:, 2 * chan :], d_aug)
        yield
        for at, size in chunks:
            e_s[at : at + size, lanes:] = e_s[at : at + size, :lanes] * (s_s[at : at + size] - inner).astype(BF16)
            yield
        low = jnp.concatenate(
            [jnp.concatenate([zero, d_att], axis=0), jnp.concatenate([q, zero], axis=0)], axis=1
        )
        d_s[:rows] = dot(e_s[...], low, (1, 1)).astype(BF16)
        yield
        d_q = (dot(k, e_s[:, lanes:]) * scale).astype(BF16)
        yield
        out_ref[p] = (x_s[...] + dot(wot_ref[...], att_b)).astype(BF16)[:, :used]
        yield
        dn = dot(wq_ref[...], d_q) + dot(wkv2_ref[...], d_s[...], (1, 1))
        nin = nb_s[...]
        g_ref[:chan] += dot(nin, d_s[...])
        both = dot(
            jnp.concatenate([nin, att_b], axis=0), jnp.concatenate([d_q, cot], axis=0), (1, 1)
        )
        g_ref[chan:] += jnp.where(half_lane, both[:chan], both[chan:])
        yield
        normed = n_s[...]
        dnn = dn * normed
        gain_s[...] += dnn
        scaled = dn * gain_ref[...]
        back = (
            scaled
            - jnp.sum(scaled, axis=0, keepdims=True) * inv_chan
            - normed * (jnp.sum(dnn * gain_ref[...], axis=0, keepdims=True) * inv_chan)
        )
        done = (cot.astype(F32) + back * rstd).astype(give_s.dtype)
        for b in range(blocks):
            give_s[b, :, p * each : (p + 1) * each] = done[:, b * each : (b + 1) * each]
        yield

    waiting = [pixel(p) for p in range(pixels)]
    active = []
    step = 0
    while waiting or active:
        if waiting and step % lag == 0:
            active += waiting[:2]
            waiting = waiting[2:]
        for run in list(active):
            try:
                next(run)
            except StopIteration:
                active.remove(run)
        step += 1
    g_gain = jnp.sum(gain_s[...], axis=1, keepdims=True)
    g_gain = jnp.sum(jnp.where(eye, g_gain, 0.0), axis=0, keepdims=True)
    g_gain = jnp.concatenate([g_gain, jnp.zeros((1, chan), F32)], axis=1)
    ggain_ref[...] = jnp.broadcast_to(g_gain, ggain_ref.shape)
    give(wires_out, give_s)


def angular(wires, cotangent, keep, gain, w_query, w_key, w_value, w_out, blocks):
    pixels, chan, lanes = cotangent.shape
    used = keep.shape[0]
    rows = round_up(used, 16)
    wire = wires[0].shape[-1]
    vmem = pl.BlockSpec(memory_space=pltpu.VMEM)
    scale = 1.0 / math.sqrt(chan)
    shapes = wire_shapes(blocks, chan, wire) + [
        jax.ShapeDtypeStruct((pixels, chan, used), BF16),
        held(blocks, (2 * chan, 2 * chan), F32),
        held(blocks, (8, 2 * chan), F32),
    ]
    *out, output, g_weights, g_gain = pl.pallas_call(
        functools.partial(angular_kernel, scale, 8, len(wires)),
        out_shape=shapes,
        in_specs=[vmem] * (len(wires) + 7),
        out_specs=[vmem] * len(shapes),
        scratch_shapes=[
            pltpu.VMEM((blocks, chan, wire), BF16),
            pltpu.VMEM((blocks, chan, wire), BF16),
            pltpu.VMEM((rows, 2 * chan), F32),
            pltpu.VMEM((chan, 1), F32),
            pltpu.VMEM((3 * chan, chan), BF16),
            pltpu.VMEM((chan, 4 * chan), BF16),
            pltpu.VMEM((chan, chan), BF16),
            pltpu.VMEM((chan, 2 * chan), BF16),
            pltpu.VMEM((chan, lanes), F32),
        ]
        + [
            pltpu.VMEM((rows, lanes), F32),
            pltpu.VMEM((rows, 2 * lanes), BF16),
            pltpu.VMEM((chan, lanes), F32),
            pltpu.VMEM((chan, lanes), F32),
            pltpu.VMEM((rows, 4 * chan), BF16),
            pltpu.VMEM((lanes, 2 * chan), BF16),
            pltpu.VMEM((chan, lanes), BF16),
        ]
        * 6,
        name="angular",
        compiler_params=grant(blocks),
    )(*here(blocks, *wires[::-1], cotangent), keep[None, :], gain[None, :], w_query, w_key, w_value, w_out)
    return out, output, g_weights, g_gain


def sum_parts(parts):
    total = parts[0].astype(F32)
    for part in parts[1:]:
        total = total + part.astype(F32)
    return total


def reduce_views(own):
    count = lax.axis_size("view")
    if not pairwise(count):
        return lax.psum(own, "view")
    own = own.astype(BF16)
    parts = [swap(own, "view", step) for step in range(1, count)]
    return sum_parts([own] + parts).astype(BF16)


def scatter_rows(parts):
    if len(parts) == 1:
        return lax.psum(parts[0], "row")
    return sum_parts(
        [parts[0]] + [swap(parts[step], "row", step) for step in range(1, len(parts))]
    )


def gather_rows(own, count):
    if count == 1:
        return [own]
    return [own] + [swap(own, "row", step) for step in range(1, count)]


def body(inputs, cotangent, keep, w_conv, gain, w_query, w_key, w_value, w_out):
    chan, view_dev, row_dev, width = inputs.shape
    blocks = lax.axis_size("view")
    breadth = width // blocks
    views = view_dev * blocks
    lanes = round_up(views, 128)
    pixels = row_dev * breadth
    odd = row_is_odd() > 0
    x = jnp.transpose(inputs, (2, 3, 0, 1))
    first, last = x[0], x[row_dev - 1]
    near, far = halo_swap(jnp.where(odd, first, last), jnp.where(odd, last, first))
    w_conv = jnp.transpose(w_conv, (2, 3, 0, 1))
    wires, frame = convolve(x, near, far, w_conv, blocks)
    wires = exchange(wires)
    cot = jnp.transpose(cotangent, (2, 3, 0, 1)).reshape(pixels, chan, views)
    cot = jnp.pad(cot, ((0, 0), (0, 0), (0, lanes - views)))
    wires, output, g_weights, g_gain = angular(
        wires, cot, keep, gain, w_query, w_key, w_value, w_out, blocks
    )
    output = jnp.transpose(output.reshape(row_dev, breadth, chan, views), (2, 3, 0, 1))
    wires, output = lax.optimization_barrier((exchange(wires)[::-1], output))
    wires = wires[::-1]
    near, far, own, *parts = weight_grads(wires, frame, g_weights, g_gain, view_dev, blocks)
    part = scatter_rows(parts)
    near, far = halo_swap(near, far)
    part, near, far = lax.optimization_barrier((reduce_views(part), near, far))
    parts = gather_rows(part, len(parts))
    d_input = input_grad(own, near, far, w_conv, view_dev, blocks)
    parts, d_input = lax.optimization_barrier((parts, d_input))
    g_conv, g_query, g_key, g_value, g_out, g_gain = unpack(parts, chan, blocks)
    d_input = jnp.transpose(d_input, (0, 3, 1, 2))
    g_conv = jnp.transpose(g_conv, (2, 3, 0, 1))
    return (output, d_input, g_conv, g_gain[0], g_query, g_key, g_value, g_out)


def solution(mesh):
    placed = (
        P(None, "view", ("groups", "row"), None),
        P(None, None, ("groups", "row"), "view"),
        P("groups"),
        P(),
        P(),
        P(),
        P(),
        P(),
        P(),
    )
    return jax.shard_map(
        body,
        mesh=mesh,
        in_specs=placed,
        out_specs=(
            P(None, None, ("groups", "row"), "view"),
            P(None, "view", ("groups", "row"), None),
            P("groups", None, None, None),
            P("groups"),
            P("groups", None),
            P("groups", None),
            P("groups", None),
            P("groups", None),
        ),
        check_vma=False,
    )
```

```python
import functools
import math

import jax
import jax.numpy as jnp
from jax import lax
from jax.experimental import pallas as pl
from jax.experimental.pallas import tpu as pltpu
from jax.sharding import PartitionSpec as P

F32 = jnp.float32
BF16 = jnp.bfloat16


def round_up(value, unit):
    return -(-value // unit) * unit


def dot(left, right, contract=(1, 0)):
    return lax.dot_general(
        left, right, (((contract[0],), (contract[1],)), ((), ())), preferred_element_type=F32
    )


def pairwise(count):
    return count <= 8 and count & (count - 1) == 0


def swap(cells, axis, step):
    count = lax.axis_size(axis)
    return lax.ppermute(cells, axis, [(i, i ^ step) for i in range(count)])


def halo_swap(near, far):
    count = lax.axis_size("row")
    pairs = []
    for i in range(1, count - 1, 2):
        pairs += [(i, i + 1), (i + 1, i)]
    got_near = lax.ppermute(near, "row", [(i, i ^ 1) for i in range(count)])
    got_far = lax.ppermute(far, "row", pairs) if pairs else jnp.zeros_like(far)
    return got_near, got_far


def row_is_odd():
    return lax.rem(lax.axis_index("row"), 2)


def give(refs, held):
    if len(refs) == 1:
        refs[0][...] = held[...].astype(refs[0].dtype)
        return
    me = lax.axis_index("view")
    for step, ref in enumerate(refs):
        ref[...] = held[me ^ step].astype(ref.dtype)


def take(refs, held):
    if len(refs) == 1:
        held[...] = refs[0][...].astype(held.dtype)
        return
    me = lax.axis_index("view")
    for step, ref in enumerate(refs):
        held[me ^ step] = ref[...].astype(held.dtype)


def here(blocks, *arrays):
    if not pairwise(blocks):
        return arrays
    return [pltpu.with_memory_space_constraint(array, pltpu.VMEM) for array in arrays]


def grant(blocks):
    return pltpu.CompilerParams(vmem_limit_bytes=(24 << 20) if pairwise(blocks) else None)


def held(blocks, shape, dtype):
    return (pltpu.VMEM if pairwise(blocks) else jax.ShapeDtypeStruct)(shape, dtype)


def wire_shapes(blocks, chan, lanes):
    if pairwise(blocks):
        return [held(blocks, (chan, lanes), BF16)] * blocks
    return [held(blocks, (blocks, chan, lanes), BF16)]


def exchange(wires):
    if len(wires) == 1:
        return [lax.all_to_all(wires[0], "view", split_axis=0, concat_axis=0, tiled=True)]
    return [wires[0]] + [swap(wires[step], "view", step) for step in range(1, len(wires))]


def taps(w_ref, rows, forward):
    chan = w_ref.shape[2]
    blank = jnp.zeros((chan, chan), F32)
    found = {}
    for i in range(3):
        for j in range(3):
            tap = w_ref[i, j].astype(F32)
            found[i, j] = tap if forward else jnp.transpose(tap)
    bands = []
    for j in range(3):
        for r in range(rows):
            row = []
            for place in range(rows + 2):
                i = place - r if forward else r + 2 - place
                row.append(found[i, j] if 0 <= i < 3 else blank)
            bands.append(jnp.concatenate(row, axis=1))
    return jnp.concatenate(bands, axis=0).astype(BF16)


def spread(frame_ref, acc_ref, weights, rows, forward):
    width, deep, lanes = frame_ref.shape
    chan = deep // (rows + 2)
    size = rows * chan
    acc_ref[...] = jnp.zeros_like(acc_ref)

    def pair(q, carry):
        two = jnp.concatenate([frame_ref[2 * q], frame_ref[2 * q + 1]], axis=1)
        part = dot(weights, two)
        for j in range(3):
            move = 1 - j if forward else j - 1
            for side in range(2):
                acc_ref[2 * q + side + move + 1] += part[
                    j * size : (j + 1) * size, side * lanes : (side + 1) * lanes
                ]
        return carry

    lax.fori_loop(0, width // 2, pair, 0, unroll=width <= 16)


def conv_kernel(blocks, x_ref, near_ref, far_ref, w_ref, gain_in, *refs):
    *wires, frame_ref, gain_out, acc_s, held_s, sem = refs
    fetch = pltpu.make_async_copy(gain_in, gain_out, sem)
    fetch.start()
    rows, width, chan, views = x_ref.shape
    own = rows * chan
    lanes = frame_ref.shape[2]
    odd = row_is_odd() > 0
    frame_ref[...] = jnp.zeros_like(frame_ref)

    def fill(w, carry):
        near, far = near_ref[w], far_ref[w]
        frame_ref[w, :chan, :views] = jnp.where(odd, near, far)
        for r in range(rows):
            frame_ref[w, (r + 1) * chan : (r + 2) * chan, :views] = x_ref[r, w]
        frame_ref[w, chan + own :, :views] = jnp.where(odd, far, near)
        return carry

    lax.fori_loop(0, width, fill, 0, unroll=width <= 16)
    weights = taps(w_ref, rows, True)
    spread(frame_ref, acc_s, weights, rows, True)
    breadth = width // blocks

    def block(b, carry):
        cells = []
        for r in range(rows):
            for k in range(breadth):
                w = b * breadth + k
                value = acc_s[w + 1, r * chan : (r + 1) * chan]
                value = value + frame_ref[w, (r + 1) * chan : (r + 2) * chan].astype(F32)
                cells.append(value[:, :views])
        cells = jnp.concatenate(cells, axis=1)
        held_s[b, :, : cells.shape[1]] = cells
        return carry

    lax.fori_loop(0, blocks, block, 0, unroll=blocks <= 4)
    give(wires, held_s)
    fetch.wait()


def convolve(x, near, far, w_conv, gain, blocks):
    rows, width, chan, views = x.shape
    own = rows * chan
    lanes = round_up(views, 128)
    wire = round_up(rows * (width // blocks) * views, 128)
    vmem = pl.BlockSpec(memory_space=pltpu.VMEM)
    shapes = wire_shapes(blocks, chan, wire)
    shapes = shapes + [
        held(blocks, (width, own + 2 * chan, lanes), BF16),
        held(blocks, (1, chan), F32),
    ]
    *wires, frame, gain = pl.pallas_call(
        functools.partial(conv_kernel, blocks),
        out_shape=shapes,
        in_specs=[vmem] * 4 + [pl.BlockSpec(memory_space=pltpu.HBM)],
        out_specs=[vmem] * len(shapes),
        scratch_shapes=[
            pltpu.VMEM((width + 2, own, lanes), F32),
            pltpu.VMEM((blocks, chan, wire), F32),
            pltpu.SemaphoreType.DMA,
        ],
        name="conv",
        compiler_params=grant(blocks),
    )(
        *here(blocks, x, near, far),
        w_conv,
        pltpu.with_memory_space_constraint(gain[None, :], pltpu.HBM),
    )
    return wires, frame, gain


def weight_kernel(count, pieces, *refs):
    wires = refs[:pieces][::-1]
    frame_ref, g_ref, gain_ref = refs[pieces : pieces + 3]
    near_ref, far_ref, own_ref, *part_refs, held_s, col_s, pack_s = refs[pieces + 3 :]
    width, own, lanes = own_ref.shape
    blocks, chan, wire = held_s.shape
    rows = own // chan
    breadth = width // blocks
    views = count
    odd = row_is_odd()
    take(wires, held_s)
    col_s[0] = jnp.zeros((own, lanes), BF16)
    col_s[width + 1] = jnp.zeros((own, lanes), BF16)

    def block(b, carry):
        cells = held_s[b]
        for r in range(rows):
            for k in range(breadth):
                at = (r * breadth + k) * views
                value = cells[:, at : at + views]
                if lanes > views:
                    value = jnp.concatenate(
                        [value, jnp.zeros((chan, lanes - views), F32)], axis=1
                    )
                col_s[b * breadth + k + 1, r * chan : (r + 1) * chan] = value.astype(BF16)
        return carry

    lax.fori_loop(0, blocks, block, 0, unroll=blocks <= 4)

    def copy(w, carry):
        cells = col_s[w + 1]
        own_ref[w] = cells
        first, last = cells[:chan], cells[own - chan :]
        near_ref[w] = jnp.where(odd > 0, first, last)
        far_ref[w] = jnp.where(odd > 0, last, first)
        return carry

    lax.fori_loop(0, width, copy, 0, unroll=width <= 16)

    def pair(q, total):
        left, right = [], []
        for side in range(2):
            w = 2 * q + side
            left.append(jnp.concatenate([col_s[w], col_s[w + 1], col_s[w + 2]], axis=0))
            right.append(frame_ref[w])
        return total + dot(
            jnp.concatenate(left, axis=1), jnp.concatenate(right, axis=1), (1, 1)
        )

    total = lax.fori_loop(
        0,
        width // 2,
        pair,
        jnp.zeros((3 * own, own + 2 * chan), F32),
        unroll=width <= 16,
    )
    bands = []
    for shift in range(3):
        band = 0.0
        for r in range(rows):
            top = (shift * rows + r) * chan
            band = band + total[top : top + chan, r * chan : (r + 3) * chan]
        bands.append(band)
    g_conv = jnp.concatenate(bands, axis=0)
    edge = 2 * chan
    pack_s[...] = jnp.zeros_like(pack_s)
    pack_s[: 2 * chan] = g_ref[...]
    pack_s[2 * chan : 2 * chan + 8] = gain_ref[...]
    at = 2 * chan + 8
    pack_s[at : at + 3 * chan] = g_conv[:, :edge]
    half = 3 * chan // 2
    rest = g_conv[:, edge:]
    pack_s[at + 3 * chan : at + 3 * chan + half] = jnp.concatenate(
        [rest[:half], rest[half:]], axis=1
    )
    size = part_refs[0].shape[0]
    for step, ref in enumerate(part_refs):
        turn = lax.axis_index("row") ^ step if len(part_refs) > 1 else 0
        ref[...] = pack_s[pl.ds(pl.multiple_of(turn * size, 16), size)].astype(ref.dtype)


def weight_grads(wires, frame, g_weights, g_gain, views, blocks):
    width, deep, lanes = frame.shape
    chan, wire = wires[0].shape[-2:]
    own = deep - 2 * chan
    count = lax.axis_size("row")
    parts = count if pairwise(count) else 1
    size = round_up(2 * chan + 8 + 9 * chan // 2, 16 * parts) // parts
    vmem = pl.BlockSpec(memory_space=pltpu.VMEM)
    return pl.pallas_call(
        functools.partial(weight_kernel, views, len(wires)),
        out_shape=(
            held(blocks, (width, chan, lanes), BF16),
            held(blocks, (width, chan, lanes), BF16),
            held(blocks, (width, own, lanes), BF16),
        )
        + (held(blocks, (size, 2 * chan), BF16 if parts > 1 else F32),) * parts,
        in_specs=[vmem] * (len(wires) + 3),
        out_specs=(vmem,) * (3 + parts),
        scratch_shapes=[
            pltpu.VMEM((blocks, chan, wire), F32),
            pltpu.VMEM((width + 2, own, lanes), BF16),
            pltpu.VMEM((parts * size, 2 * chan), F32),
        ],
        name="weights",
        compiler_params=grant(blocks),
    )(*here(blocks, *wires[::-1], frame, g_weights, g_gain))


def input_kernel(own_ref, near_ref, far_ref, w_ref, out_ref, frame_s, acc_s):
    width, own, lanes = own_ref.shape
    chan = near_ref.shape[1]
    rows = own // chan
    views = out_ref.shape[3]
    odd = row_is_odd() > 0

    def fill(w, carry):
        near, far = near_ref[w], far_ref[w]
        frame_s[w, :chan] = jnp.where(odd, near, far)
        frame_s[w, chan : chan + own] = own_ref[w]
        frame_s[w, chan + own :] = jnp.where(odd, far, near)
        return carry

    lax.fori_loop(0, width, fill, 0, unroll=width <= 16)
    spread(frame_s, acc_s, taps(w_ref, rows, False), rows, False)

    def columns(q, carry):
        at = pl.multiple_of(16 * q, 16)
        cells = []
        for k in range(16):
            cells.append(acc_s[at + k + 1] + own_ref[at + k].astype(F32))
        cells = jnp.swapaxes(jnp.stack(cells), 0, 1).astype(BF16)
        for r in range(rows):
            out_ref[:, r, pl.ds(at, 16), :] = cells[r * chan : (r + 1) * chan, :, :views]
        return carry

    lax.fori_loop(0, width // 16, columns, 0)


def input_grad(own, near, far, w_conv, views, blocks):
    width, size, lanes = own.shape
    chan = near.shape[1]
    vmem = pl.BlockSpec(memory_space=pltpu.VMEM)
    return pl.pallas_call(
        input_kernel,
        out_shape=jax.ShapeDtypeStruct((chan, size // chan, width, views), BF16),
        in_specs=[vmem] * 4,
        out_specs=vmem,
        scratch_shapes=[
            pltpu.VMEM((width, size + 2 * chan, lanes), BF16),
            pltpu.VMEM((width + 2, size, lanes), F32),
        ],
        name="input",
        compiler_params=grant(blocks),
    )(*here(blocks, own, near, far), w_conv)


def unpack_kernel(parts, *refs):
    conv_ref, q_ref, k_ref, v_ref, o_ref, gain_ref, pack_s = refs[parts:]
    size = refs[0].shape[0]
    chan = q_ref.shape[0]
    for step in range(parts):
        turn = lax.axis_index("row") ^ step if parts > 1 else 0
        pack_s[pl.ds(pl.multiple_of(turn * size, 16), size)] = refs[step][...].astype(F32)
    k_ref[...] = pack_s[:chan, :chan]
    v_ref[...] = pack_s[:chan, chan:]
    q_ref[...] = pack_s[chan : 2 * chan, :chan]
    o_ref[...] = pack_s[chan : 2 * chan, chan:]
    gain_ref[...] = pack_s[2 * chan : 2 * chan + 1, :chan]
    at = 2 * chan + 8
    half = 3 * chan // 2
    for j in range(3):
        top = (2 - j) * chan
        for i in range(2):
            conv_ref[i, j] = pack_s[at + top : at + top + chan, i * chan : (i + 1) * chan]
        for low in range(0, chan, chan // 2):
            row = top + low
            side = row // half
            start = at + 3 * chan + row - side * half
            conv_ref[2, j, low : low + chan // 2] = pack_s[
                start : start + chan // 2, side * chan : (side + 1) * chan
            ]


def unpack(parts, chan, blocks):
    vmem = pl.BlockSpec(memory_space=pltpu.VMEM)
    square = jax.ShapeDtypeStruct((chan, chan), F32)
    return pl.pallas_call(
        functools.partial(unpack_kernel, len(parts)),
        out_shape=(
            jax.ShapeDtypeStruct((3, 3, chan, chan), F32),
            square,
            square,
            square,
            square,
            jax.ShapeDtypeStruct((1, chan), F32),
        ),
        in_specs=[vmem] * len(parts),
        out_specs=(vmem,) * 6,
        scratch_shapes=[pltpu.VMEM((len(parts) * parts[0].shape[0], 2 * chan), F32)],
        name="unpack",
        compiler_params=grant(blocks),
    )(*here(blocks, *parts))


def angular_kernel(
    scale,
    lag,
    pieces,
    *refs,
):
    wires_in = refs[:pieces][::-1]
    cot_ref, keep_ref, gain_row, wq_ref, wkey_ref, wv_ref, wo_ref = refs[pieces : pieces + 7]
    refs = refs[pieces + 7 :]
    wires_out = refs[:pieces]
    out_ref, g_ref, ggain_ref = refs[pieces : pieces + 3]
    refs = refs[pieces + 3 :]
    held_s, give_s, bias_ref, gain_ref, wqkv_ref, wkv_ref, wot_ref, wkv2_ref, gain_s = refs[:9]
    scratch = refs[9:]
    blocks = held_s.shape[0]
    pixels, chan, lanes = cot_ref.shape
    used = keep_ref.shape[1]
    each = used // blocks
    rows = bias_ref.shape[0]
    per = 7
    slots = len(scratch) // per
    inv_chan = 1.0 / chan
    take(wires_in, held_s)
    live = jnp.where(keep_ref[...] > 0, 0.0, -1e30).astype(F32)
    live = jnp.concatenate([live, jnp.full((1, lanes - used), -1e30, F32)], axis=1)
    live = jnp.transpose(jnp.broadcast_to(live, (128, lanes)))[:rows]
    lane = lax.broadcasted_iota(jnp.int32, (rows, 128), 1)
    bias_ref[...] = jnp.where(lane == chan, live, 0.0)[:, : 2 * chan]
    eye = lax.broadcasted_iota(jnp.int32, (chan, chan), 0) == lax.broadcasted_iota(
        jnp.int32, (chan, chan), 1
    )
    gain_ref[...] = jnp.sum(jnp.where(eye, gain_row[...], 0.0), axis=1, keepdims=True)
    w_q, w_k, w_v = (ref[...].astype(F32) for ref in (wq_ref, wkey_ref, wv_ref))
    wqkv_ref[...] = jnp.concatenate(
        [jnp.transpose(w_q), jnp.transpose(w_k), jnp.transpose(w_v)], axis=0
    ).astype(BF16)
    blank = jnp.zeros((chan, chan), F32)
    wkv_ref[...] = jnp.concatenate([w_k, blank, w_v, blank], axis=1).astype(BF16)
    wkv2_ref[...] = jnp.concatenate([w_k, w_v], axis=1).astype(BF16)
    wot_ref[...] = jnp.transpose(wo_ref[...].astype(F32)).astype(BF16)
    g_ref[...] = jnp.zeros_like(g_ref)
    gain_s[...] = jnp.zeros_like(gain_s)
    for slot in range(slots):
        d_s = scratch[per * slot + 5]
        d_s[rows:] = jnp.zeros((lanes - rows, 2 * chan), BF16)
    chunks = []
    at = 0
    while at < rows:
        size = min(80, rows - at)
        chunks.append((at, size))
        at += size
    half_lane = lax.broadcasted_iota(jnp.int32, (chan, 2 * chan), 1) < chan

    def pixel(p):
        start = per * (p % slots)
        s_s, e_s, n_s, x_s, kv_s, d_s, nb_s = scratch[start : start + per]
        cells = [held_s[b, :, p * each : (p + 1) * each] for b in range(blocks)]
        if lanes > used:
            cells.append(jnp.zeros((chan, lanes - used), held_s.dtype))
        s = jnp.concatenate(cells, axis=1).astype(F32)
        x_s[...] = s
        cen = s - jnp.sum(s, axis=0, keepdims=True) * inv_chan
        rstd = lax.rsqrt(jnp.sum(cen * cen, axis=0, keepdims=True) * inv_chan + 1e-05)
        normed = cen * rstd
        n_s[...] = normed
        nin32 = normed * gain_ref[...]
        nin = nin32.astype(BF16)
        nb_s[...] = nin
        nin_t = jnp.transpose(nin32)[:rows].astype(BF16)
        yield
        kv = dot(nin_t, wkv_ref[...])
        kv_s[:, : 2 * chan] = (kv[:, : 2 * chan] + bias_ref[...]).astype(BF16)
        kv_s[:, 2 * chan :] = kv[:, 2 * chan :].astype(BF16)
        yield
        qkv = dot(wqkv_ref[...], nin)
        q = (qkv[:chan].astype(BF16).astype(F32) * scale).astype(BF16)
        k = qkv[chan : 2 * chan, :rows].astype(BF16)
        v = qkv[2 * chan :, :rows].astype(BF16)
        zero = jnp.zeros((chan, lanes), BF16)
        q_aug = jnp.concatenate([q, jnp.ones((16, lanes), BF16), zero[16:]], axis=0)
        yield
        s_s[...] = dot(kv_s[:, : 2 * chan], q_aug)
        yield
        high = None
        for at, size in chunks:
            top = jnp.max(s_s[at : at + size].reshape(size // 8, 8, lanes), axis=0)
            high = top if high is None else jnp.maximum(high, top)
        high = jnp.max(high, axis=0, keepdims=True)
        yield
        for at, size in chunks:
            e_s[at : at + size, :lanes] = jnp.exp(s_s[at : at + size] - high).astype(BF16)
            yield
        v_aug = jnp.concatenate([v, jnp.ones((16, rows), BF16)], axis=0)
        att_aug = dot(v_aug, e_s[:, :lanes])
        yield
        cot = cot_ref[p]
        d_att32 = dot(wo_ref[...], cot).astype(BF16).astype(F32)
        inv = 1.0 / att_aug[chan : chan + 1]
        att = att_aug[:chan] * inv
        att_b = att.astype(BF16)
        d_att = (d_att32 * inv).astype(BF16)
        inner = jnp.sum(att * d_att.astype(F32), axis=0, keepdims=True)
        yield
        d_aug = jnp.concatenate([d_att, zero], axis=0)
        s_s[...] = dot(kv_s[:, 2 * chan :], d_aug)
        yield
        for at, size in chunks:
            e_s[at : at + size, lanes:] = e_s[at : at + size, :lanes] * (s_s[at : at + size] - inner).astype(BF16)
            yield
        low = jnp.concatenate(
            [jnp.concatenate([zero, d_att], axis=0), jnp.concatenate([q, zero], axis=0)], axis=1
        )
        d_s[:rows] = dot(e_s[...], low, (1, 1)).astype(BF16)
        yield
        d_q = (dot(k, e_s[:, lanes:]) * scale).astype(BF16)
        yield
        out_ref[p] = (x_s[...] + dot(wot_ref[...], att_b)).astype(BF16)[:, :used]
        yield
        dn = dot(wq_ref[...], d_q) + dot(wkv2_ref[...], d_s[...], (1, 1))
        nin = nb_s[...]
        g_ref[:chan] += dot(nin, d_s[...])
        both = dot(
            jnp.concatenate([nin, att_b], axis=0), jnp.concatenate([d_q, cot], axis=0), (1, 1)
        )
        g_ref[chan:] += jnp.where(half_lane, both[:chan], both[chan:])
        yield
        normed = n_s[...]
        dnn = dn * normed
        gain_s[...] += dnn
        scaled = dn * gain_ref[...]
        back = (
            scaled
            - jnp.sum(scaled, axis=0, keepdims=True) * inv_chan
            - normed * (jnp.sum(dnn * gain_ref[...], axis=0, keepdims=True) * inv_chan)
        )
        done = (cot.astype(F32) + back * rstd).astype(give_s.dtype)
        for b in range(blocks):
            give_s[b, :, p * each : (p + 1) * each] = done[:, b * each : (b + 1) * each]
        yield

    waiting = [pixel(p) for p in range(pixels)]
    active = []
    step = 0
    while waiting or active:
        if waiting and step % lag == 0:
            active += waiting[:2]
            waiting = waiting[2:]
        for run in list(active):
            try:
                next(run)
            except StopIteration:
                active.remove(run)
        step += 1
    g_gain = jnp.sum(gain_s[...], axis=1, keepdims=True)
    g_gain = jnp.sum(jnp.where(eye, g_gain, 0.0), axis=0, keepdims=True)
    g_gain = jnp.concatenate([g_gain, jnp.zeros((1, chan), F32)], axis=1)
    ggain_ref[...] = jnp.broadcast_to(g_gain, ggain_ref.shape)
    give(wires_out, give_s)


def angular(wires, cotangent, keep, gain, w_query, w_key, w_value, w_out, blocks):
    pixels, chan, lanes = cotangent.shape
    used = keep.shape[0]
    rows = round_up(used, 16)
    wire = wires[0].shape[-1]
    vmem = pl.BlockSpec(memory_space=pltpu.VMEM)
    scale = 1.0 / math.sqrt(chan)
    shapes = wire_shapes(blocks, chan, wire) + [
        jax.ShapeDtypeStruct((pixels, chan, used), BF16),
        held(blocks, (2 * chan, 2 * chan), F32),
        held(blocks, (8, 2 * chan), F32),
    ]
    *out, output, g_weights, g_gain = pl.pallas_call(
        functools.partial(angular_kernel, scale, 8, len(wires)),
        out_shape=shapes,
        in_specs=[vmem] * (len(wires) + 7),
        out_specs=[vmem] * len(shapes),
        scratch_shapes=[
            pltpu.VMEM((blocks, chan, wire), BF16),
            pltpu.VMEM((blocks, chan, wire), BF16),
            pltpu.VMEM((rows, 2 * chan), F32),
            pltpu.VMEM((chan, 1), F32),
            pltpu.VMEM((3 * chan, chan), BF16),
            pltpu.VMEM((chan, 4 * chan), BF16),
            pltpu.VMEM((chan, chan), BF16),
            pltpu.VMEM((chan, 2 * chan), BF16),
            pltpu.VMEM((chan, lanes), F32),
        ]
        + [
            pltpu.VMEM((rows, lanes), F32),
            pltpu.VMEM((rows, 2 * lanes), BF16),
            pltpu.VMEM((chan, lanes), F32),
            pltpu.VMEM((chan, lanes), F32),
            pltpu.VMEM((rows, 4 * chan), BF16),
            pltpu.VMEM((lanes, 2 * chan), BF16),
            pltpu.VMEM((chan, lanes), BF16),
        ]
        * 6,
        name="angular",
        compiler_params=grant(blocks),
    )(*here(blocks, *wires[::-1], cotangent), keep[None, :], *here(blocks, gain), w_query, w_key, w_value, w_out)
    return out, output, g_weights, g_gain


def sum_parts(parts):
    total = parts[0].astype(F32)
    for part in parts[1:]:
        total = total + part.astype(F32)
    return total


def reduce_views(own):
    count = lax.axis_size("view")
    if not pairwise(count):
        return lax.psum(own, "view")
    own = own.astype(BF16)
    parts = [swap(own, "view", step) for step in range(1, count)]
    return sum_parts([own] + parts).astype(BF16)


def scatter_rows(parts):
    if len(parts) == 1:
        return lax.psum(parts[0], "row")
    return sum_parts(
        [parts[0]] + [swap(parts[step], "row", step) for step in range(1, len(parts))]
    )


def gather_rows(own, count):
    if count == 1:
        return [own]
    return [own] + [swap(own, "row", step) for step in range(1, count)]


def body(inputs, cotangent, keep, w_conv, gain, w_query, w_key, w_value, w_out):
    chan, view_dev, row_dev, width = inputs.shape
    blocks = lax.axis_size("view")
    breadth = width // blocks
    views = view_dev * blocks
    lanes = round_up(views, 128)
    pixels = row_dev * breadth
    odd = row_is_odd() > 0
    x = jnp.transpose(inputs, (2, 3, 0, 1))
    first, last = x[0], x[row_dev - 1]
    near, far = halo_swap(jnp.where(odd, first, last), jnp.where(odd, last, first))
    w_conv = jnp.transpose(w_conv, (2, 3, 0, 1))
    wires, frame, gain = convolve(x, near, far, w_conv, gain, blocks)
    wires = exchange(wires)
    cot = jnp.transpose(cotangent, (2, 3, 0, 1)).reshape(pixels, chan, views)
    cot = jnp.pad(cot, ((0, 0), (0, 0), (0, lanes - views)))
    wires, output, g_weights, g_gain = angular(
        wires, cot, keep, gain, w_query, w_key, w_value, w_out, blocks
    )
    output = jnp.transpose(output.reshape(row_dev, breadth, chan, views), (2, 3, 0, 1))
    wires, output = lax.optimization_barrier((exchange(wires)[::-1], output))
    wires = wires[::-1]
    near, far, own, *parts = weight_grads(wires, frame, g_weights, g_gain, view_dev, blocks)
    part = scatter_rows(parts)
    near, far = halo_swap(near, far)
    part, near, far = lax.optimization_barrier((reduce_views(part), near, far))
    parts = gather_rows(part, len(parts))
    d_input = input_grad(own, near, far, w_conv, view_dev, blocks)
    parts, d_input = lax.optimization_barrier((parts, d_input))
    g_conv, g_query, g_key, g_value, g_out, g_gain = unpack(parts, chan, blocks)
    d_input = jnp.transpose(d_input, (0, 3, 1, 2))
    g_conv = jnp.transpose(g_conv, (2, 3, 0, 1))
    return (output, d_input, g_conv, g_gain[0], g_query, g_key, g_value, g_out)


def solution(mesh):
    placed = (
        P(None, "view", ("groups", "row"), None),
        P(None, None, ("groups", "row"), "view"),
        P("groups"),
        P(),
        P(),
        P(),
        P(),
        P(),
        P(),
    )
    return jax.shard_map(
        body,
        mesh=mesh,
        in_specs=placed,
        out_specs=(
            P(None, None, ("groups", "row"), "view"),
            P(None, "view", ("groups", "row"), None),
            P("groups", None, None, None),
            P("groups"),
            P("groups", None),
            P("groups", None),
            P("groups", None),
            P("groups", None),
        ),
        check_vma=False,
    )
```
